32 devices in a mesh: dp: 8 (over y, x, core), blk: 4 (over z).
Axes of the slice: x: 2, y: 2, z: 4, core: 2. Of those that a mesh axis runs over, the one named last changes fastest.
Arguments:
- raw_input: float32 [8, 1024, 768], P('dp', 'blk'), may hold values from -72 to 72
- cotangent: bfloat16 [8, 1024, 768], P('dp', 'blk'), may hold values from -36 to 36
- segment_ids: int32 [8, 1024], P('dp', 'blk'), may hold values from 0 to 3, never falling along the last dimension, each value on 1 to 512 neighbouring positions
- step_count: int32 [1], replicated, may hold values from 10 to 20
- inlet_copy: bfloat16 [768, 2304], replicated, may hold values from -0.3125 to 0.3125
- inlet_master: float32 [768, 2304], P('dp'), may hold values from -0.3125 to 0.3125
- inlet_moment: float32 [768, 2304], P('dp'), may hold values from -512 to 512
- inlet_square: float32 [768, 2304], P('dp'), may hold values from 2703.36 to 22118.4
- outlet_copy: bfloat16 [768, 768], replicated, may hold values from -0.875 to 0.875
- outlet_master: float32 [768, 768], P('dp'), may hold values from -0.875 to 0.875
- outlet_moment: float32 [768, 768], P('dp'), may hold values from -256 to 256
- outlet_square: float32 [768, 768], P('dp'), may hold values from 548.864 to 4423.68
- expand_copy: bfloat16 [768, 3072], replicated, may hold values from -0.21875 to 0.21875
- expand_master: float32 [768, 3072], P('dp'), may hold values from -0.21875 to 0.21875
- expand_moment: float32 [768, 3072], P('dp'), may hold values from -256 to 256
- expand_square: float32 [768, 3072], P('dp'), may hold values from 548.864 to 4423.68
- shrink_copy: bfloat16 [3072, 768], replicated, may hold values from -0.109375 to 0.109375
- shrink_master: float32 [3072, 768], P('dp'), may hold values from -0.109375 to 0.109375
- shrink_moment: float32 [3072, 768], P('dp'), may hold values from -512 to 512
- shrink_square: float32 [3072, 768], P('dp'), may hold values from 2211.84 to 18022.4
- vector_copy: bfloat16 [12, 768], replicated, may hold values from -2 to 2
- vector_master: float32 [12, 768], P(None, 'dp'), may hold values from -2 to 2
- vector_moment: float32 [12, 768], P(None, 'dp'), may hold values from -512 to 512
- vector_square: float32 [12, 768], P(None, 'dp'), may hold values from 2703.36 to 22118.4
Outputs:
- layer_output: bfloat16 [8, 1024, 768], P('dp', 'blk')
- input_gradient: float32 [8, 1024, 768], P('dp', 'blk')
- band_mean: float32 [768], replicated
- band_variance: float32 [768], replicated
- inlet_weight: float32 [768, 2304], P('dp')
- inlet_drift: float32 [768, 2304], P('dp')
- inlet_spread: float32 [768, 2304], P('dp')
- inlet_shadow: bfloat16 [768, 2304], P('dp')
- outlet_weight: float32 [768, 768], P('dp')
- outlet_drift: float32 [768, 768], P('dp')
- outlet_spread: float32 [768, 768], P('dp')
- outlet_shadow: bfloat16 [768, 768], P('dp')
- expand_weight: float32 [768, 3072], P('dp')
- expand_drift: float32 [768, 3072], P('dp')
- expand_spread: float32 [768, 3072], P('dp')
- expand_shadow: bfloat16 [768, 3072], P('dp')
- shrink_weight: float32 [3072, 768], P('dp')
- shrink_drift: float32 [3072, 768], P('dp')
- shrink_spread: float32 [3072, 768], P('dp')
- shrink_shadow: bfloat16 [3072, 768], P('dp')
- vector_weight: float32 [12, 768], P(None, 'dp')
- vector_drift: float32 [12, 768], P(None, 'dp')
- vector_spread: float32 [12, 768], P(None, 'dp')
- vector_shadow: bfloat16 [12, 768], P(None, 'dp')
The draws below stay inside these ranges and needn't reach their ends.
Inputs may be any that keep to these rules, and one draw needn't show every extreme that they name: `segment_ids`: within each sequence the ids never fall; each segment holds 1 to 512 positions, one of them exactly that many.
All inputs are finite; a program needn't handle non-finite values.
Results may differ from the reference program's by a relative error of at most 0.014.
Values may be sent and summed in bfloat16 or wider, within the bound.
No kernel may reach another device: no remote copies, remote signals or barrier semaphores. Data moves between devices by JAX's collectives and lax.ppermute only.
A program may use at most 256 MiB of HBM per device.

```python
import math
import jax
import jax.numpy as jnp
import numpy as np
from jax import lax

D = 768
HEADS = 12
HEAD_DIM = 64
FF = 3072
SEQ_LEN = 1024
SEQS = 8
TOKENS = 8192


def place_grids(leading, length):
    seq_place = jnp.arange(leading, dtype=jnp.float32)[:, None, None] / max(leading - 1, 1)
    token_place = jnp.arange(length, dtype=jnp.float32)[None, :, None] / max(length - 1, 1)
    return (seq_place, token_place)


def rising_rows(leading, length):
    seq_place, token_place = place_grids(leading, length)
    return (1.0 + 2.0 * seq_place) * (1.0 + 2.0 * token_place) / 3.0


def raw_parts(key):
    streams = jax.random.split(jax.random.fold_in(key, 11), 4)
    roughness = jax.random.uniform(streams[0], (SEQS, SEQ_LEN, 1), minval=0.7, maxval=1.3)
    centres = jax.random.uniform(streams[1], (D,), minval=-1.0, maxval=1.0)
    spreads = jnp.exp(jax.random.uniform(streams[2], (D,), minval=math.log(0.5), maxval=math.log(3.0)))
    shaping = rising_rows(SEQS, SEQ_LEN) * roughness
    basis = jnp.clip(jax.random.normal(streams[3], (SEQS, SEQ_LEN, D)), -6.0, 6.0)
    return (centres, spreads, shaping * basis)


def draw_raw_input(key, part):
    centres, spreads, pattern = raw_parts(key)
    return centres + spreads * pattern


def draw_cotangent(key, part):
    centres, spreads, pattern = raw_parts(key)
    streams = jax.random.split(jax.random.fold_in(key, 12), 2)
    roughness = jax.random.uniform(streams[0], (SEQS, SEQ_LEN, 1), minval=0.7, maxval=1.3)
    basis = jnp.clip(jax.random.normal(streams[1], (SEQS, SEQ_LEN, D)), -6.0, 6.0)
    seq_place, token_place = place_grids(SEQS, SEQ_LEN)
    coupling = 0.1 + 0.2 * (seq_place + token_place)
    return (rising_rows(SEQS, SEQ_LEN) * roughness * basis + coupling * pattern).astype(jnp.bfloat16)


def vector_rows(stream_key):
    streams = jax.random.split(stream_key, 2)
    shifts = 0.3 * jnp.clip(jax.random.normal(streams[0], (12, D)), -6.0, 6.0)
    gains = 1.0 + jax.random.uniform(streams[1], (12, D), minval=-0.3, maxval=0.3)
    row_index = jnp.arange(12)
    gain_rows = (row_index == 0) | (row_index == 2)
    return jnp.where(gain_rows[:, None], gains, shifts)


def draw_vector_copy(key, part):
    return vector_rows(jax.random.fold_in(key, 21)).astype(jnp.bfloat16)


def draw_vector_master(key, part):
    return vector_rows(jax.random.fold_in(key, 22))


def block_levels(rng, dims, shards, least, high):
    loudness = 1.0
    for position, parts in shards:
        draws = jax.random.uniform(jax.random.fold_in(jax.random.fold_in(rng, 6), position), (parts,), jnp.float32, least / len(shards), high / len(shards))
        loudness = loudness * jnp.repeat(jnp.exp(draws), dims[position] // parts).reshape((-1,) + (1,) * (len(dims) - 1 - position))
    return loudness


def profile(number_of, total, most, skew):
    portions = [(1 << 20) // math.isqrt(grade ** skew) + 1 for grade in range(2, number_of + 1)]
    surplus, given = total - most - (number_of - 1), [1] * (number_of - 1)
    while surplus > 0:
        candidates = [i for i in range(number_of - 1) if given[i] < most]
        pool, left = sum([portions[i] for i in candidates]), surplus
        for i in candidates:
            extra = min(most - given[i], max(1, left * portions[i] // pool), surplus)
            given[i] = given[i] + extra
            surplus = surplus - extra
    return np.array([most] + given)


def uneven_parts(key, number_of, total, bound, lean):
    if number_of == 2:
        one = jax.random.randint(key, (), max(1, total - bound), min(bound, total - 1) + 1)
        return jnp.stack([one, total - one])
    tallies = jnp.asarray(profile(number_of, total, bound, lean), jnp.int32)
    pairs = (number_of - 1) // 2
    giver, receiver = tallies[1:1 + 2 * pairs:2], tallies[2:2 + 2 * pairs:2]
    room = jnp.minimum(giver - 1, bound - receiver)
    shifted = jax.random.randint(jax.random.fold_in(key, 1), (pairs,), 0, 1 << 20) % (room + 1)
    tallies = tallies.at[1:1 + 2 * pairs:2].set(giver - shifted).at[2:2 + 2 * pairs:2].set(receiver + shifted)
    return tallies[jax.random.permutation(jax.random.fold_in(key, 2), number_of)]


def gaussian(rng, dims, deviation, bound, cuts=(), kind=jnp.bfloat16):
    array = jax.random.normal(rng, dims, jnp.float32) * deviation
    if len(cuts) > 0:
        array = block_levels(rng, dims, cuts, -0.22, 0.18) * array
    return jnp.clip(array, min=-bound, max=bound).astype(kind)


def setup_inputs(seed: int = 0) -> dict:
    seeds = jax.random.split(jax.random.key(seed), 25)
    raw_input = draw_raw_input(jax.random.fold_in(seeds[24], 71), 0)
    cotangent = draw_cotangent(jax.random.fold_in(seeds[24], 71), 0)
    segment_ids = jax.vmap(lambda own: jnp.searchsorted(jnp.cumsum(uneven_parts(own, 4, SEQ_LEN, SEQ_LEN // 2, 0)), jnp.arange(SEQ_LEN), side="right"))(jax.random.split(seeds[2], SEQS)).reshape((SEQS, SEQ_LEN)).astype(jnp.int32)
    step_count = jax.random.randint(seeds[3], (1,), 10, 21).astype(jnp.int32)
    inlet_copy = gaussian(seeds[4], (D, 3 * D), (D // 2) ** -0.5, 0.3125)
    inlet_master = gaussian(seeds[5], (D, 3 * D), (D // 2) ** -0.5, 0.3125, ((0, 8),), jnp.float32)
    inlet_moment = gaussian(seeds[6], (D, 3 * D), (TOKENS ** 0.5), 512.0, ((0, 8),), jnp.float32)
    inlet_square = jnp.clip(jnp.exp(math.log(22118.4) - 2.1019144 * jax.random.uniform(seeds[7], (D, 3 * D), jnp.float32) ** block_levels(seeds[7], (D, 3 * D), ((0, 8),), -0.2, 0.2)), 2703.36, 22118.4)
    outlet_copy = gaussian(seeds[8], (D, D), (D // 16) ** -0.5, 0.875)
    outlet_master = gaussian(seeds[9], (D, D), (D // 16) ** -0.5, 0.875, ((0, 8),), jnp.float32)
    outlet_moment = gaussian(seeds[10], (D, D), (0.45 * TOKENS ** 0.5), 256.0, ((0, 8),), jnp.float32)
    outlet_square = jnp.clip(jnp.exp(math.log(4423.68) - 2.08687653 * jax.random.uniform(seeds[11], (D, D), jnp.float32) ** block_levels(seeds[11], (D, D), ((0, 8),), -0.2, 0.2)), 548.864, 4423.68)
    expand_copy = gaussian(seeds[12], (D, FF), D ** -0.5, 0.21875)
    expand_master = gaussian(seeds[13], (D, FF), D ** -0.5, 0.21875, ((0, 8),), jnp.float32)
    expand_moment = gaussian(seeds[14], (D, FF), (0.45 * TOKENS ** 0.5), 256.0, ((0, 8),), jnp.float32)
    expand_square = jnp.clip(jnp.exp(math.log(4423.68) - 2.08687653 * jax.random.uniform(seeds[15], (D, FF), jnp.float32) ** block_levels(seeds[15], (D, FF), ((0, 8),), -0.2, 0.2)), 548.864, 4423.68)
    shrink_copy = gaussian(seeds[16], (FF, D), FF ** -0.5, 0.109375)
    shrink_master = gaussian(seeds[17], (FF, D), FF ** -0.5, 0.109375, ((0, 8),), jnp.float32)
    shrink_moment = gaussian(seeds[18], (FF, D), (0.9 * TOKENS ** 0.5), 512.0, ((0, 8),), jnp.float32)
    shrink_square = jnp.clip(jnp.exp(math.log(18022.4) - 2.0977907 * jax.random.uniform(seeds[19], (FF, D), jnp.float32) ** block_levels(seeds[19], (FF, D), ((0, 8),), -0.2, 0.2)), 2211.84, 18022.4)
    vector_copy = draw_vector_copy(jax.random.fold_in(seeds[24], 71), 0)
    vector_master = draw_vector_master(jax.random.fold_in(seeds[24], 71), 0)
    vector_moment = gaussian(seeds[22], (12, D), (TOKENS ** 0.5), 512.0, ((1, 8),), jnp.float32)
    vector_square = jnp.clip(jnp.exp(math.log(22118.4) - 2.1019144 * jax.random.uniform(seeds[23], (12, D), jnp.float32) ** block_levels(seeds[23], (12, D), ((1, 8),), -0.2, 0.2)), 2703.36, 22118.4)
    return {"raw_input": raw_input, "cotangent": cotangent, "segment_ids": segment_ids, "step_count": step_count, "inlet_copy": inlet_copy, "inlet_master": inlet_master, "inlet_moment": inlet_moment, "inlet_square": inlet_square, "outlet_copy": outlet_copy, "outlet_master": outlet_master, "outlet_moment": outlet_moment, "outlet_square": outlet_square, "expand_copy": expand_copy, "expand_master": expand_master, "expand_moment": expand_moment, "expand_square": expand_square, "shrink_copy": shrink_copy, "shrink_master": shrink_master, "shrink_moment": shrink_moment, "shrink_square": shrink_square, "vector_copy": vector_copy, "vector_master": vector_master, "vector_moment": vector_moment, "vector_square": vector_square}


@jax.custom_vjp
def low(v):
    return lax.optimization_barrier(v.astype(jnp.bfloat16)).astype(jnp.float32)

@jax.custom_vjp
def low_back(v):
    return v

def low_keep(v):
    return (low(v), None)

def low_pass(kept, grad):
    return (grad,)

def back_keep(v):
    return (v, None)

def back_low(kept, grad):
    return (low(grad),)
low.defvjp(low_keep, low_pass)
low_back.defvjp(back_keep, back_low)
ln_epsilon = 1e-05
stat_epsilon = 1e-06
beta_one = 0.5
beta_two = 0.6
rate_matrix = 0.04
rate_vector = 0.8
warmup_length = 20.0
decay_matrix = 0.05
adam_epsilon = 1e-08
score_scale = 0.125
masked_score = -1e+30
highest = lax.Precision.HIGHEST

def layer_norm(inputs, scaling, offset):
    centred = inputs - lax.optimization_barrier(jnp.mean(inputs, axis=-1, keepdims=True))
    spread = lax.optimization_barrier(jnp.mean(centred * centred, axis=-1, keepdims=True))
    return centred * lax.rsqrt(spread + ln_epsilon) * scaling + offset

def product(left, right):
    return jnp.dot(left, right, precision=highest)

def sequence_layer(normed, segments, inlet_full, outlet_full, expand_full, shrink_full, vector_full):
    length = normed.shape[0]
    features = normed.shape[1]
    first_in = low(layer_norm(normed, vector_full[0], vector_full[1]))
    mixed = product(first_in, inlet_full)
    queries = low_back(low((mixed[:, :features] + vector_full[4]) * score_scale))
    keys_all = low_back(low(mixed[:, features:2 * features]))
    values_all = low_back(low(mixed[:, 2 * features:] + vector_full[5]))
    query_heads = queries.reshape(length, HEADS, HEAD_DIM)
    key_heads = keys_all.reshape(length, HEADS, HEAD_DIM)
    value_heads = values_all.reshape(length, HEADS, HEAD_DIM)
    scores = low_back(jnp.einsum('qhd,khd->hqk', query_heads, key_heads, precision=highest))
    allowed = (segments[:, None] == segments[None, :])[None]
    scores = jnp.where(allowed, scores, masked_score)
    largest = lax.optimization_barrier(jnp.max(scores, axis=-1, keepdims=True))
    weights = jnp.where(allowed, jnp.exp(scores - largest), 0.0)
    weights = low(weights / lax.optimization_barrier(jnp.sum(weights, axis=-1, keepdims=True)))
    attended = jnp.einsum('hqk,khd->qhd', weights, value_heads, precision=highest).reshape(length, features)
    attended = low_back(low(attended))
    branch = low_back(product(attended, outlet_full) + vector_full[6])
    middle = normed + branch
    second_in = low(layer_norm(middle, vector_full[2], vector_full[3]))
    hidden_pre = low_back(product(second_in, expand_full) + vector_full[8:12].reshape(-1))
    hidden = low(jax.nn.gelu(hidden_pre, approximate=False))
    output_part = low_back(product(hidden, shrink_full) + vector_full[7])
    return middle + output_part

def whole_layer(raw_values, segment_ids, inlet_full, outlet_full, expand_full, shrink_full, vector_full):
    flattened = raw_values.reshape(-1, raw_values.shape[-1])
    band_mean = lax.optimization_barrier(jnp.mean(flattened, axis=0))
    band_variance = lax.optimization_barrier(jnp.mean(flattened * flattened, axis=0)) - band_mean * band_mean
    normed = (raw_values - band_mean) * lax.rsqrt(band_variance + stat_epsilon)
    layer_step = jax.checkpoint(sequence_layer)

    def one_sequence(carried, pieces):
        return (carried, layer_step(pieces[0], pieces[1], inlet_full, outlet_full, expand_full, shrink_full, vector_full))
    unused, outputs = lax.scan(one_sequence, jnp.zeros((), raw_values.dtype), (normed, segment_ids))
    return (outputs, (band_mean, band_variance))

def adam_rule(master, moment, square, gradient, step_value, step_rate, weight_decay):
    moment_new = beta_one * moment + (1.0 - beta_one) * gradient
    square_new = beta_two * square + (1.0 - beta_two) * gradient * gradient
    fix_first = 1.0 - jnp.power(beta_one, step_value)
    fix_second = 1.0 - jnp.power(beta_two, step_value)
    planned = step_rate * jnp.minimum(1.0, step_value / warmup_length)
    direction = moment_new / fix_first / (jnp.sqrt(square_new / fix_second) + adam_epsilon)
    weight_new = master - planned * (direction + weight_decay * master)
    return (weight_new, moment_new, square_new, weight_new.astype(jnp.bfloat16))

def reference(raw_input, cotangent, segment_ids, step_count, inlet_copy, inlet_master, inlet_moment, inlet_square, outlet_copy, outlet_master, outlet_moment, outlet_square, expand_copy, expand_master, expand_moment, expand_square, shrink_copy, shrink_master, shrink_moment, shrink_square, vector_copy, vector_master, vector_moment, vector_square):

    def forward(raw_values, inlet_full, outlet_full, expand_full, shrink_full, vector_full):
        return whole_layer(raw_values, segment_ids, inlet_full, outlet_full, expand_full, shrink_full, vector_full)
    outputs, pullback, statistics = jax.vjp(forward, raw_input, inlet_copy.astype(jnp.float32), outlet_copy.astype(jnp.float32), expand_copy.astype(jnp.float32), shrink_copy.astype(jnp.float32), vector_copy.astype(jnp.float32), has_aux=True)
    gradients = pullback(cotangent.astype(jnp.float32))
    step_value = step_count[0].astype(jnp.float32)
    inlet_weight, inlet_drift, inlet_spread, inlet_shadow = adam_rule(inlet_master, inlet_moment, inlet_square, gradients[1], step_value, rate_matrix, decay_matrix)
    outlet_weight, outlet_drift, outlet_spread, outlet_shadow = adam_rule(outlet_master, outlet_moment, outlet_square, gradients[2], step_value, rate_matrix, decay_matrix)
    expand_weight, expand_drift, expand_spread, expand_shadow = adam_rule(expand_master, expand_moment, expand_square, gradients[3], step_value, rate_matrix, decay_matrix)
    shrink_weight, shrink_drift, shrink_spread, shrink_shadow = adam_rule(shrink_master, shrink_moment, shrink_square, gradients[4], step_value, rate_matrix, decay_matrix)
    vector_weight, vector_drift, vector_spread, vector_shadow = adam_rule(vector_master, vector_moment, vector_square, gradients[5], step_value, rate_vector, 0.0)
    return (outputs.astype(jnp.bfloat16), gradients[0], statistics[0], statistics[1], inlet_weight, inlet_drift, inlet_spread, inlet_shadow, outlet_weight, outlet_drift, outlet_spread, outlet_shadow, expand_weight, expand_drift, expand_spread, expand_shadow, shrink_weight, shrink_drift, shrink_spread, shrink_shadow, vector_weight, vector_drift, vector_spread, vector_shadow)
```

```python
import functools

import jax
import jax.numpy as jnp
from jax import lax
from jax.experimental import pallas as pl
from jax.experimental.pallas import tpu as pltpu
from jax.sharding import PartitionSpec as P

HEADS = 12
HEAD_WIDTH = 64
GROUP = 4

ln_epsilon = 1e-05
stat_epsilon = 1e-06
beta_one = 0.5
beta_two = 0.6
rate_matrix = 0.04
rate_vector = 0.8
warmup_length = 20.0
decay_matrix = 0.05
adam_epsilon = 1e-08
score_scale = 0.125
masked_score = -1e30

f32 = jnp.float32
bf16 = jnp.bfloat16


def nn(a, b):
    return lax.dot_general(a, b, (((1,), (0,)), ((), ())), preferred_element_type=f32)


def nt(a, b):
    return lax.dot_general(a, b, (((1,), (1,)), ((), ())), preferred_element_type=f32)


def tn(a, b):
    return lax.dot_general(a, b, (((0,), (0,)), ((), ())), preferred_element_type=f32)


def flipped(block, axis, bit):
    size = lax.axis_size(axis)
    return lax.ppermute(block, axis, [(i, i ^ bit) for i in range(size)])


def moved(block, axis, distance):
    size = lax.axis_size(axis)
    route = [(i, i + distance) for i in range(size) if 0 <= i + distance < size]
    return lax.ppermute(block, axis, route)


def bits_of(axis):
    size = lax.axis_size(axis)
    return [1 << i for i in range(size.bit_length() - 1)]


def everywhere_sum(block):
    for axis in ("dp", "blk"):
        for bit in bits_of(axis):
            block = block + flipped(block, axis, bit)
    return block


def halves(block, axis, way, position):
    own = (lax.axis_index(axis) // way) % 2
    keep = lax.dynamic_index_in_dim(block, own, position, keepdims=False)
    send = lax.dynamic_index_in_dim(block, 1 - own, position, keepdims=False)
    return keep, send


def owned_sum(gradient, order):
    dp_bits = bits_of("dp")
    count = len(dp_bits)
    rows, columns = gradient.shape
    owners = lax.axis_size("dp")
    block = gradient.reshape((2,) * count + (rows // owners, columns))
    left = list(reversed(dp_bits))
    for bit in order:
        where = left.index(bit)
        keep, send = halves(block, "dp", bit, where)
        block = (keep.astype(f32) + flipped(send, "dp", bit).astype(f32)).astype(bf16)
        left.pop(where)
    share = block
    blk_bits = bits_of("blk")
    trail = []
    for bit in blk_bits[:-1]:
        keep, send = halves(share.reshape(2, share.shape[0] // 2, columns), "blk", bit, 0)
        share = (keep.astype(f32) + flipped(send, "blk", bit).astype(f32)).astype(bf16)
        trail.append(bit)
    if blk_bits:
        share = (share.astype(f32) + flipped(share, "blk", blk_bits[-1]).astype(f32)).astype(bf16)
    for bit in reversed(trail):
        other = flipped(share, "blk", bit)
        own = (lax.axis_index("blk") // bit) % 2
        share = jnp.where(
            own == 0, jnp.concatenate([share, other], 0), jnp.concatenate([other, share], 0)
        )
    return share


def lane_half(rows, which):
    lanes = lax.broadcasted_iota(jnp.int32, (rows, 128), 1)
    return (lanes >= 64) if which else (lanes < 64)


def attend_kernel(bounds, q_ref, k_ref, v_ref, qid_ref, kid_ref, o_ref, lse_ref, acc, top, total):
    width = q_ref.shape[0]
    top[...] = jnp.full_like(top, masked_score)
    total[...] = jnp.zeros_like(total)
    acc[...] = jnp.zeros_like(acc)
    own = qid_ref[...]
    masked_q = []
    for h in range(GROUP):
        pair = q_ref[:, 128 * (h // 2) : 128 * (h // 2) + 128]
        masked_q.append(jnp.where(lane_half(width, h % 2), pair, jnp.zeros_like(pair)))

    def step(s, carry):
        keys = k_ref[s]
        values_t = v_ref[s].T
        allowed = kid_ref[s] == own
        for h in range(GROUP):
            lanes = slice(128 * (h // 2), 128 * (h // 2) + 128)
            score = jnp.where(allowed, nt(keys[:, lanes], masked_q[h]), masked_score)
            old = top[h : h + 1, :]
            new = jnp.maximum(old, jnp.max(score, axis=0, keepdims=True))
            fade = jnp.exp(old - new)
            weight = jnp.exp(score - new)
            total[h : h + 1, :] = total[h : h + 1, :] * fade + jnp.sum(
                weight, axis=0, keepdims=True
            )
            top[h : h + 1, :] = new
            rows = slice(64 * h, 64 * h + 64)
            acc[rows, :] = acc[rows, :] * fade + nn(values_t[rows, :], weight.astype(bf16))
        return carry

    lax.fori_loop(bounds[0], bounds[1], step, 0)
    for h in range(GROUP):
        rows = slice(64 * h, 64 * h + 64)
        acc[rows, :] = acc[rows, :] / total[h : h + 1, :]
    o_ref[...] = acc[...].T
    lse_ref[0] = top[0:GROUP, :] + jnp.log(total[0:GROUP, :])


def attend(bounds, queries, pairs, own_ids, slot_ids):
    slots, width, _ = pairs.shape
    features = queries.shape[1]
    lanes = GROUP * HEAD_WIDTH
    steps = features // lanes
    return pl.pallas_call(
        attend_kernel,
        grid_spec=pltpu.PrefetchScalarGridSpec(
            num_scalar_prefetch=1,
            grid=(steps,),
            in_specs=[
                pl.BlockSpec((width, lanes), lambda i, b: (0, i)),
                pl.BlockSpec((slots, width, lanes), lambda i, b: (0, 0, i)),
                pl.BlockSpec((slots, width, lanes), lambda i, b: (0, 0, i + steps)),
                pl.BlockSpec((1, width), lambda i, b: (0, 0)),
                pl.BlockSpec((slots, width, 1), lambda i, b: (0, 0, 0)),
            ],
            out_specs=[
                pl.BlockSpec((width, lanes), lambda i, b: (0, i)),
                pl.BlockSpec((1, GROUP, width), lambda i, b: (i, 0, 0)),
            ],
            scratch_shapes=[
                pltpu.VMEM((lanes, width), f32),
                pltpu.VMEM((8, width), f32),
                pltpu.VMEM((8, width), f32),
            ],
        ),
        out_shape=[
            jax.ShapeDtypeStruct((width, features), f32),
            jax.ShapeDtypeStruct((steps, GROUP, width), f32),
        ],
        name="attend",
    )(bounds, queries, pairs, pairs, own_ids, slot_ids)


def attend_back_kernel(
    bounds, q_ref, k_ref, v_ref, o_ref, g_ref, lse_ref, qid_ref, kid_ref, dq_ref, dk_ref, dv_ref, acc
):
    width = q_ref.shape[0]
    slots = k_ref.shape[0]
    acc[...] = jnp.zeros_like(acc)
    own = qid_ref[...]
    product = (g_ref[...].astype(f32) * o_ref[...]).T
    masked_q, masked_g, deltas, lses = [], [], [], []
    for h in range(GROUP):
        lanes = slice(128 * (h // 2), 128 * (h // 2) + 128)
        half = lane_half(width, h % 2)
        pair = q_ref[:, lanes]
        masked_q.append(jnp.where(half, pair, jnp.zeros_like(pair)))
        pair = g_ref[:, lanes]
        masked_g.append(jnp.where(half, pair, jnp.zeros_like(pair)))
        deltas.append(jnp.sum(product[64 * h : 64 * h + 64, :], axis=0, keepdims=True))
        lses.append(lse_ref[0, h : h + 1, :])

    def blank(s, carry):
        dk_ref[s] = jnp.zeros(dk_ref.shape[1:], dk_ref.dtype)
        dv_ref[s] = jnp.zeros(dv_ref.shape[1:], dv_ref.dtype)
        return carry

    lax.fori_loop(0, bounds[0], blank, 0)
    lax.fori_loop(bounds[1], slots, blank, 0)

    def step(s, carry):
        keys = k_ref[s]
        values = v_ref[s]
        keys_t = keys.T
        allowed = kid_ref[s] == own
        for j in range(GROUP // 2):
            lanes = slice(128 * j, 128 * j + 128)
            key_part, value_part = None, None
            for h in (2 * j, 2 * j + 1):
                score = jnp.where(allowed, nt(keys[:, lanes], masked_q[h]), masked_score)
                prob = jnp.exp(score - lses[h])
                grad = (prob * (nt(values[:, lanes], masked_g[h]) - deltas[h])).astype(bf16)
                rows = slice(64 * h, 64 * h + 64)
                acc[rows, :] += nn(keys_t[rows, :], grad)
                k_now = nn(grad, masked_q[h])
                v_now = nn(prob.astype(bf16), masked_g[h])
                key_part = k_now if key_part is None else key_part + k_now
                value_part = v_now if value_part is None else value_part + v_now
            dk_ref[s, :, lanes] = key_part.astype(bf16)
            dv_ref[s, :, lanes] = value_part.astype(bf16)
        return carry

    lax.fori_loop(bounds[0], bounds[1], step, 0)
    dq_ref[...] = (acc[...].T.astype(bf16).astype(f32) * score_scale).astype(bf16)


def attend_back(bounds, queries, pairs, outputs, grads, lse, own_ids, slot_ids):
    slots, width, _ = pairs.shape
    features = queries.shape[1]
    lanes = GROUP * HEAD_WIDTH
    steps = features // lanes
    flat = pl.BlockSpec((width, lanes), lambda i, b: (0, i))
    return pl.pallas_call(
        attend_back_kernel,
        grid_spec=pltpu.PrefetchScalarGridSpec(
            num_scalar_prefetch=1,
            grid=(steps,),
            in_specs=[
                flat,
                pl.BlockSpec((slots, width, lanes), lambda i, b: (0, 0, i)),
                pl.BlockSpec((slots, width, lanes), lambda i, b: (0, 0, i + steps)),
                flat,
                flat,
                pl.BlockSpec((1, GROUP, width), lambda i, b: (i, 0, 0)),
                pl.BlockSpec((1, width), lambda i, b: (0, 0)),
                pl.BlockSpec((slots, width, 1), lambda i, b: (0, 0, 0)),
            ],
            out_specs=[
                flat,
                pl.BlockSpec((slots, width, lanes), lambda i, b: (0, 0, i)),
                pl.BlockSpec((slots, width, lanes), lambda i, b: (0, 0, i)),
            ],
            scratch_shapes=[pltpu.VMEM((lanes, width), f32)],
        ),
        out_shape=[
            jax.ShapeDtypeStruct((width, features), bf16),
            jax.ShapeDtypeStruct((slots, width, features), bf16),
            jax.ShapeDtypeStruct((slots, width, features), bf16),
        ],
        name="attend_back",
    )(bounds, queries, pairs, pairs, outputs, grads, lse, own_ids, slot_ids)


def norm_parts(inputs):
    centred = inputs - jnp.mean(inputs, axis=-1, keepdims=True)
    scale = lax.rsqrt(jnp.mean(centred * centred, axis=-1, keepdims=True) + ln_epsilon)
    return centred * scale, scale


def norm_back(grad, unit, scale, gain):
    inner = grad * gain
    return scale * (
        inner
        - jnp.mean(inner, axis=-1, keepdims=True)
        - unit * jnp.mean(inner * unit, axis=-1, keepdims=True)
    )


def adam_rule(master, moment, square, gradient, step_value, step_rate, weight_decay):
    moment_new = beta_one * moment + (1.0 - beta_one) * gradient
    square_new = beta_two * square + (1.0 - beta_two) * gradient * gradient
    fix_first = 1.0 - jnp.power(beta_one, step_value)
    fix_second = 1.0 - jnp.power(beta_two, step_value)
    planned = step_rate * jnp.minimum(1.0, step_value / warmup_length)
    direction = moment_new / fix_first / (jnp.sqrt(square_new / fix_second) + adam_epsilon)
    weight_new = master - planned * (direction + weight_decay * master)
    return (weight_new, moment_new, square_new, weight_new.astype(bf16))


def per_device(
    raw_input,
    cotangent,
    segment_ids,
    step_count,
    inlet_copy,
    inlet_master,
    inlet_moment,
    inlet_square,
    outlet_copy,
    outlet_master,
    outlet_moment,
    outlet_square,
    expand_copy,
    expand_master,
    expand_moment,
    expand_square,
    shrink_copy,
    shrink_master,
    shrink_moment,
    shrink_square,
    vector_copy,
    vector_master,
    vector_moment,
    vector_square,
):
    sequences, block_length, features = raw_input.shape
    assert sequences == 1
    group_size = lax.axis_size("blk")
    group_index = lax.axis_index("blk")
    owners = lax.axis_size("dp")
    total_tokens = owners * group_size * block_length
    reach = group_size // 2
    slots = 2 * reach + 1
    vectors = vector_copy.astype(f32)
    raw = raw_input.reshape(block_length, features)
    grad_down = cotangent.reshape(block_length, features)

    own_ids = segment_ids.astype(jnp.int32)
    slot_ids = [None] * slots
    slot_ids[reach] = own_ids
    ahead, behind = own_ids + 1, own_ids + 1
    for d in range(1, reach + 1):
        ahead, behind = moved(ahead, "blk", 1), moved(behind, "blk", -1)
        slot_ids[reach - d], slot_ids[reach + d] = ahead - 1, behind - 1
    slot_ids = jnp.concatenate(slot_ids, axis=0)
    active = (slot_ids[:, -1] >= own_ids[0, 0]) & (slot_ids[:, 0] <= own_ids[0, -1])
    places = jnp.arange(slots, dtype=jnp.int32)
    bounds = jnp.stack(
        [
            jnp.min(jnp.where(active, places, slots)),
            jnp.max(jnp.where(active, places + 1, 0)),
        ]
    ).astype(jnp.int32)
    slot_columns = slot_ids[:, :, None]

    band_totals = everywhere_sum(jnp.stack([jnp.sum(raw, axis=0), jnp.sum(raw * raw, axis=0)]))
    band_mean = band_totals[0] / total_tokens
    band_variance = band_totals[1] / total_tokens - band_mean * band_mean
    inverse_std = lax.rsqrt(band_variance + stat_epsilon)
    normed = (raw - band_mean) * inverse_std
    unit_one, scale_one = norm_parts(normed)
    first_in = (unit_one * vectors[0] + vectors[1]).astype(bf16)

    blocks = [None] * slots
    blocks[reach] = first_in
    ahead, behind = first_in, first_in
    for d in range(1, reach + 1):
        ahead, behind = moved(ahead, "blk", 1), moved(behind, "blk", -1)
        blocks[reach - d], blocks[reach + d] = ahead, behind
    stacked = jnp.concatenate(blocks, axis=0)

    queries = (
        (nn(first_in, inlet_copy[:, :features]) + vectors[4]) * score_scale
    ).astype(bf16)
    pair_bias = jnp.concatenate([jnp.zeros((features,), f32), vectors[5]])
    pairs = (nn(stacked, inlet_copy[:, features:]) + pair_bias).astype(bf16)
    pairs = pairs.reshape(slots, block_length, 2 * features)
    attended, lse = attend(bounds, queries, pairs, own_ids, slot_columns)
    attended_low = attended.astype(bf16)

    middle = normed + nn(attended_low, outlet_copy) + vectors[6]
    unit_two, scale_two = norm_parts(middle)
    second_in = (unit_two * vectors[2] + vectors[3]).astype(bf16)
    hidden_pre = nn(second_in, expand_copy) + vectors[8:12].reshape(-1)
    half_erf = 0.5 * (1.0 + lax.erf(hidden_pre * (0.5**0.5)))
    hidden = (hidden_pre * half_erf).astype(bf16)
    bell = jnp.exp(-0.5 * hidden_pre * hidden_pre) * (1.0 / (2.0 * jnp.pi) ** 0.5)
    slope = half_erf + hidden_pre * bell
    result = middle + nn(hidden, shrink_copy) + vectors[7]
    layer_output = result.astype(bf16).reshape(sequences, block_length, features)

    bits = bits_of("dp")
    order_one = bits
    order_two = bits[:1] + bits[:0:-1]

    shrink_grad = tn(hidden, grad_down).astype(bf16)
    shrink_share = owned_sum(shrink_grad, order_one)
    down_grad = jnp.sum(grad_down.astype(f32), axis=0)
    grad_pre = (slope * nt(grad_down, shrink_copy)).astype(bf16)
    expand_grad = tn(second_in, grad_pre).astype(bf16)
    expand_share = owned_sum(expand_grad, order_two)
    up_grad = jnp.sum(grad_pre.astype(f32), axis=0)
    grad_second = nt(grad_pre, expand_copy)
    gain_two = jnp.sum(grad_second * unit_two, axis=0)
    shift_two = jnp.sum(grad_second, axis=0)
    grad_middle = grad_down.astype(f32) + norm_back(grad_second, unit_two, scale_two, vectors[2])
    grad_branch = grad_middle.astype(bf16)
    outlet_grad = tn(attended_low, grad_branch).astype(bf16)
    outlet_share = owned_sum(outlet_grad, order_two)
    out_grad = jnp.sum(grad_branch.astype(f32), axis=0)
    grad_attended = nt(grad_branch, outlet_copy).astype(bf16)

    query_low, key_low, value_low = attend_back(
        bounds, queries, pairs, attended, grad_attended, lse, own_ids, slot_columns
    )
    tokens = slots * block_length
    key_low = key_low.reshape(tokens, features)
    value_low = value_low.reshape(tokens, features)
    inlet_grad = jnp.concatenate(
        [tn(first_in, query_low), tn(stacked, key_low), tn(stacked, value_low)], axis=1
    ).astype(bf16)
    middle_column = inlet_grad.shape[1] // 2
    inlet_share = jnp.concatenate(
        [
            owned_sum(inlet_grad[:, :middle_column], order_one),
            owned_sum(inlet_grad[:, middle_column:], order_two),
        ],
        axis=1,
    )
    query_grad = jnp.sum(query_low.astype(f32), axis=0)
    value_grad = jnp.sum(value_low.astype(f32), axis=0)

    parts = nt(key_low, inlet_copy[:, features : 2 * features]) + nt(
        value_low, inlet_copy[:, 2 * features :]
    )
    parts = parts.reshape(slots, block_length, features)
    to_left = parts[0].astype(bf16)
    to_right = parts[slots - 1].astype(bf16)
    for d in range(reach - 1, 0, -1):
        to_left = (parts[reach - d] + moved(to_left, "blk", -1).astype(f32)).astype(bf16)
        to_right = (parts[reach + d] + moved(to_right, "blk", 1).astype(f32)).astype(bf16)
    grad_first = (
        parts[reach]
        + nt(query_low, inlet_copy[:, :features])
        + moved(to_left, "blk", -1).astype(f32)
        + moved(to_right, "blk", 1).astype(f32)
    )
    gain_one = jnp.sum(grad_first * unit_one, axis=0)
    shift_one = jnp.sum(grad_first, axis=0)
    grad_normed = grad_middle + norm_back(grad_first, unit_one, scale_one, vectors[0])
    small = jnp.stack(
        [
            gain_one,
            shift_one,
            gain_two,
            shift_two,
            query_grad,
            value_grad,
            out_grad,
            down_grad,
        ]
        + [up_grad[i * features : (i + 1) * features] for i in range(4)]
        + [jnp.sum(grad_normed, axis=0), jnp.sum(grad_normed * (raw - band_mean), axis=0)]
    )
    small = everywhere_sum(small)
    back_totals = small[12:14]
    grad_variance = -0.5 * back_totals[1] * inverse_std * inverse_std * inverse_std
    grad_centre = -inverse_std * back_totals[0] - 2.0 * band_mean * grad_variance
    input_gradient = (
        grad_normed * inverse_std
        + grad_centre / total_tokens
        + 2.0 * grad_variance * raw / total_tokens
    ).reshape(sequences, block_length, features)
    owner = lax.axis_index("dp")
    columns = vector_master.shape[1]
    vector_share = lax.dynamic_slice_in_dim(small[:12], owner * columns, columns, 1)

    step_value = step_count[0].astype(f32)
    updates = []
    for master, moment, square, share in (
        (inlet_master, inlet_moment, inlet_square, inlet_share),
        (outlet_master, outlet_moment, outlet_square, outlet_share),
        (expand_master, expand_moment, expand_square, expand_share),
        (shrink_master, shrink_moment, shrink_square, shrink_share),
    ):
        updates.extend(
            adam_rule(
                master, moment, square, share.astype(f32), step_value, rate_matrix, decay_matrix
            )
        )
    updates.extend(
        adam_rule(
            vector_master, vector_moment, vector_square, vector_share, step_value, rate_vector, 0.0
        )
    )
    return (layer_output, input_gradient, band_mean, band_variance, *updates)


def solution(mesh):
    tokens = P("dp", "blk", None)
    rows = P("dp", None)
    columns = P(None, "dp")
    matrix = (P(), rows, rows, rows)
    return jax.shard_map(
        per_device,
        mesh=mesh,
        in_specs=(tokens, tokens, P("dp", "blk"), P())
        + matrix * 4
        + (P(), columns, columns, columns),
        out_specs=(tokens, tokens, P(), P()) + (rows,) * 16 + (columns,) * 4,
        check_vma=False,
    )
```

```python
import functools

import jax
import jax.numpy as jnp
from jax import lax
from jax.experimental import pallas as pl
from jax.experimental.pallas import tpu as pltpu
from jax.sharding import PartitionSpec as P

HEADS = 12
HEAD_WIDTH = 64
GROUP = 4

ln_epsilon = 1e-05
stat_epsilon = 1e-06
beta_one = 0.5
beta_two = 0.6
rate_matrix = 0.04
rate_vector = 0.8
warmup_length = 20.0
decay_matrix = 0.05
adam_epsilon = 1e-08
score_scale = 0.125
masked_score = -1e30

f32 = jnp.float32
bf16 = jnp.bfloat16


def nn(a, b):
    return lax.dot_general(a, b, (((1,), (0,)), ((), ())), preferred_element_type=f32)


def nt(a, b):
    return lax.dot_general(a, b, (((1,), (1,)), ((), ())), preferred_element_type=f32)


def tn(a, b):
    return lax.dot_general(a, b, (((0,), (0,)), ((), ())), preferred_element_type=f32)


def flipped(block, axis, bit):
    size = lax.axis_size(axis)
    return lax.ppermute(block, axis, [(i, i ^ bit) for i in range(size)])


def moved(block, axis, distance):
    size = lax.axis_size(axis)
    route = [(i, i + distance) for i in range(size) if 0 <= i + distance < size]
    return lax.ppermute(block, axis, route)


def bits_of(axis):
    size = lax.axis_size(axis)
    return [1 << i for i in range(size.bit_length() - 1)]


def everywhere_sum(block):
    for axis in ("dp", "blk"):
        bits = bits_of(axis)
        rounds = [bits[:1]] if len(bits) % 2 else []
        rounds += [bits[i : i + 2] for i in range(len(bits) % 2, len(bits), 2)]
        for part in rounds:
            if len(part) == 1:
                block = block + flipped(block, axis, part[0])
            else:
                low, high = part
                others = [flipped(block, axis, bit) for bit in (low, high, low | high)]
                block = (block + others[0]) + (others[1] + others[2])
    return block


def added(kept, arrived):
    return (kept.astype(f32) + arrived.astype(f32)).astype(bf16)


class Scatter:
    def __init__(self, block, order):
        self.block, self.order = block, list(order)
        self.left = list(bits_of("dp")[1:])

    def send(self):
        where = self.left.index(self.order.pop(0))
        bit = self.left.pop(where)
        self.keep = lax.index_in_dim(self.block, 0, where, keepdims=False)
        self.arrived = flipped(lax.index_in_dim(self.block, 1, where, keepdims=False), "dp", bit)

    def add(self):
        self.block = added(self.keep, self.arrived)


class Line:
    def __init__(self, first, second):
        self.bits = bits_of("blk")
        own = lax.axis_index("blk") % 2
        self.trail = []
        self.keep = jnp.where(own == 0, first, second)
        self.sent = jnp.where(own == 0, second, first)

    def scatter(self):
        self.arrived = flipped(self.sent, "blk", 1)

    def exchange(self):
        share = added(self.keep, self.arrived)
        for bit in self.bits[1:-1]:
            own = (lax.axis_index("blk") // bit) % 2
            parts = share.reshape(2, share.shape[0] // 2, share.shape[1])
            keep = lax.dynamic_index_in_dim(parts, own, 0, keepdims=False)
            sent = lax.dynamic_index_in_dim(parts, 1 - own, 0, keepdims=False)
            share = added(keep, flipped(sent, "blk", bit))
            self.trail.append((bit, own))
        self.keep = share
        self.arrived = flipped(share, "blk", self.bits[-1])

    def gather(self):
        share = added(self.keep, self.arrived)
        for bit, own in reversed(self.trail):
            other = flipped(share, "blk", bit)
            share = jnp.concatenate(
                [jnp.where(own == 0, share, other), jnp.where(own == 0, other, share)], axis=0
            )
        self.keep = share
        self.arrived = flipped(share, "blk", 1)

    def result(self):
        own = lax.axis_index("blk") % 2
        mine, other = self.keep, self.arrived
        return jnp.concatenate(
            [jnp.where(own == 0, mine, other), jnp.where(own == 0, other, mine)], axis=0
        )


def together(*values):
    return lax.optimization_barrier(values)


def whole(shape):
    return pl.BlockSpec(shape, lambda *a: (0,) * len(shape))


def call(kernel, name, grid, ins, outs, scratch, operands, table, aliases=None, flops=0, moved_bytes=0, mib=16):
    return pl.pallas_call(
        kernel,
        grid_spec=pltpu.PrefetchScalarGridSpec(
            num_scalar_prefetch=1,
            grid=grid,
            in_specs=[spec for spec, _ in ins],
            out_specs=[spec for spec, _ in outs],
            scratch_shapes=scratch,
        ),
        out_shape=[shape for _, shape in outs],
        input_output_aliases=aliases or {},
        cost_estimate=pl.CostEstimate(
            flops=flops, bytes_accessed=moved_bytes, transcendentals=0
        ),
        compiler_params=pltpu.CompilerParams(vmem_limit_bytes=mib << 20),
        name=name,
    )(table, *[operand for _, operand in ins])


def struct(shape, dtype):
    return jax.ShapeDtypeStruct(shape, dtype)


def unit_rows(rows):
    centred = rows - jnp.mean(rows, axis=-1, keepdims=True)
    scale = lax.rsqrt(jnp.mean(centred * centred, axis=-1, keepdims=True) + ln_epsilon)
    return centred * scale, scale


def norm_back(grad, unit, scale, gain):
    inner = grad * gain
    return scale * (
        inner
        - jnp.mean(inner, axis=-1, keepdims=True)
        - unit * jnp.mean(inner * unit, axis=-1, keepdims=True)
    )


def column_sum(rows):
    return jnp.sum(rows, axis=0, keepdims=True)


def totals_kernel(table, raw_ref, out_ref):
    raw = raw_ref[...]
    out_ref[0:1, :] = column_sum(raw)
    out_ref[1:2, :] = column_sum(raw * raw)


def enter_kernel(total_tokens, table, raw_ref, sum_ref, vec_ref, id_ref, x_ref, mean_ref, var_ref, std_ref):
    width = raw_ref.shape[0]
    mean = sum_ref[0:1, :] / total_tokens
    variance = sum_ref[1:2, :] / total_tokens - mean * mean
    inverse = lax.rsqrt(variance + stat_epsilon)
    mean_ref[...] = mean
    var_ref[...] = variance
    std_ref[...] = inverse
    unit, _ = unit_rows((raw_ref[...] - mean) * inverse)
    x_ref[0:width, :] = (unit * vec_ref[0:1, :] + vec_ref[1:2, :]).astype(bf16)
    x_ref[width:, :] = jnp.zeros((x_ref.shape[0] - width, x_ref.shape[1]), bf16)
    ids = jnp.broadcast_to(id_ref[...], (16, width)).astype(f32).astype(bf16)
    x_ref[width:, 0:width] = ids


def project_own_kernel(table, x_ref, w_ref, vec_ref, q_ref, kv_ref, id_ref):
    width = q_ref.shape[0]
    features = q_ref.shape[1]
    x = x_ref[0:width, :]
    q_ref[...] = (
        (nn(x, w_ref[:, :features]) + vec_ref[4:5, :]) * score_scale
    ).astype(bf16)
    kv_ref[0, :, :features] = nn(x, w_ref[:, features : 2 * features]).astype(bf16)
    kv_ref[0, :, features:] = (nn(x, w_ref[:, 2 * features :]) + vec_ref[5:6, :]).astype(bf16)
    id_ref[0] = id_columns(x_ref, width)


def id_columns(x_ref, width):
    rows = jnp.broadcast_to(x_ref[width : width + 8, 0:width].astype(f32)[0:1], (128, width))
    return rows.T


def project_pair_kernel(table, xa_ref, xb_ref, w_ref, vec_ref, kv_in, id_in, kv_ref, id_ref):
    width = kv_ref.shape[1]
    features = kv_ref.shape[2] // 2
    step = pl.program_id(0)

    def fill(x_ref, inside):
        x = x_ref[0:width, :]
        kv_ref[0, :, :features] = nn(x, w_ref[:, features : 2 * features]).astype(bf16)
        kv_ref[0, :, features:] = (nn(x, w_ref[:, 2 * features :]) + vec_ref[5:6, :]).astype(bf16)
        ids = id_columns(x_ref, width)
        id_ref[0] = jnp.where(inside > 0, ids, -1.0 - jnp.zeros_like(ids))

    @pl.when(step == 0)
    def _():
        fill(xa_ref, table[0])

    @pl.when(step == 1)
    def _():
        fill(xb_ref, table[1])


def lane_half(rows, which):
    lanes = lax.broadcasted_iota(jnp.int32, (rows, 128), 1)
    return (lanes >= 64) if which else (lanes < 64)


def attend_kernel(
    reach, table, q_ref, k_ref, v_ref, qid_ref, kid_ref, o_ref, lse_ref, bound_ref, acc, top, total
):
    width = q_ref.shape[0]
    slots = k_ref.shape[0]

    @pl.when(pl.program_id(0) == 0)
    def _():
        low = kid_ref[reach, 0:1, :]
        high = kid_ref[reach, width - 1 : width, :]
        start = jnp.full_like(low, float(reach))
        end = jnp.full_like(low, float(reach))
        for s in range(slots):
            active = (kid_ref[s, width - 1 : width, :] >= low) & (kid_ref[s, 0:1, :] <= high)
            start = jnp.where(active, jnp.minimum(start, float(s)), start)
            end = jnp.where(active, jnp.maximum(end, float(s)), end)
        bound_ref[0] = jnp.min(start).astype(jnp.int32)
        bound_ref[1] = jnp.max(end).astype(jnp.int32) + 1

    top[...] = jnp.full_like(top, masked_score)
    total[...] = jnp.zeros_like(total)
    acc[...] = jnp.zeros_like(acc)
    own = qid_ref[...].astype(f32)
    masked_q = []
    for h in range(GROUP):
        pair = q_ref[:, 128 * (h // 2) : 128 * (h // 2) + 128]
        masked_q.append(jnp.where(lane_half(width, h % 2), pair, jnp.zeros_like(pair)))

    def step(s, carry):
        keys = k_ref[s]
        values_t = v_ref[s].T
        column = kid_ref[s]
        allowed = jnp.concatenate([column] * (width // 128), axis=1) == own
        for h in range(GROUP):
            lanes = slice(128 * (h // 2), 128 * (h // 2) + 128)
            score = jnp.where(allowed, nt(keys[:, lanes], masked_q[h]), masked_score)
            old = top[h : h + 1, :]
            new = jnp.maximum(old, jnp.max(score, axis=0, keepdims=True))
            fade = jnp.exp(old - new)
            weight = jnp.exp(score - new)
            total[h : h + 1, :] = total[h : h + 1, :] * fade + column_sum(weight)
            top[h : h + 1, :] = new
            rows = slice(64 * h, 64 * h + 64)
            acc[rows, :] = acc[rows, :] * fade + nn(values_t[rows, :], weight.astype(bf16))
        return carry

    lax.fori_loop(bound_ref[0], bound_ref[1], step, 0)
    for h in range(GROUP):
        rows = slice(64 * h, 64 * h + 64)
        acc[rows, :] = acc[rows, :] / total[h : h + 1, :]
    o_ref[...] = acc[...].T.astype(bf16)
    lse_ref[0] = top[0:GROUP, :] + jnp.log(total[0:GROUP, :])


def ffn_kernel(
    half,
    table,
    o_ref,
    wo_ref,
    raw_ref,
    mean_ref,
    std_ref,
    vec_ref,
    cot_ref,
    w1_ref,
    w2_ref,
    ub_ref,
    middle_ref,
    out_ref,
    gsec_ref,
    sk_ref,
    ss_ref,
    ek_ref,
    es_ref,
    ug_ref,
    s2,
    s2t,
    plain_t,
    rows_s,
    acc,
):
    step = pl.program_id(0)
    features = middle_ref.shape[1]
    owners = 2 * half
    owned = features // owners

    @pl.when(step == 0)
    def _():
        normed = (raw_ref[...] - mean_ref[...]) * std_ref[...]
        middle = normed + nn(o_ref[...], wo_ref[...]) + vec_ref[6:7, :]
        middle_ref[...] = middle
        unit, _ = unit_rows(middle)
        second = unit * vec_ref[2:3, :] + vec_ref[3:4, :]
        s2[...] = second.astype(bf16)
        plain_t[...] = second.T.astype(bf16)
        for p in range(owners):
            place = pl.multiple_of(table[half + p] * owned, 16)
            s2t[owned * p : owned * p + owned, :] = plain_t[pl.ds(place, owned), :]
        acc[...] = jnp.zeros_like(acc)
        gsec_ref[...] = jnp.zeros_like(gsec_ref)

    pre = nn(s2[...], w1_ref[...]) + ub_ref[...]
    area = 0.5 * (1.0 + lax.erf(pre * (0.5**0.5)))
    bell = jnp.exp(-0.5 * pre * pre) * (1.0 / (2.0 * jnp.pi) ** 0.5)
    hidden = (pre * area).astype(bf16)
    grad = ((area + pre * bell) * nt(cot_ref[...], w2_ref[...])).astype(bf16)
    acc[...] += nn(hidden, w2_ref[...])
    gsec_ref[...] += nt(grad, w1_ref[...])
    ug_ref[...] = column_sum(grad.astype(f32))
    wide = rows_s.shape[0] // 2
    rows_s[...] = nn(hidden.T, cot_ref[...]).astype(bf16)
    own = table[half] % 2
    sk_ref[0] = rows_s[pl.ds(pl.multiple_of(own * wide, 16), wide), :]
    ss_ref[0] = rows_s[pl.ds(pl.multiple_of((1 - own) * wide, 16), wide), :]
    ek_ref[...] = nn(s2t[: features // 2, :], grad).astype(bf16)
    es_ref[...] = nn(s2t[features // 2 :, :], grad).astype(bf16)

    @pl.when(step == half - 1)
    def _():
        out_ref[...] = (middle_ref[...] + acc[...] + vec_ref[7:8, :]).astype(bf16)


def branch_kernel(table, gsec_ref, middle_ref, cot_ref, vec_ref, wo_ref, gm_ref, gb_ref, ga_ref, row_ref):
    unit, scale = unit_rows(middle_ref[...])
    grad = gsec_ref[...]
    cot = cot_ref[...].astype(f32)
    row_ref[0:1, :] = column_sum(grad * unit)
    row_ref[1:2, :] = column_sum(grad)
    grad_middle = cot + norm_back(grad, unit, scale, vec_ref[2:3, :])
    gm_ref[...] = grad_middle
    branch = grad_middle.astype(bf16)
    gb_ref[...] = branch
    row_ref[2:3, :] = column_sum(branch.astype(f32))
    row_ref[3:4, :] = column_sum(cot)
    ga_ref[...] = nt(branch, wo_ref[...]).astype(bf16)


def attend_back_kernel(
    bounds,
    q_ref,
    k_ref,
    v_ref,
    o_ref,
    g_ref,
    lse_ref,
    qid_ref,
    kid_ref,
    dq_ref,
    dk_ref,
    dv_ref,
    row_ref,
    acc,
):
    width = q_ref.shape[0]
    slots = k_ref.shape[0]
    acc[...] = jnp.zeros_like(acc)
    own = qid_ref[...].astype(f32)
    product = (g_ref[...].astype(f32) * o_ref[...].astype(f32)).T
    masked_q, masked_g, deltas, lses = [], [], [], []
    for h in range(GROUP):
        lanes = slice(128 * (h // 2), 128 * (h // 2) + 128)
        half = lane_half(width, h % 2)
        pair = q_ref[:, lanes]
        masked_q.append(jnp.where(half, pair, jnp.zeros_like(pair)))
        pair = g_ref[:, lanes]
        masked_g.append(jnp.where(half, pair, jnp.zeros_like(pair)))
        deltas.append(column_sum(product[64 * h : 64 * h + 64, :]))
        lses.append(lse_ref[0, h : h + 1, :])
    row_ref[...] = jnp.zeros_like(row_ref)

    def blank(s, carry):
        dk_ref[s] = jnp.zeros(dk_ref.shape[1:], dk_ref.dtype)
        dv_ref[s] = jnp.zeros(dv_ref.shape[1:], dv_ref.dtype)
        return carry

    lax.fori_loop(0, bounds[0], blank, 0)
    lax.fori_loop(bounds[1], slots, blank, 0)

    def step(s, carry):
        keys = k_ref[s]
        values = v_ref[s]
        keys_t = keys.T
        column = kid_ref[s]
        allowed = jnp.concatenate([column] * (width // 128), axis=1) == own
        for j in range(GROUP // 2):
            lanes = slice(128 * j, 128 * j + 128)
            key_part, value_part = None, None
            for h in (2 * j, 2 * j + 1):
                score = jnp.where(allowed, nt(keys[:, lanes], masked_q[h]), masked_score)
                prob = jnp.exp(score - lses[h])
                grad = (prob * (nt(values[:, lanes], masked_g[h]) - deltas[h])).astype(bf16)
                rows = slice(64 * h, 64 * h + 64)
                acc[rows, :] += nn(keys_t[rows, :], grad)
                k_now = nn(grad, masked_q[h])
                v_now = nn(prob.astype(bf16), masked_g[h])
                key_part = k_now if key_part is None else key_part + k_now
                value_part = v_now if value_part is None else value_part + v_now
            dk_ref[s, :, lanes] = key_part.astype(bf16)
            dv_ref[s, :, lanes] = value_part.astype(bf16)
            row_ref[1:2, lanes] += column_sum(value_part)
        return carry

    lax.fori_loop(bounds[0], bounds[1], step, 0)
    dq = (acc[...].T.astype(bf16).astype(f32) * score_scale).astype(bf16)
    dq_ref[...] = dq
    row_ref[0:1, :] = column_sum(dq.astype(f32))


def parts_kernel(reach, bounds, dq_ref, dk_ref, dv_ref, w_ref, p_ref, own_ref):
    step = pl.program_id(0)
    features = dq_ref.shape[1]
    slot = jnp.where(step % 2 == 0, step // 2, 2 * reach - step // 2)
    active = (slot >= bounds[0]) & (slot < bounds[1])

    @pl.when(jnp.logical_not(active))
    def _():
        p_ref[0] = jnp.zeros(p_ref.shape[1:], p_ref.dtype)

    @pl.when(active)
    def _():
        part = nt(dk_ref[0], w_ref[:, features : 2 * features]) + nt(
            dv_ref[0], w_ref[:, 2 * features :]
        )
        p_ref[0] = part.astype(bf16)

        @pl.when(step == 2 * reach)
        def _():
            own_ref[...] = part + nt(dq_ref[...], w_ref[:, :features])


def weight_kernel(reach, owners, table, *refs):
    slots = 2 * reach + 1
    xs = refs[:slots]
    dq_ref, dk_ref, dv_ref, o_ref, gb_ref, keep_ref, send_ref, xt, ot, plain = refs[slots:]
    width, features = dq_ref.shape
    owned = features // owners
    step = pl.program_id(0)

    def turn(rows, ref, lanes):
        plain[...] = rows.T
        for p in range(owners):
            place = pl.multiple_of(table[2 + p] * owned, 16)
            ref[owned * p : owned * p + owned, lanes] = plain[pl.ds(place, owned), :]

    @pl.when(step == 0)
    def _():
        for s in range(slots):
            turn(xs[s][0:width, :], xt, slice(width * s, width * s + width))
        turn(o_ref[...], ot, slice(0, width))
        own = slice(width * reach, width * reach + width)
        keep_ref[...] = nn(xt[: features // 2, own], dq_ref[...]).astype(bf16)
        send_ref[...] = nn(xt[features // 2 :, own], dq_ref[...]).astype(bf16)

    def summed(d_ref):
        few = min(3, slots)
        small = table[1] - table[0] <= few

        def over(start, size):
            lanes = pl.ds(pl.multiple_of(start * width, 128), size * width)
            rows = d_ref[pl.ds(start, size)].reshape(size * width, features)
            keep_ref[...] = nn(xt[: features // 2, lanes], rows).astype(bf16)
            send_ref[...] = nn(xt[features // 2 :, lanes], rows).astype(bf16)

        @pl.when(small)
        def _():
            over(jnp.minimum(table[0], slots - few), few)

        @pl.when(jnp.logical_not(small))
        def _():
            over(0, slots)

    @pl.when(step == 1)
    def _():
        summed(dk_ref)

    @pl.when(step == 2)
    def _():
        summed(dv_ref)

    @pl.when(step == 3)
    def _():
        keep_ref[...] = nn(ot[: features // 2, :], gb_ref[...]).astype(bf16)
        send_ref[...] = nn(ot[features // 2 :, :], gb_ref[...]).astype(bf16)


def leave_kernel(
    table,
    raw_ref,
    mean_ref,
    std_ref,
    vec_ref,
    gm_ref,
    own_ref,
    left_ref,
    right_ref,
    branch_rows,
    attend_rows,
    up_ref,
    gn_ref,
    row_ref,
):
    features = raw_ref.shape[1]
    centred = raw_ref[...] - mean_ref[...]
    unit, scale = unit_rows(centred * std_ref[...])
    grad = own_ref[...] + left_ref[...].astype(f32) + right_ref[...].astype(f32)
    row_ref[0:1, :] = column_sum(grad * unit)
    row_ref[1:2, :] = column_sum(grad)
    row_ref[2:4, :] = branch_rows[0:2, :]
    row_ref[4:6, :] = attend_rows[0:2, :]
    row_ref[6:8, :] = branch_rows[2:4, :]
    for r in range(4):
        row_ref[8 + r : 9 + r, :] = up_ref[0:1, r * features : (r + 1) * features]
    whole_grad = gm_ref[...] + norm_back(grad, unit, scale, vec_ref[0:1, :])
    gn_ref[...] = whole_grad
    row_ref[12:13, :] = column_sum(whole_grad)
    row_ref[13:14, :] = column_sum(whole_grad * centred)
    row_ref[14:16, :] = jnp.zeros((2, features), f32)


def adam_rule(master, moment, square, gradient, step_value, step_rate, weight_decay):
    moment_new = beta_one * moment + (1.0 - beta_one) * gradient
    square_new = beta_two * square + (1.0 - beta_two) * gradient * gradient
    fix_first = 1.0 - jnp.power(beta_one, step_value)
    fix_second = 1.0 - jnp.power(beta_two, step_value)
    planned = step_rate * jnp.minimum(1.0, step_value / warmup_length)
    direction = moment_new / fix_first / (jnp.sqrt(square_new / fix_second) + adam_epsilon)
    weight_new = master - planned * (direction + weight_decay * master)
    return (weight_new, moment_new, square_new, weight_new.astype(bf16))


def per_device(
    raw_input,
    cotangent,
    segment_ids,
    step_count,
    inlet_copy,
    inlet_master,
    inlet_moment,
    inlet_square,
    outlet_copy,
    outlet_master,
    outlet_moment,
    outlet_square,
    expand_copy,
    expand_master,
    expand_moment,
    expand_square,
    shrink_copy,
    shrink_master,
    shrink_moment,
    shrink_square,
    vector_copy,
    vector_master,
    vector_moment,
    vector_square,
):
    sequences, block_length, features = raw_input.shape
    assert sequences == 1
    width = block_length
    group_size = lax.axis_size("blk")
    group_index = lax.axis_index("blk")
    owners = lax.axis_size("dp")
    owner = lax.axis_index("dp")
    half = owners // 2
    total_tokens = owners * group_size * block_length
    reach = group_size // 2
    slots = 2 * reach + 1
    inner = expand_copy.shape[1]
    chunk = inner // half
    vectors = vector_copy.astype(f32)
    up_bias = vectors[8:12].reshape(1, inner)
    raw = raw_input.reshape(width, features)
    cot = cotangent.reshape(width, features)
    own_ids = segment_ids
    no_table = jnp.zeros((1,), jnp.int32)

    count = owners.bit_length() - 1

    def reversed_bits(value, size):
        return int(format(value, f"0{size}b")[::-1], 2) if size else 0

    pair_order = (owner // 2) ^ jnp.array(
        [reversed_bits(i, count - 1) for i in range(half)], jnp.int32
    )
    owner_order = owner ^ jnp.array([reversed_bits(i, count) for i in range(owners)], jnp.int32)
    table = jnp.concatenate([pair_order, owner_order])

    tokens = (width, features)
    row = (1, features)

    (totals,) = call(
        totals_kernel,
        "totals",
        (1,),
        [(whole(tokens), raw)],
        [(whole((2, features)), struct((2, features), f32))],
        [],
        None,
        no_table,
        mib=4,
    )
    totals = everywhere_sum(totals)
    packed = width + 16
    x, band_mean, band_variance, inverse_std = call(
        functools.partial(enter_kernel, total_tokens),
        "enter",
        (1,),
        [(whole(tokens), raw), (whole((2, features)), totals), (whole((12, features)), vectors), (whole((1, width)), own_ids)],
        [(whole((packed, features)), struct((packed, features), bf16))]
        + [(whole(row), struct(row, f32))] * 3,
        [],
        None,
        no_table,
        mib=8,
    )

    xs = [None] * slots
    xs[reach] = x
    wkv = 3 * features
    queries, pairs, columns = call(
        project_own_kernel,
        "project_own",
        (1,),
        [(whole((packed, features)), x), (whole((features, wkv)), inlet_copy), (whole((12, features)), vectors)],
        [
            (whole(tokens), struct(tokens, bf16)),
            (pl.BlockSpec((1, width, 2 * features), lambda i, t: (reach, 0, 0)), struct((slots, width, 2 * features), bf16)),
            (pl.BlockSpec((1, width, 128), lambda i, t: (reach, 0, 0)), struct((slots, width, 128), f32)),
        ],
        [],
        None,
        no_table,
        flops=2 * width * features * wkv,
        mib=12,
    )
    ahead, behind = x, x
    for d in range(1, reach + 1):
        ahead, behind = moved(ahead, "blk", 1), moved(behind, "blk", -1)
        xs[reach - d], xs[reach + d] = ahead, behind
        inside = jnp.stack([group_index >= d, group_index + d < group_size]).astype(jnp.int32)
        place = lambda i, t, d=d: (reach - d + 2 * d * i, 0, 0)
        pairs, columns = call(
            project_pair_kernel,
            "project_pair",
            (2,),
            [
                (whole((packed, features)), ahead),
                (whole((packed, features)), behind),
                (whole((features, wkv)), inlet_copy),
                (whole((12, features)), vectors),
                (pl.BlockSpec(memory_space=pl.ANY), pairs),
                (pl.BlockSpec(memory_space=pl.ANY), columns),
            ],
            [
                (pl.BlockSpec((1, width, 2 * features), place), struct(pairs.shape, bf16)),
                (pl.BlockSpec((1, width, 128), place), struct(columns.shape, f32)),
            ],
            [],
            None,
            inside,
            aliases={5: 0, 6: 1},
            flops=8 * width * features * features,
        mib=14,
    )

    lanes = GROUP * HEAD_WIDTH
    steps = features // lanes
    flat = pl.BlockSpec((width, lanes), lambda i, t: (0, i))
    first_part = pl.BlockSpec((slots, width, lanes), lambda i, t: (0, 0, i))
    second_part = pl.BlockSpec((slots, width, lanes), lambda i, t: (0, 0, i + steps))
    lse_spec = pl.BlockSpec((1, GROUP, width), lambda i, t: (i, 0, 0))
    attended, lse, bounds = call(
        functools.partial(attend_kernel, reach),
        "attend",
        (steps,),
        [
            (flat, queries),
            (first_part, pairs),
            (second_part, pairs),
            (whole((1, width)), own_ids),
            (whole(columns.shape), columns),
        ],
        [
            (flat, struct(tokens, bf16)),
            (lse_spec, struct((steps, GROUP, width), f32)),
            (pl.BlockSpec(memory_space=pltpu.SMEM), struct((2,), jnp.int32)),
        ],
        [pltpu.VMEM((lanes, width), f32), pltpu.VMEM((8, width), f32), pltpu.VMEM((8, width), f32)],
        None,
        no_table,
        flops=4 * slots * width * width * features,
        mib=10,
    )

    owned_wide = inner // owners
    middle, layer_output, grad_second, shrink_keep, shrink_send, expand_keep, expand_send, up_grad = call(
        functools.partial(ffn_kernel, half),
        "ffn",
        (half,),
        [
            (whole(tokens), attended),
            (whole((features, features)), outlet_copy),
            (whole(tokens), raw),
            (whole(row), band_mean),
            (whole(row), inverse_std),
            (whole((12, features)), vectors),
            (whole(tokens), cot),
            (pl.BlockSpec((features, chunk), lambda i, t: (0, t[i])), expand_copy),
            (pl.BlockSpec((chunk, features), lambda i, t: (t[i], 0)), shrink_copy),
            (pl.BlockSpec((1, chunk), lambda i, t: (0, t[i])), up_bias),
        ],
        [
            (whole(tokens), struct(tokens, f32)),
            (whole(tokens), struct(tokens, bf16)),
            (whole(tokens), struct(tokens, f32)),
            (pl.BlockSpec((1, owned_wide, features), lambda i, t: (i, 0, 0)), struct((half, owned_wide, features), bf16)),
            (pl.BlockSpec((1, owned_wide, features), lambda i, t: (i, 0, 0)), struct((half, owned_wide, features), bf16)),
            (pl.BlockSpec((features // 2, chunk), lambda i, t: (0, t[i])), struct((features // 2, inner), bf16)),
            (pl.BlockSpec((features // 2, chunk), lambda i, t: (0, t[i])), struct((features // 2, inner), bf16)),
            (pl.BlockSpec((1, chunk), lambda i, t: (0, t[i])), struct((1, inner), f32)),
        ],
        [
            pltpu.VMEM(tokens, bf16),
            pltpu.VMEM((features, width), bf16),
            pltpu.VMEM((features, width), bf16),
            pltpu.VMEM((chunk, features), bf16),
            pltpu.VMEM(tokens, f32),
        ],
        None,
        table,
        flops=12 * width * features * inner,
        mib=30,
    )
    bits = bits_of("dp")
    order_one, order_two = bits[1:], bits[:0:-1]
    relative = (2,) * (count - 1)
    owned = features // owners
    shrink_in = flipped(shrink_send, "dp", 1)
    expand_in = flipped(expand_send, "dp", 1)

    def scatters(block, rows):
        block = block.reshape(relative + (2, rows // 2, block.shape[-1]))
        return [
            Scatter(lax.index_in_dim(block, h, count - 1, keepdims=False), order)
            for h, order in ((0, order_one), (1, order_two))
        ]

    grad_middle, grad_branch, grad_attended, branch_rows = call(
        branch_kernel,
        "branch",
        (1,),
        [
            (whole(tokens), grad_second),
            (whole(tokens), middle),
            (whole(tokens), cot),
            (whole((12, features)), vectors),
            (whole((features, features)), outlet_copy),
        ],
        [
            (whole(tokens), struct(tokens, f32)),
            (whole(tokens), struct(tokens, bf16)),
            (whole(tokens), struct(tokens, bf16)),
            (whole((4, features)), struct((4, features), f32)),
        ],
        [],
        None,
        no_table,
        flops=2 * width * features * features,
        mib=10,
    )
    shrink_sum, expand_sum = added(shrink_keep, shrink_in), added(expand_keep, expand_in)
    shrink_sum, expand_sum, grad_attended = together(shrink_sum, expand_sum, grad_attended)
    first = scatters(shrink_sum, owned_wide)
    second = scatters(expand_sum, owned)
    for one in first + second:
        one.send()
    spread = (slots, width, features)
    query_low, key_low, value_low, attend_rows = call(
        attend_back_kernel,
        "attend_back",
        (steps,),
        [
            (flat, queries),
            (first_part, pairs),
            (second_part, pairs),
            (flat, attended),
            (flat, grad_attended),
            (lse_spec, lse),
            (whole((1, width)), own_ids),
            (whole(columns.shape), columns),
        ],
        [
            (flat, struct(tokens, bf16)),
            (first_part, struct(spread, bf16)),
            (first_part, struct(spread, bf16)),
            (pl.BlockSpec((2, lanes), lambda i, t: (0, i)), struct((2, features), f32)),
        ],
        [pltpu.VMEM((lanes, width), f32)],
        None,
        bounds,
        flops=10 * slots * width * width * features,
        mib=12,
    )

    query_low, key_low, value_low, first[0].arrived, first[1].arrived = together(
        query_low, key_low, value_low, first[0].arrived, first[1].arrived
    )
    for one in first:
        one.add()
        if one.order:
            one.send()

    def slot_at(i, t):
        return (jnp.where(i % 2 == 0, i // 2, 2 * reach - i // 2), 0, 0)

    one_slot = pl.BlockSpec((1, width, features), slot_at)
    parts, own_part = call(
        functools.partial(parts_kernel, reach),
        "parts",
        (slots,),
        [
            (whole(tokens), query_low),
            (one_slot, key_low),
            (one_slot, value_low),
            (whole((features, wkv)), inlet_copy),
        ],
        [(one_slot, struct(spread, bf16)), (whole(tokens), struct(tokens, f32))],
        [],
        None,
        bounds,
        flops=4 * slots * width * features * features,
        mib=14,
    )
    to_left, to_right = parts[0], parts[slots - 1]
    for d in range(reach - 1, 0, -1):
        to_left = added(parts[reach - d], moved(to_left, "blk", -1))
        to_right = added(parts[reach + d], moved(to_right, "blk", 1))
    from_right, from_left = moved(to_left, "blk", -1), moved(to_right, "blk", 1)

    from_right, from_left, query_low, key_low, value_low, second[0].arrived, second[1].arrived = (
        together(from_right, from_left, query_low, key_low, value_low, second[0].arrived, second[1].arrived)
    ) if False else (from_right, from_left, query_low, key_low, value_low, second[0].arrived, second[1].arrived)
    column_block = pl.BlockSpec((features // 2, features), lambda i, t: (0, i))
    inlet_keep, inlet_send = call(
        functools.partial(weight_kernel, reach, owners),
        "weights",
        (4,),
        [(whole((packed, features)), block) for block in xs]
        + [
            (whole(tokens), query_low),
            (whole(spread), key_low),
            (whole(spread), value_low),
            (whole(tokens), attended),
            (whole(tokens), grad_branch),
        ],
        [
            (column_block, struct((features // 2, 4 * features), bf16)),
            (column_block, struct((features // 2, 4 * features), bf16)),
        ],
        [
            pltpu.VMEM((features, slots * width), bf16),
            pltpu.VMEM((features, width), bf16),
            pltpu.VMEM((features, width), bf16),
        ],
        None,
        jnp.concatenate([bounds, owner_order]),
        flops=4 * (slots + 1) * width * features * features,
        mib=24,
    )
    inlet_in = flipped(inlet_send, "dp", 1)
    for one in second:
        one.add()
        if one.order:
            one.send()
    third = scatters(added(inlet_keep, inlet_in), owned)
    for one in first + second:
        while one.order:
            one.add()
            one.send()
        one.add()
    for one in third:
        one.send()
        while one.order:
            one.add()
            one.send()
        one.add()
    lines = [Line(a.block, b.block) for a, b in (first, second, third)]
    for line in lines:
        line.scatter()
        line.exchange()
        line.gather()
    shrink_share, expand_share, last_share = [line.result() for line in lines]

    grad_normed, small = call(
        leave_kernel,
        "leave",
        (1,),
        [
            (whole(tokens), raw),
            (whole(row), band_mean),
            (whole(row), inverse_std),
            (whole((12, features)), vectors),
            (whole(tokens), grad_middle),
            (whole(tokens), own_part),
            (whole(tokens), from_left),
            (whole(tokens), from_right),
            (whole((4, features)), branch_rows),
            (whole((2, features)), attend_rows),
            (whole((1, inner)), up_grad),
        ],
        [(whole(tokens), struct(tokens, f32)), (whole((16, features)), struct((16, features), f32))],
        [],
        None,
        no_table,
        mib=12,
    )
    small = everywhere_sum(small)
    back_totals = small[12:14]
    mean, inverse = band_mean[0], inverse_std[0]
    grad_variance = -0.5 * back_totals[1] * inverse * inverse * inverse
    grad_centre = -inverse * back_totals[0] - 2.0 * mean * grad_variance
    input_gradient = (
        grad_normed * inverse
        + grad_centre / total_tokens
        + 2.0 * grad_variance * raw / total_tokens
    ).reshape(sequences, block_length, features)
    column_count = vector_master.shape[1]
    vector_share = lax.dynamic_slice_in_dim(small[:12], owner * column_count, column_count, 1)

    step_value = step_count[0].astype(f32)
    updates = []
    for master, moment, square, share in (
        (inlet_master, inlet_moment, inlet_square, last_share[:, :wkv]),
        (outlet_master, outlet_moment, outlet_square, last_share[:, wkv:]),
        (expand_master, expand_moment, expand_square, expand_share),
        (shrink_master, shrink_moment, shrink_square, shrink_share),
    ):
        updates.extend(
            adam_rule(
                master, moment, square, share.astype(f32), step_value, rate_matrix, decay_matrix
            )
        )
    updates.extend(
        adam_rule(
            vector_master, vector_moment, vector_square, vector_share, step_value, rate_vector, 0.0
        )
    )
    layer_output = layer_output.reshape(sequences, block_length, features)
    return (layer_output, input_gradient, band_mean[0], band_variance[0], *updates)


def solution(mesh):
    tokens = P("dp", "blk", None)
    rows = P("dp", None)
    columns = P(None, "dp")
    matrix = (P(), rows, rows, rows)
    return jax.shard_map(
        per_device,
        mesh=mesh,
        in_specs=(tokens, tokens, P("dp", "blk"), P())
        + matrix * 4
        + (P(), columns, columns, columns),
        out_specs=(tokens, tokens, P(), P()) + (rows,) * 16 + (columns,) * 4,
        check_vma=False,
    )
```

```python
import functools

import jax
import jax.numpy as jnp
from jax import lax
from jax.experimental import pallas as pl
from jax.experimental.pallas import tpu as pltpu
from jax.sharding import PartitionSpec as P

HEADS = 12
HEAD_WIDTH = 64
GROUP = 4

ln_epsilon = 1e-05
stat_epsilon = 1e-06
beta_one = 0.5
beta_two = 0.6
rate_matrix = 0.04
rate_vector = 0.8
warmup_length = 20.0
decay_matrix = 0.05
adam_epsilon = 1e-08
score_scale = 0.125
masked_score = -1e30

f32 = jnp.float32
bf16 = jnp.bfloat16


def nn(a, b):
    return lax.dot_general(a, b, (((1,), (0,)), ((), ())), preferred_element_type=f32)


def nt(a, b):
    return lax.dot_general(a, b, (((1,), (1,)), ((), ())), preferred_element_type=f32)


def tn(a, b):
    return lax.dot_general(a, b, (((0,), (0,)), ((), ())), preferred_element_type=f32)


def flipped(block, axis, bit):
    size = lax.axis_size(axis)
    return lax.ppermute(block, axis, [(i, i ^ bit) for i in range(size)])


def moved(block, axis, distance):
    size = lax.axis_size(axis)
    route = [(i, i + distance) for i in range(size) if 0 <= i + distance < size]
    return lax.ppermute(block, axis, route)


def bits_of(axis):
    size = lax.axis_size(axis)
    return [1 << i for i in range(size.bit_length() - 1)]


class SmallSum:
    def __init__(self, block, paired=True):
        self.block, self.rounds = block, []
        for axis in ("dp", "blk"):
            bits = bits_of(axis)
            odd = len(bits) % 2 if paired else len(bits)
            if not paired:
                self.rounds += [(axis, [bit]) for bit in bits]
                continue
            parts = [bits[:odd]] * odd + [bits[i : i + 2] for i in range(odd, len(bits), 2)]
            self.rounds += [(axis, part) for part in parts]

    def left(self):
        return len(self.rounds)

    def send(self):
        axis, part = self.rounds.pop(0)
        ways = part if len(part) == 1 else [part[0], part[1], part[0] | part[1]]
        self.arrived = [flipped(self.block, axis, way) for way in ways]

    def take(self, tie=lambda *values: values):
        others = tie(*self.arrived)
        if len(others) == 1:
            self.block = self.block + others[0]
        else:
            self.block = (self.block + others[0]) + (others[1] + others[2])


def added(kept, arrived):
    return (kept.astype(f32) + arrived.astype(f32)).astype(bf16)


def summed(addends):
    total = addends[0].astype(f32)
    for addend in addends[1:]:
        total = total + addend.astype(f32)
    return total.astype(bf16)


class Scatter:
    def __init__(self, addends, order):
        self.addends, self.order = list(addends), list(order)

    def prepare(self):
        self.sent = summed([addend[1] for addend in self.addends])

    def send(self):
        self.arrived = flipped(self.sent, "dp", self.order.pop(0))

    def take(self):
        self.addends = [addend[0] for addend in self.addends] + [self.arrived]


class Line:
    def __init__(self, first, second, lows):
        self.bits, self.lows = bits_of("blk"), lows
        first, second = summed(first.addends), summed(second.addends)
        self.keep = jnp.where(lows[0], first, second)
        self.sent = jnp.where(lows[0], second, first)

    def scatter(self):
        self.arrived = flipped(self.sent, "blk", 1)

    def exchange(self):
        share = added(self.keep, self.arrived)
        for bit, low in zip(self.bits[1:-1], self.lows[1:]):
            middle = share.shape[0] // 2
            keep = jnp.where(low, share[:middle], share[middle:])
            sent = jnp.where(low, share[middle:], share[:middle])
            share = added(keep, flipped(sent, "blk", bit))
        self.keep = share
        self.arrived = flipped(share, "blk", self.bits[-1])

    def joined(self, low):
        mine, other = self.keep, self.arrived
        return jnp.concatenate(
            [jnp.where(low, mine, other), jnp.where(low, other, mine)], axis=0
        )

    def gather(self):
        share = added(self.keep, self.arrived)
        for bit, low in reversed(list(zip(self.bits[1:-1], self.lows[1:]))):
            self.keep, self.arrived = share, flipped(share, "blk", bit)
            share = self.joined(low)
        self.keep = share
        self.arrived = flipped(share, "blk", 1)

    def result(self):
        return self.joined(self.lows[0])


def together(*values):
    return lax.optimization_barrier(values)


def whole(shape):
    return pl.BlockSpec(shape, lambda *a: (0,) * len(shape))


def call(kernel, name, table, operands, outs, scratch=(), mib=8):
    scalar = pl.BlockSpec(memory_space=pltpu.SMEM)
    return pl.pallas_call(
        kernel,
        grid_spec=pltpu.PrefetchScalarGridSpec(
            num_scalar_prefetch=1,
            grid=(1,),
            in_specs=[
                spec if isinstance(spec, pl.BlockSpec) else whole(spec.shape)
                for spec in (o[0] if isinstance(o, tuple) else o for o in operands)
            ],
            out_specs=[scalar if o.shape == (2,) else whole(o.shape) for o in outs],
            scratch_shapes=list(scratch),
        ),
        out_shape=outs,
        cost_estimate=pl.CostEstimate(flops=1 << 20, bytes_accessed=1 << 16, transcendentals=0),
        compiler_params=pltpu.CompilerParams(vmem_limit_bytes=mib << 20),
        name=name,
    )(table, *[o[1] if isinstance(o, tuple) else o for o in operands])


def struct(shape, dtype):
    return jax.ShapeDtypeStruct(shape, dtype)


def unit_rows(rows):
    centred = rows - jnp.mean(rows, axis=-1, keepdims=True)
    scale = lax.rsqrt(jnp.mean(centred * centred, axis=-1, keepdims=True) + ln_epsilon)
    return centred * scale, scale


def norm_back(grad, unit, scale, gain):
    inner = grad * gain
    return scale * (
        inner
        - jnp.mean(inner, axis=-1, keepdims=True)
        - unit * jnp.mean(inner * unit, axis=-1, keepdims=True)
    )


def column_sum(rows):
    return jnp.sum(rows, axis=0, keepdims=True)


def totals_kernel(table, raw_ref, out_ref):
    raw = raw_ref[...]
    out_ref[0:1, :] = column_sum(raw)
    out_ref[1:2, :] = column_sum(raw * raw)


def enter_kernel(total_tokens, table, raw_ref, sum_ref, vec_ref, id_ref, x_ref, mean_ref, std_ref):
    width = raw_ref.shape[0]
    mean = sum_ref[0:1, :] / total_tokens
    variance = sum_ref[1:2, :] / total_tokens - mean * mean
    inverse = lax.rsqrt(variance + stat_epsilon)
    mean_ref[...] = mean
    std_ref[...] = inverse
    unit, _ = unit_rows((raw_ref[...] - mean) * inverse)
    x_ref[0:width, :] = (unit * vec_ref[0:1, :] + vec_ref[1:2, :]).astype(bf16)
    x_ref[width:, :] = jnp.zeros((x_ref.shape[0] - width, x_ref.shape[1]), bf16)
    ids = jnp.broadcast_to(id_ref[...], (16, width)).astype(f32).astype(bf16)
    x_ref[width:, 0:width] = ids


def id_columns(x_ref, width):
    rows = jnp.broadcast_to(x_ref[width : width + 8, 0:width].astype(f32)[0:1], (128, width))
    return rows.T


def project_own_kernel(table, x_ref, w_ref, vec_ref, q_ref, kv_ref, id_ref):
    width = q_ref.shape[0]
    features = q_ref.shape[1]
    slot = kv_ref.shape[0] // 2
    x = x_ref[0:width, :]
    q_ref[...] = ((nn(x, w_ref[:, :features]) + vec_ref[4:5, :]) * score_scale).astype(bf16)
    kv_ref[slot, :, :features] = nn(x, w_ref[:, features : 2 * features]).astype(bf16)
    kv_ref[slot, :, features:] = (nn(x, w_ref[:, 2 * features :]) + vec_ref[5:6, :]).astype(bf16)
    id_ref[slot] = id_columns(x_ref, width)


def project_pair_kernel(d, inside_at, table, xa_ref, xb_ref, x_ref, w_ref, vec_ref, kv_in, id_in, kv_ref, id_ref):
    width = kv_ref.shape[1]
    features = kv_ref.shape[2] // 2
    reach = kv_ref.shape[0] // 2
    done = slice(reach - d + 1, reach + d)
    kv_ref[done] = kv_in[done]
    id_ref[done] = id_in[done]
    own = x_ref[width : width + 8, 0:width].astype(f32)[0:1]
    low, high = jnp.min(own), jnp.max(own)
    for slot, inside, ref in ((reach - d, 0, xa_ref), (reach + d, 1, xb_ref)):
        ids = ref[width : width + 8, 0:width].astype(f32)[0:1]
        near = (table[inside_at + inside] > 0) & (jnp.max(ids) >= low) & (jnp.min(ids) <= high)
        id_ref[slot] = jnp.full((width, 128), -1.0, f32)

        @pl.when(near)
        def _(ref=ref, slot=slot):
            x = ref[0:width, :]
            kv_ref[slot, :, :features] = nn(x, w_ref[:, features : 2 * features]).astype(bf16)
            kv_ref[slot, :, features:] = (
                nn(x, w_ref[:, 2 * features :]) + vec_ref[5:6, :]
            ).astype(bf16)
            id_ref[slot] = id_columns(ref, width)


def lane_half(rows, which):
    lanes = lax.broadcasted_iota(jnp.int32, (rows, 128), 1)
    return (lanes >= 64) if which else (lanes < 64)


def mask_rows(own_row, width):
    ids = lax.broadcasted_iota(jnp.int32, (64, width), 0).astype(f32)
    return jnp.where(ids == own_row, 0.0, masked_score).astype(bf16)


def key_marks(column, width):
    lane_ids = (lax.broadcasted_iota(jnp.int32, (width, 128), 1) % 64).astype(f32)
    return (column == lane_ids).astype(f32).astype(bf16)


def lane_group(g):
    return pl.ds(pl.multiple_of(g * GROUP * HEAD_WIDTH, 128), GROUP * HEAD_WIDTH)


def attend_kernel(reach, table, q_ref, kv_ref, qid_ref, kid_ref, o_ref, lse_ref, bound_ref, acc, top, qm, sc):
    width, features = q_ref.shape
    slots = kv_ref.shape[0]
    steps = features // (GROUP * HEAD_WIDTH)
    low = kid_ref[reach, 0:1, :]
    high = kid_ref[reach, width - 1 : width, :]
    start = jnp.full_like(low, float(reach))
    end = jnp.full_like(low, float(reach))
    for s in range(slots):
        active = (kid_ref[s, width - 1 : width, :] >= low) & (kid_ref[s, 0:1, :] <= high)
        start = jnp.where(active, jnp.minimum(start, float(s)), start)
        end = jnp.where(active, jnp.maximum(end, float(s)), end)
    bound_ref[0] = jnp.min(start).astype(jnp.int32)
    bound_ref[1] = jnp.max(end).astype(jnp.int32) + 1
    barred = mask_rows(qid_ref[...].astype(f32), width)
    upper = lane_half(width, 1)
    one_rows = (lax.broadcasted_iota(jnp.int32, (16, width), 0) == 0).astype(f32).astype(bf16)

    def group(g, carry):
        lanes_g = lane_group(g)
        lanes_v = pl.ds(pl.multiple_of(features + g * GROUP * HEAD_WIDTH, 128), GROUP * HEAD_WIDTH)
        top[...] = jnp.full_like(top, masked_score)
        acc[...] = jnp.zeros_like(acc)
        q_t = q_ref[:, lanes_g].T
        for h in range(GROUP):
            head = q_t[64 * h : 64 * h + 64, :]
            qm[h, 0:64, :] = barred if h % 2 else head
            qm[h, 64:128, :] = head if h % 2 else barred

        def step(s, carry):
            keys = kv_ref[s, :, lanes_g]
            values_t = kv_ref[s, :, lanes_v].T
            marks = key_marks(kid_ref[s], width)
            for h in range(GROUP):
                lanes = slice(128 * (h // 2), 128 * (h // 2) + 128)
                pair = keys[:, lanes]
                marked = jnp.where(upper, pair, marks) if h % 2 else jnp.where(upper, marks, pair)
                sc[h] = nn(marked, qm[h])
            for h in range(GROUP):
                score = sc[h]
                old = top[h : h + 1, :]
                new = jnp.maximum(old, jnp.max(score, axis=0, keepdims=True))
                fade = jnp.exp(old - new)
                weight = jnp.exp(score - new).astype(bf16)
                top[h : h + 1, :] = new
                rows = slice(80 * h, 80 * h + 80)
                left = jnp.concatenate([values_t[64 * h : 64 * h + 64, :], one_rows], axis=0)
                acc[rows, :] = acc[rows, :] * fade + nn(left, weight)
            return carry

        lax.fori_loop(bound_ref[0], bound_ref[1], step, 0)
        outs, lses = [], []
        for h in range(GROUP):
            total = acc[80 * h + 64 : 80 * h + 65, :]
            outs.append(acc[80 * h : 80 * h + 64, :] / total)
            lses.append(top[h : h + 1, :] + jnp.log(total))
        o_ref[:, lanes_g] = jnp.concatenate(outs, axis=0).T.astype(bf16)
        lse_ref[g] = jnp.concatenate(lses, axis=0)
        return carry

    lax.fori_loop(0, steps, group, 0)


def spread_rows(table, plain, target, lanes, half):
    part = plain.shape[0] // (4 * half)
    for side in range(2):
        for h in range(2):
            for p in range(half):
                owner = table[half * (1 + 2 * h + side) + p]
                place = pl.multiple_of((2 * owner + h) * part, 8)
                to = ((side * 2 + h) * half + p) * part
                target[to : to + part, lanes] = plain[pl.ds(place, part), :].astype(bf16)


def ffn_kernel(
    half,
    table,
    o_ref,
    wo_ref,
    raw_ref,
    mean_ref,
    std_ref,
    vec_ref,
    cot_ref,
    w1_ref,
    w2_ref,
    out_ref,
    gm_ref,
    ga_ref,
    sk_ref,
    ss_ref,
    ek_ref,
    es_ref,
    row_ref,
    middle_s,
    gsec,
    s2,
    s2t,
    ot,
    plain,
    rows_s,
    acc,
):
    features = gm_ref.shape[1]
    inner = w1_ref.shape[1]
    chunk = inner // half
    wide = chunk // 2
    normed = (raw_ref[...] - mean_ref[...]) * std_ref[...]
    middle = normed + nn(o_ref[...], wo_ref[...]) + vec_ref[6:7, :]
    middle_s[...] = middle
    unit, _ = unit_rows(middle)
    second = unit * vec_ref[2:3, :] + vec_ref[3:4, :]
    s2[...] = second.astype(bf16)
    plain[...] = second.T
    spread_rows(table, plain, s2t, slice(None), half)
    plain[...] = o_ref[...].T.astype(f32)
    spread_rows(table, plain, ot, slice(None), half)
    acc[...] = jnp.zeros_like(acc)
    gsec[...] = jnp.zeros_like(gsec)
    own = table[half] % 2

    def step(i, carry):
        place = table[i] * chunk
        lanes = pl.ds(pl.multiple_of(place, 128), chunk)
        row = pl.ds(8 + place // features, 1)
        row_lanes = pl.ds(pl.multiple_of(place % features, 128), chunk)
        w1 = w1_ref[:, lanes]
        w2 = w2_ref[lanes, :]
        pre = nn(s2[...], w1) + vec_ref[row, row_lanes]
        back = nt(cot_ref[...], w2)
        area = 0.5 * (1.0 + lax.erf(pre * (0.5**0.5)))
        bell = jnp.exp(-0.5 * pre * pre) * (1.0 / (2.0 * jnp.pi) ** 0.5)
        hidden = (pre * area).astype(bf16)
        grad = ((area + pre * bell) * back).astype(bf16)
        acc[...] += nn(hidden, w2)
        gsec[...] += nt(grad, w1)
        row_ref[row, row_lanes] = column_sum(grad.astype(f32))
        rows_s[...] = nn(hidden.T, cot_ref[...]).astype(bf16)
        for side, ref in ((0, sk_ref), (1, ss_ref)):
            first = jnp.where(own == side, 0, wide)
            for h, at in ((0, i), (1, table[5 * half + i])):
                start = pl.multiple_of(first + h * (wide // 2), 16)
                ref[h, at] = rows_s[pl.ds(start, wide // 2), :]
        ek_ref[:, lanes] = nn(s2t[: features // 2, :], grad).astype(bf16)
        es_ref[:, lanes] = nn(s2t[features // 2 :, :], grad).astype(bf16)
        return carry

    lax.fori_loop(0, half, step, 0)
    out_ref[...] = (middle_s[...] + acc[...] + vec_ref[7:8, :]).astype(bf16)
    unit, scale = unit_rows(middle_s[...])
    grad = gsec[...]
    cot = cot_ref[...].astype(f32)
    row_ref[0:1, :] = column_sum(grad * unit)
    row_ref[1:2, :] = column_sum(grad)
    grad_middle = cot + norm_back(grad, unit, scale, vec_ref[2:3, :])
    gm_ref[...] = grad_middle
    branch = grad_middle.astype(bf16)
    row_ref[2:3, :] = column_sum(branch.astype(f32))
    row_ref[3:4, :] = column_sum(cot)
    ga_ref[...] = nt(branch, wo_ref[...]).astype(bf16)
    ek_ref[:, inner:] = nn(ot[: features // 2, :], branch).astype(bf16)
    es_ref[:, inner:] = nn(ot[features // 2 :, :], branch).astype(bf16)


def attend_back_kernel(
    g,
    bounds,
    q_ref,
    kv_ref,
    o_ref,
    g_ref,
    lse_ref,
    qid_ref,
    kid_ref,
    dq_ref,
    dk_ref,
    dv_ref,
    row_ref,
    acc,
    qm,
    gm,
    q_stack,
    g_stack,
    sc,
    dp,
    p_wide,
    g_wide,
    rows_s,
):
    width, features = q_ref.shape
    slots = kv_ref.shape[0]
    barred = mask_rows(qid_ref[...].astype(f32), width)
    nothing = jnp.zeros((64, width), bf16)
    upper = lane_half(width, 1)

    def blank(s, carry):
        dk_ref[s] = jnp.zeros(dk_ref.shape[1:], dk_ref.dtype)
        dv_ref[s] = jnp.zeros(dv_ref.shape[1:], dv_ref.dtype)
        return carry

    lax.fori_loop(0, bounds[0], blank, 0)
    lax.fori_loop(bounds[1], slots, blank, 0)

    base = g * GROUP * HEAD_WIDTH
    lanes_g = slice(base, base + GROUP * HEAD_WIDTH)
    lanes_v = slice(features + base, features + base + GROUP * HEAD_WIDTH)
    acc[...] = jnp.zeros_like(acc)
    q_all, g_all = q_ref[:, lanes_g], g_ref[:, lanes_g]
    product = (g_all.astype(f32) * o_ref[:, lanes_g].astype(f32)).T
    q_t, g_t = q_all.T, g_all.T
    for h in range(GROUP):
        lanes = slice(128 * (h // 2), 128 * (h // 2) + 128)
        rows = slice(64 * h, 64 * h + 64)
        odd = h % 2
        qm[h, 0:64, :] = barred if odd else q_t[rows, :]
        qm[h, 64:128, :] = q_t[rows, :] if odd else barred
        gm[h, 0:64, :] = nothing if odd else g_t[rows, :]
        gm[h, 64:128, :] = g_t[rows, :] if odd else nothing
        half = lane_half(width, odd)
        place = slice(width * odd, width * odd + width)
        pair = q_all[:, lanes]
        q_stack[h // 2, place, :] = jnp.where(half, pair, jnp.zeros_like(pair))
        pair = g_all[:, lanes]
        g_stack[h // 2, place, :] = jnp.where(half, pair, jnp.zeros_like(pair))
        rows_s[h : h + 1, :] = column_sum(product[rows, :])
    rows_s[8:9, :] = jnp.zeros((1, GROUP * HEAD_WIDTH), f32)

    def step(s, carry):
        keys = kv_ref[s, :, lanes_g]
        values = kv_ref[s, :, lanes_v]
        keys_t = keys.T
        marks = key_marks(kid_ref[s], width)
        for h in range(GROUP):
            lanes = slice(128 * (h // 2), 128 * (h // 2) + 128)
            pair = keys[:, lanes]
            marked = jnp.where(upper, pair, marks) if h % 2 else jnp.where(upper, marks, pair)
            sc[h] = nn(marked, qm[h])
            dp[h] = nn(values[:, lanes], gm[h])
        for h in range(GROUP):
            place = slice(width * (h % 2), width * (h % 2) + width)
            prob = jnp.exp(sc[h] - lse_ref[g, h : h + 1, :])
            p_wide[h // 2, :, place] = prob.astype(bf16)
            g_wide[h // 2, :, place] = (prob * (dp[h] - rows_s[h : h + 1, :])).astype(bf16)
        for h in range(GROUP):
            place = slice(width * (h % 2), width * (h % 2) + width)
            rows = slice(64 * h, 64 * h + 64)
            acc[rows, :] += nn(keys_t[rows, :], g_wide[h // 2, :, place])
        key_parts, value_parts = [], []
        for j in range(GROUP // 2):
            value_parts.append(nn(p_wide[j], g_stack[j]))
            key_parts.append(nn(g_wide[j], q_stack[j]))
        value_all = jnp.concatenate(value_parts, axis=1)
        dk_ref[s] = jnp.concatenate(key_parts, axis=1).astype(bf16)
        dv_ref[s] = value_all.astype(bf16)
        rows_s[8:9, :] += column_sum(value_all)
        return carry

    lax.fori_loop(bounds[0], bounds[1], step, 0)
    dq = (acc[...].T.astype(bf16).astype(f32) * score_scale).astype(bf16)
    dq_ref[...] = dq
    row_ref[0:1, :] = column_sum(dq.astype(f32))
    row_ref[1:2, :] = rows_s[8:9, :]


def parts_kernel(reach, bounds, *refs):
    groups = (len(refs) - 3) // 3
    dqs, dks, dvs = (refs[k * groups : (k + 1) * groups] for k in range(3))
    w_ref, p_ref, own_ref = refs[3 * groups :]
    features = p_ref.shape[2]
    size = features // groups

    def part(s):
        total = None
        for g in range(groups):
            for ref, base in ((dks[g], features), (dvs[g], 2 * features)):
                now = nt(ref[s], w_ref[:, base + g * size : base + (g + 1) * size])
                total = now if total is None else total + now
        return total

    def one(s, to):
        active = (s >= bounds[0]) & (s < bounds[1])

        @pl.when(active)
        def _():
            p_ref[to] = part(s).astype(bf16)

        @pl.when(jnp.logical_not(active))
        def _():
            p_ref[to] = jnp.zeros(p_ref.shape[1:], p_ref.dtype)

    def some(i, carry):
        one(jnp.where(i < reach, i, i + 1), i)
        return carry

    lax.fori_loop(0, 2 * reach, some, 0)
    total = part(reach)
    for g in range(groups):
        total = total + nt(dqs[g][...], w_ref[:, g * size : (g + 1) * size])
    own_ref[...] = total


def weight_kernel(reach, half, groups, table, *refs):
    slots = 2 * reach + 1
    xs, bounds = refs[:slots], refs[slots]
    refs = refs[slots + 1 :]
    dqs, dks, dvs = (refs[k * groups : (k + 1) * groups] for k in range(3))
    keep_ref, send_ref, xt, plain = refs[3 * groups :]
    width, size = dqs[0].shape
    features = size * groups
    few = min(3, slots)
    small = bounds[1] - bounds[0] <= few
    start = jnp.minimum(bounds[0], slots - few)

    for s in range(slots):

        @pl.when(jnp.logical_not(small) | ((s >= start) & (s < start + few)))
        def _(s=s):
            plain[...] = xs[s][0:width, :].T.astype(f32)
            spread_rows(table, plain, xt, slice(width * s, width * s + width), half)

    def put(tokens, right, base):
        lanes = slice(base, base + size)
        keep_ref[:, lanes] = nn(xt[: features // 2, tokens], right).astype(bf16)
        send_ref[:, lanes] = nn(xt[features // 2 :, tokens], right).astype(bf16)

    for g in range(groups):
        put(slice(width * reach, width * reach + width), dqs[g][...], g * size)

    def over(start, count):
        tokens = pl.ds(pl.multiple_of(start * width, 128), count * width)
        for base, group in ((features, dks), (2 * features, dvs)):
            for g in range(groups):
                rows = group[g][pl.ds(start, count)].reshape(count * width, size)
                put(tokens, rows, base + g * size)

    @pl.when(small)
    def _():
        over(start, few)

    @pl.when(jnp.logical_not(small))
    def _():
        over(0, slots)


def leave_kernel(
    table,
    raw_ref,
    mean_ref,
    std_ref,
    vec_ref,
    gm_ref,
    own_ref,
    left_ref,
    right_ref,
    ffn_rows,
    *refs,
):
    attend_rows, (gn_ref, row_ref) = refs[:-2], refs[-2:]
    features = raw_ref.shape[1]
    centred = raw_ref[...] - mean_ref[...]
    unit, scale = unit_rows(centred * std_ref[...])
    grad = own_ref[...] + left_ref[...].astype(f32) + right_ref[...].astype(f32)
    row_ref[0:1, :] = column_sum(grad * unit)
    row_ref[1:2, :] = column_sum(grad)
    row_ref[2:4, :] = ffn_rows[0:2, :]
    size = features // len(attend_rows)
    for g, ref in enumerate(attend_rows):
        row_ref[4:6, g * size : (g + 1) * size] = ref[...]
    row_ref[6:8, :] = ffn_rows[2:4, :]
    row_ref[8:12, :] = ffn_rows[8:12, :]
    whole_grad = gm_ref[...] + norm_back(grad, unit, scale, vec_ref[0:1, :])
    gn_ref[...] = whole_grad
    row_ref[12:13, :] = column_sum(whole_grad)
    row_ref[13:14, :] = column_sum(whole_grad * centred)
    row_ref[14:16, :] = jnp.zeros((2, features), f32)


def adam_rule(master, moment, square, gradient, step_value, step_rate, weight_decay):
    moment_new = beta_one * moment + (1.0 - beta_one) * gradient
    square_new = beta_two * square + (1.0 - beta_two) * gradient * gradient
    fix_first = 1.0 - jnp.power(beta_one, step_value)
    fix_second = 1.0 - jnp.power(beta_two, step_value)
    planned = step_rate * jnp.minimum(1.0, step_value / warmup_length)
    direction = moment_new / fix_first / (jnp.sqrt(square_new / fix_second) + adam_epsilon)
    weight_new = master - planned * (direction + weight_decay * master)
    return (weight_new, moment_new, square_new, weight_new.astype(bf16))


def per_device(
    raw_input,
    cotangent,
    segment_ids,
    step_count,
    inlet_copy,
    inlet_master,
    inlet_moment,
    inlet_square,
    outlet_copy,
    outlet_master,
    outlet_moment,
    outlet_square,
    expand_copy,
    expand_master,
    expand_moment,
    expand_square,
    shrink_copy,
    shrink_master,
    shrink_moment,
    shrink_square,
    vector_copy,
    vector_master,
    vector_moment,
    vector_square,
):
    sequences, block_length, features = raw_input.shape
    assert sequences == 1
    width = block_length
    group_size = lax.axis_size("blk")
    group_index = lax.axis_index("blk")
    owners = lax.axis_size("dp")
    owner = lax.axis_index("dp")
    half = owners // 2
    total_tokens = owners * group_size * block_length
    reach = group_size // 2
    slots = 2 * reach + 1
    inner = expand_copy.shape[1]
    chunk = inner // half
    vectors = vector_copy.astype(f32)
    raw = raw_input.reshape(width, features)
    cot = cotangent.reshape(width, features)
    own_ids = segment_ids
    count = owners.bit_length() - 1
    scalar = pl.BlockSpec(memory_space=pltpu.SMEM)
    vmem = pltpu.VMEM

    def reversed_bits(value):
        return int(format(value, f"0{count - 1}b")[::-1], 2) if count > 1 else 0

    straight = [reversed_bits(p) for p in range(half)]
    other_way = list(range(half))
    relative = jnp.array(
        [2 * v for v in straight]
        + [2 * v for v in straight]
        + [2 * v + 1 for v in straight]
        + [2 * v for v in other_way]
        + [2 * v + 1 for v in other_way],
        jnp.int32,
    ) ^ owner
    inside = [group_index >= d for d in range(1, reach + 1)]
    inside += [group_index + d < group_size for d in range(1, reach + 1)]
    table = jnp.concatenate(
        [
            relative[:half] // 2,
            relative[half:],
            jnp.array(straight, jnp.int32),
            jnp.stack([flag for pair in zip(inside[:reach], inside[reach:]) for flag in pair]).astype(jnp.int32),
        ]
    )
    lows = [(group_index // bit) % 2 == 0 for bit in bits_of("blk")]
    column_count = vector_master.shape[1]
    column_start = owner * column_count
    step_value = step_count[0].astype(f32)

    tokens, row = (width, features), (1, features)
    wkv = 3 * features
    lanes = GROUP * HEAD_WIDTH
    steps = features // lanes

    (totals,) = call(
        totals_kernel, "totals", jnp.zeros((1,), jnp.int32), [raw], [struct((2, features), f32)], mib=2
    )
    rounds = SmallSum(totals)
    rounds.send()
    tied = together(*rounds.arrived, table, column_start, vectors, *lows)
    ways = len(rounds.arrived)
    rounds.arrived = list(tied[:ways])
    table, column_start, vectors = tied[ways : ways + 3]
    lows = list(tied[ways + 3 :])
    rounds.take()
    while rounds.left():
        rounds.send()
        rounds.take()
    totals = rounds.block
    packed = width + 16
    x, mean_row, inverse_row = call(
        functools.partial(enter_kernel, total_tokens),
        "enter",
        table,
        [raw, totals, vectors, own_ids],
        [struct((packed, features), bf16), struct(row, f32), struct(row, f32)],
        mib=6,
    )

    xs = [None] * slots
    xs[reach] = x
    ahead, behind = moved(x, "blk", 1), moved(x, "blk", -1)
    queries, pairs, columns = call(
        project_own_kernel,
        "project_own",
        table,
        [x, inlet_copy, vectors],
        [
            struct(tokens, bf16),
            struct((slots, width, 2 * features), bf16),
            struct((slots, width, 128), f32),
        ],
        mib=6,
    )
    ahead, behind, queries = together(ahead, behind, queries)
    for d in range(1, reach + 1):
        if d > 1:
            ahead, behind = moved(ahead, "blk", 1), moved(behind, "blk", -1)
            ahead, behind, pairs = together(ahead, behind, pairs)
        xs[reach - d], xs[reach + d] = ahead, behind
        pairs, columns = call(
            functools.partial(project_pair_kernel, d, 6 * half + 2 * (d - 1)),
            "project_pair",
            table,
            [ahead, behind, x, inlet_copy, vectors, pairs, columns],
            [struct(pairs.shape, bf16), struct(columns.shape, f32)],
            mib=6,
        )

    attended, lse, bounds = call(
        functools.partial(attend_kernel, reach),
        "attend",
        table,
        [queries, pairs, own_ids, columns],
        [struct(tokens, bf16), struct((steps, GROUP, width), f32), struct((2,), jnp.int32)],
        [
            vmem((80 * GROUP, width), f32),
            vmem((8, width), f32),
            vmem((GROUP, 128, width), bf16),
            vmem((GROUP, width, width), f32),
        ],
        mib=6,
    )

    owned_wide, owned = inner // owners, features // owners
    kept_shrink = struct((2, half, owned_wide // 2, features), bf16)
    kept_expand = struct((features // 2, inner + features), bf16)
    layer_output, grad_middle, grad_attended, shrink_keep, shrink_send, expand_keep, expand_send, ffn_rows = call(
        functools.partial(ffn_kernel, half),
        "ffn",
        table,
        [attended, outlet_copy, raw, mean_row, inverse_row, vectors, cot, expand_copy, shrink_copy],
        [
            struct(tokens, bf16),
            struct(tokens, f32),
            struct(tokens, bf16),
            kept_shrink,
            kept_shrink,
            kept_expand,
            kept_expand,
            struct((12, features), f32),
        ],
        [
            vmem(tokens, f32),
            vmem(tokens, f32),
            vmem(tokens, bf16),
            vmem((features, width), bf16),
            vmem((features, width), bf16),
            vmem((features, width), f32),
            vmem((chunk, features), bf16),
            vmem(tokens, f32),
        ],
        mib=14,
    )
    bits = bits_of("dp")
    orders = (bits[1:], bits[:0:-1])

    def scatters(keep, arrived, rows):
        shape = (2,) + (2,) * (count - 1) + (rows // 2, keep.shape[-1])
        keep, arrived = keep.reshape(shape), arrived.reshape(shape)
        return [Scatter([keep[h], arrived[h]], orders[h]) for h in range(2)]

    token = [grad_attended]

    def after(*values):
        tied = together(*values, *token)[: len(values)]
        token[:] = tied
        return tied

    def launch(pair):
        for one in pair:
            one.prepare()
        token[:] = [one.sent for one in pair]
        for one in pair:
            one.send()

    def advance(pair):
        for one, value in zip(pair, after(*[one.arrived for one in pair])):
            one.arrived = value
            one.take()
        if pair[0].order:
            launch(pair)

    def follow(line, stage):
        (line.arrived,) = after(line.arrived)
        stage(line)
        token[:] = [line.keep]

    def begin(pair):
        line = Line(*pair, lows)
        token[:] = [line.sent]
        line.scatter()
        return line

    def next_round():
        rounds.take(after)
        token[:] = [rounds.block]
        if rounds.left():
            rounds.send()

    shrink_in = flipped(shrink_send, "dp", 1)
    expand_in = flipped(expand_send, "dp", 1)
    spread = struct((slots, width, lanes), bf16)
    back = []
    for g in range(steps):
        (grad_attended,) = after(grad_attended)
        back.append(
            call(
                functools.partial(attend_back_kernel, g),
                "attend_back",
                bounds,
                [queries, pairs, attended, grad_attended, lse, own_ids, columns],
                [struct((width, lanes), bf16), spread, spread, struct((2, lanes), f32)],
                [
                    vmem((lanes, width), f32),
                    vmem((GROUP, 128, width), bf16),
                    vmem((GROUP, 128, width), bf16),
                    vmem((GROUP // 2, 2 * width, 128), bf16),
                    vmem((GROUP // 2, 2 * width, 128), bf16),
                    vmem((GROUP, width, width), f32),
                    vmem((GROUP, width, width), f32),
                    vmem((GROUP // 2, width, 2 * width), bf16),
                    vmem((GROUP // 2, width, 2 * width), bf16),
                    vmem((16, width), f32),
                ],
                mib=8,
            )
        )
        token[:] = [back[-1][0]]
        if g == 0:
            (shrink_in,) = after(shrink_in)
            first = scatters(shrink_keep, shrink_in, owned_wide)
            launch(first)
    query_low, key_low, value_low, attend_rows = zip(*back)
    grads = [*query_low, *key_low, *value_low]
    advance(first)

    grads = after(*grads)
    parts, own_part = call(
        functools.partial(parts_kernel, reach),
        "parts",
        bounds,
        [*grads, inlet_copy],
        [struct((2 * reach, width, features), bf16), struct(tokens, f32)],
        mib=6,
    )
    to_left, to_right = parts[0], parts[2 * reach - 1]
    token[:] = [to_left, to_right]
    from_right, from_left = moved(to_left, "blk", -1), moved(to_right, "blk", 1)

    kept_inlet = struct((features // 2, wkv), bf16)
    grads = after(*grads)
    inlet_keep, inlet_send = call(
        functools.partial(weight_kernel, reach, half, steps),
        "weights",
        table,
        xs + [(scalar, bounds), *grads],
        [kept_inlet, kept_inlet],
        [vmem((features, slots * width), bf16), vmem((features, width), f32)],
        mib=8,
    )
    token[:] = [inlet_keep]
    inlet_in = flipped(inlet_send, "dp", 1)
    while first[0].order:
        advance(first)
    advance(first)
    (expand_in,) = after(expand_in)
    second = scatters(expand_keep, expand_in, owned)
    launch(second)
    for d in range(reach - 1, 0, -1):
        from_right, from_left = after(from_right, from_left)
        to_left = added(parts[reach - d], from_right)
        to_right = added(parts[reach + d - 1], from_left)
        token[:] = [to_left, to_right]
        from_right, from_left = moved(to_left, "blk", -1), moved(to_right, "blk", 1)
    line_one = begin(first)
    from_right, from_left = after(from_right, from_left)
    grad_normed, small = call(
        leave_kernel,
        "leave",
        table,
        [
            raw,
            mean_row,
            inverse_row,
            vectors,
            grad_middle,
            own_part,
            from_left,
            from_right,
            ffn_rows,
            *attend_rows,
        ],
        [struct(tokens, f32), struct((16, features), f32)],
        mib=8,
    )
    token[:] = [small]
    rounds = SmallSum(small, paired=False)
    rounds.send()
    advance(second)
    (inlet_in,) = after(inlet_in)
    third = scatters(inlet_keep, inlet_in, owned)
    launch(third)
    next_round()
    follow(line_one, Line.exchange)
    while second[0].order:
        advance(second)
    advance(second)
    line_two = begin(second)
    next_round()
    advance(third)
    follow(line_two, Line.exchange)
    follow(line_one, Line.gather)
    next_round()
    while third[0].order:
        advance(third)
    advance(third)
    line_three = begin(third)
    while rounds.left():
        next_round()
    follow(line_three, Line.exchange)
    (line_one.arrived,) = after(line_one.arrived)
    shrink_share = line_one.result()
    token[:] = [shrink_share]
    follow(line_two, Line.gather)
    next_round()
    small = rounds.block
    follow(line_three, Line.gather)
    (line_two.arrived,) = after(line_two.arrived)
    expand_share = line_two.result()
    token[:] = [expand_share]
    inlet_share = line_three.result()

    band_mean = totals[0] / total_tokens
    band_variance = totals[1] / total_tokens - band_mean * band_mean
    inverse = lax.rsqrt(band_variance + stat_epsilon)
    back_totals = small[12:14]
    grad_variance = -0.5 * back_totals[1] * inverse * inverse * inverse
    grad_centre = -inverse * back_totals[0] - 2.0 * band_mean * grad_variance
    input_gradient = (
        grad_normed * inverse
        + grad_centre / total_tokens
        + 2.0 * grad_variance * raw / total_tokens
    ).reshape(sequences, block_length, features)
    vector_share = lax.dynamic_slice_in_dim(small[:12], column_start, column_count, 1)

    updates = []
    for master, moment, square, share in (
        (inlet_master, inlet_moment, inlet_square, inlet_share),
        (outlet_master, outlet_moment, outlet_square, expand_share[:, inner:]),
        (expand_master, expand_moment, expand_square, expand_share[:, :inner]),
        (shrink_master, shrink_moment, shrink_square, shrink_share),
    ):
        updates.extend(
            adam_rule(
                master, moment, square, share.astype(f32), step_value, rate_matrix, decay_matrix
            )
        )
    updates.extend(
        adam_rule(
            vector_master, vector_moment, vector_square, vector_share, step_value, rate_vector, 0.0
        )
    )
    layer_output = layer_output.reshape(sequences, block_length, features)
    return (layer_output, input_gradient, band_mean, band_variance, *updates)


def solution(mesh):
    tokens = P("dp", "blk", None)
    rows = P("dp", None)
    columns = P(None, "dp")
    matrix = (P(), rows, rows, rows)
    return jax.shard_map(
        per_device,
        mesh=mesh,
        in_specs=(tokens, tokens, P("dp", "blk"), P())
        + matrix * 4
        + (P(), columns, columns, columns),
        out_specs=(tokens, tokens, P(), P()) + (rows,) * 16 + (columns,) * 4,
        check_vma=False,
    )
```

```python
import functools

import jax
import jax.numpy as jnp
from jax import lax
from jax.experimental import pallas as pl
from jax.experimental.pallas import tpu as pltpu
from jax.sharding import PartitionSpec as P

HEADS = 12
HEAD_WIDTH = 64
GROUP = 4

ln_epsilon = 1e-05
stat_epsilon = 1e-06
beta_one = 0.5
beta_two = 0.6
rate_matrix = 0.04
rate_vector = 0.8
warmup_length = 20.0
decay_matrix = 0.05
adam_epsilon = 1e-08
score_scale = 0.125
masked_score = -1e30

f32 = jnp.float32
bf16 = jnp.bfloat16


def nn(a, b):
    return lax.dot_general(a, b, (((1,), (0,)), ((), ())), preferred_element_type=f32)


def nt(a, b):
    return lax.dot_general(a, b, (((1,), (1,)), ((), ())), preferred_element_type=f32)


def tn(a, b):
    return lax.dot_general(a, b, (((0,), (0,)), ((), ())), preferred_element_type=f32)


def flipped(block, axis, bit):
    size = lax.axis_size(axis)
    return lax.ppermute(block, axis, [(i, i ^ bit) for i in range(size)])


def moved(block, axis, distance):
    size = lax.axis_size(axis)
    route = [(i, i + distance) for i in range(size) if 0 <= i + distance < size]
    return lax.ppermute(block, axis, route)


def bits_of(axis):
    size = lax.axis_size(axis)
    return [1 << i for i in range(size.bit_length() - 1)]


class SmallSum:
    def __init__(self, block, paired=True):
        self.block, self.rounds = block, []
        if not paired:
            self.rounds = [(axis, [bit]) for axis in ("blk", "dp") for bit in bits_of(axis)]
            return
        for axis in ("dp", "blk"):
            bits = bits_of(axis)
            odd = len(bits) % 2
            parts = [bits[:odd]] * odd + [bits[i : i + 2] for i in range(odd, len(bits), 2)]
            self.rounds += [(axis, part) for part in parts]

    def left(self):
        return len(self.rounds)

    def send(self):
        axis, part = self.rounds.pop(0)
        ways = part if len(part) == 1 else [part[0], part[1], part[0] | part[1]]
        self.arrived = [flipped(self.block, axis, way) for way in ways]

    def take(self, tie=lambda *values: values):
        others = tie(*self.arrived)
        if len(others) == 1:
            self.block = self.block + others[0]
        else:
            self.block = (self.block + others[0]) + (others[1] + others[2])


def added(kept, arrived):
    return (kept.astype(f32) + arrived.astype(f32)).astype(bf16)


def summed(addends):
    total = addends[0].astype(f32)
    for addend in addends[1:]:
        total = total + addend.astype(f32)
    return total.astype(bf16)


class Scatter:
    def __init__(self, addends, order):
        self.addends, self.order = list(addends), list(order)

    def prepare(self):
        self.sent = summed([addend[1] for addend in self.addends])

    def send(self):
        self.arrived = flipped(self.sent, "dp", self.order.pop(0))

    def take(self):
        self.addends = [addend[0] for addend in self.addends] + [self.arrived]


class Line:
    def __init__(self, first, second, lows):
        self.bits, self.lows = bits_of("blk"), lows
        first, second = summed(first.addends), summed(second.addends)
        self.keep = jnp.where(lows[0], first, second)
        self.sent = jnp.where(lows[0], second, first)

    def scatter(self):
        self.arrived = flipped(self.sent, "blk", 1)

    def exchange(self):
        share = added(self.keep, self.arrived)
        for bit, low in zip(self.bits[1:-1], self.lows[1:]):
            middle = share.shape[0] // 2
            keep = jnp.where(low, share[:middle], share[middle:])
            sent = jnp.where(low, share[middle:], share[:middle])
            share = added(keep, flipped(sent, "blk", bit))
        self.keep = share
        self.arrived = flipped(share, "blk", self.bits[-1])

    def joined(self, low):
        mine, other = self.keep, self.arrived
        return jnp.concatenate(
            [jnp.where(low, mine, other), jnp.where(low, other, mine)], axis=0
        )

    def gather(self):
        share = added(self.keep, self.arrived)
        for bit, low in reversed(list(zip(self.bits[1:-1], self.lows[1:]))):
            self.keep, self.arrived = share, flipped(share, "blk", bit)
            share = self.joined(low)
        self.keep = share
        self.arrived = flipped(share, "blk", 1)

    def result(self):
        return self.joined(self.lows[0])


def together(*values):
    return lax.optimization_barrier(values)


def whole(shape):
    return pl.BlockSpec(shape, lambda *a: (0,) * len(shape))


def call(kernel, name, table, operands, outs, scratch=(), mib=8):
    scalar = pl.BlockSpec(memory_space=pltpu.SMEM)
    return pl.pallas_call(
        kernel,
        grid_spec=pltpu.PrefetchScalarGridSpec(
            num_scalar_prefetch=1,
            grid=(1,),
            in_specs=[
                spec if isinstance(spec, pl.BlockSpec) else whole(spec.shape)
                for spec in (o[0] if isinstance(o, tuple) else o for o in operands)
            ],
            out_specs=[scalar if o.shape == (2,) else whole(o.shape) for o in outs],
            scratch_shapes=list(scratch),
        ),
        out_shape=outs,
        cost_estimate=pl.CostEstimate(flops=1 << 20, bytes_accessed=1 << 16, transcendentals=0),
        compiler_params=pltpu.CompilerParams(vmem_limit_bytes=mib << 20),
        name=name,
    )(table, *[o[1] if isinstance(o, tuple) else o for o in operands])


def struct(shape, dtype):
    return jax.ShapeDtypeStruct(shape, dtype)


def unit_rows(rows):
    centred = rows - jnp.mean(rows, axis=-1, keepdims=True)
    scale = lax.rsqrt(jnp.mean(centred * centred, axis=-1, keepdims=True) + ln_epsilon)
    return centred * scale, scale


def norm_back(grad, unit, scale, gain):
    inner = grad * gain
    return scale * (
        inner
        - jnp.mean(inner, axis=-1, keepdims=True)
        - unit * jnp.mean(inner * unit, axis=-1, keepdims=True)
    )


def column_sum(rows):
    return jnp.sum(rows, axis=0, keepdims=True)


def totals_kernel(table, raw_ref, out_ref):
    raw = raw_ref[...]
    out_ref[0:1, :] = column_sum(raw)
    out_ref[1:2, :] = column_sum(raw * raw)


def enter_kernel(total_tokens, table, raw_ref, sum_ref, vec_ref, id_ref, x_ref, mean_ref, std_ref):
    width = raw_ref.shape[0]
    mean = sum_ref[0:1, :] / total_tokens
    variance = sum_ref[1:2, :] / total_tokens - mean * mean
    inverse = lax.rsqrt(variance + stat_epsilon)
    mean_ref[...] = mean
    std_ref[...] = inverse
    unit, _ = unit_rows((raw_ref[...] - mean) * inverse)
    x_ref[0:width, :] = (unit * vec_ref[0:1, :] + vec_ref[1:2, :]).astype(bf16)
    x_ref[width:, :] = jnp.zeros((x_ref.shape[0] - width, x_ref.shape[1]), bf16)
    ids = jnp.broadcast_to(id_ref[...], (16, width)).astype(f32).astype(bf16)
    x_ref[width:, 0:width] = ids


def id_columns(x_ref, width):
    rows = jnp.broadcast_to(x_ref[width : width + 8, 0:width].astype(f32)[0:1], (128, width))
    return rows.T


def project_own_kernel(table, x_ref, w_ref, vec_ref, q_ref, kv_ref, id_ref):
    width = q_ref.shape[0]
    features = q_ref.shape[1]
    slot = kv_ref.shape[0] // 2
    x = x_ref[0:width, :]
    q_ref[...] = ((nn(x, w_ref[:, :features]) + vec_ref[4:5, :]) * score_scale).astype(bf16)
    kv_ref[slot, :, :features] = nn(x, w_ref[:, features : 2 * features]).astype(bf16)
    kv_ref[slot, :, features:] = (nn(x, w_ref[:, 2 * features :]) + vec_ref[5:6, :]).astype(bf16)
    id_ref[slot] = id_columns(x_ref, width)


def project_pair_kernel(d, inside_at, table, xa_ref, xb_ref, x_ref, w_ref, vec_ref, kv_in, id_in, kv_ref, id_ref):
    width = kv_ref.shape[1]
    features = kv_ref.shape[2] // 2
    reach = kv_ref.shape[0] // 2
    done = slice(reach - d + 1, reach + d)
    kv_ref[done] = kv_in[done]
    id_ref[done] = id_in[done]
    own = x_ref[width : width + 8, 0:width].astype(f32)[0:1]
    low, high = jnp.min(own), jnp.max(own)
    for slot, inside, ref in ((reach - d, 0, xa_ref), (reach + d, 1, xb_ref)):
        ids = ref[width : width + 8, 0:width].astype(f32)[0:1]
        near = (table[inside_at + inside] > 0) & (jnp.max(ids) >= low) & (jnp.min(ids) <= high)
        id_ref[slot] = jnp.full((width, 128), -1.0, f32)

        @pl.when(near)
        def _(ref=ref, slot=slot):
            x = ref[0:width, :]
            kv_ref[slot, :, :features] = nn(x, w_ref[:, features : 2 * features]).astype(bf16)
            kv_ref[slot, :, features:] = (
                nn(x, w_ref[:, 2 * features :]) + vec_ref[5:6, :]
            ).astype(bf16)
            id_ref[slot] = id_columns(ref, width)


def lane_half(rows, which):
    lanes = lax.broadcasted_iota(jnp.int32, (rows, 128), 1)
    return (lanes >= 64) if which else (lanes < 64)


def mask_rows(own_row, width):
    ids = lax.broadcasted_iota(jnp.int32, (64, width), 0).astype(f32)
    return jnp.where(ids == own_row, 0.0, masked_score).astype(bf16)


def key_marks(column, width):
    lane_ids = (lax.broadcasted_iota(jnp.int32, (width, 128), 1) % 64).astype(f32)
    return (column == lane_ids).astype(f32).astype(bf16)


def lane_group(g):
    return pl.ds(pl.multiple_of(g * GROUP * HEAD_WIDTH, 128), GROUP * HEAD_WIDTH)


def attend_kernel(reach, table, q_ref, kv_ref, qid_ref, kid_ref, o_ref, lse_ref, bound_ref, acc, top, qm, sc):
    width, features = q_ref.shape
    slots = kv_ref.shape[0]
    steps = features // (GROUP * HEAD_WIDTH)
    low = kid_ref[reach, 0:1, :]
    high = kid_ref[reach, width - 1 : width, :]
    start = jnp.full_like(low, float(reach))
    end = jnp.full_like(low, float(reach))
    for s in range(slots):
        active = (kid_ref[s, width - 1 : width, :] >= low) & (kid_ref[s, 0:1, :] <= high)
        start = jnp.where(active, jnp.minimum(start, float(s)), start)
        end = jnp.where(active, jnp.maximum(end, float(s)), end)
    bound_ref[0] = jnp.min(start).astype(jnp.int32)
    bound_ref[1] = jnp.max(end).astype(jnp.int32) + 1
    barred = mask_rows(qid_ref[...].astype(f32), width)
    upper = lane_half(width, 1)
    one_rows = (lax.broadcasted_iota(jnp.int32, (16, width), 0) == 0).astype(f32).astype(bf16)

    def group(g, carry):
        lanes_g = lane_group(g)
        lanes_v = pl.ds(pl.multiple_of(features + g * GROUP * HEAD_WIDTH, 128), GROUP * HEAD_WIDTH)
        top[...] = jnp.full_like(top, masked_score)
        acc[...] = jnp.zeros_like(acc)
        q_t = q_ref[:, lanes_g].T
        for h in range(GROUP):
            head = q_t[64 * h : 64 * h + 64, :]
            qm[h, 0:64, :] = barred if h % 2 else head
            qm[h, 64:128, :] = head if h % 2 else barred

        def step(s, carry):
            keys = kv_ref[s, :, lanes_g]
            values_t = kv_ref[s, :, lanes_v].T
            marks = key_marks(kid_ref[s], width)
            for h in range(GROUP):
                lanes = slice(128 * (h // 2), 128 * (h // 2) + 128)
                pair = keys[:, lanes]
                marked = jnp.where(upper, pair, marks) if h % 2 else jnp.where(upper, marks, pair)
                sc[h] = nn(marked, qm[h])
            for h in range(GROUP):
                score = sc[h]
                old = top[h : h + 1, :]
                new = jnp.maximum(old, jnp.max(score, axis=0, keepdims=True))
                fade = jnp.exp(old - new)
                weight = jnp.exp(score - new).astype(bf16)
                top[h : h + 1, :] = new
                rows = slice(80 * h, 80 * h + 80)
                left = jnp.concatenate([values_t[64 * h : 64 * h + 64, :], one_rows], axis=0)
                acc[rows, :] = acc[rows, :] * fade + nn(left, weight)
            return carry

        lax.fori_loop(bound_ref[0], bound_ref[1], step, 0)
        outs, lses = [], []
        for h in range(GROUP):
            total = acc[80 * h + 64 : 80 * h + 65, :]
            outs.append(acc[80 * h : 80 * h + 64, :] / total)
            lses.append(top[h : h + 1, :] + jnp.log(total))
        o_ref[:, lanes_g] = jnp.concatenate(outs, axis=0).T.astype(bf16)
        lse_ref[g] = jnp.concatenate(lses, axis=0)
        return carry

    lax.fori_loop(0, steps, group, 0)


def spread_rows(table, plain, target, lanes, half):
    part = plain.shape[0] // (4 * half)
    for side in range(2):
        for h in range(2):
            for p in range(half):
                owner = table[half * (1 + 2 * h + side) + p]
                place = pl.multiple_of((2 * owner + h) * part, 8)
                to = ((side * 2 + h) * half + p) * part
                target[to : to + part, lanes] = plain[pl.ds(place, part), :].astype(bf16)


def ffn_kernel(
    half,
    table,
    o_ref,
    wo_ref,
    raw_ref,
    mean_ref,
    std_ref,
    vec_ref,
    cot_ref,
    w1_ref,
    w2_ref,
    out_ref,
    gm_ref,
    ga_ref,
    sk_ref,
    ss_ref,
    ek_ref,
    es_ref,
    row_ref,
    middle_s,
    gsec,
    s2,
    s2t,
    ot,
    plain,
    rows_s,
    acc,
):
    features = gm_ref.shape[1]
    inner = w1_ref.shape[1]
    chunk = inner // half
    wide = chunk // 2
    normed = (raw_ref[...] - mean_ref[...]) * std_ref[...]
    middle = normed + nn(o_ref[...], wo_ref[...]) + vec_ref[6:7, :]
    middle_s[...] = middle
    unit, _ = unit_rows(middle)
    second = unit * vec_ref[2:3, :] + vec_ref[3:4, :]
    s2[...] = second.astype(bf16)
    plain[...] = second.T
    spread_rows(table, plain, s2t, slice(None), half)
    plain[...] = o_ref[...].T.astype(f32)
    spread_rows(table, plain, ot, slice(None), half)
    acc[...] = jnp.zeros_like(acc)
    gsec[...] = jnp.zeros_like(gsec)
    own = table[half] % 2

    def step(i, carry):
        place = table[i] * chunk
        lanes = pl.ds(pl.multiple_of(place, 128), chunk)
        row = pl.ds(8 + place // features, 1)
        row_lanes = pl.ds(pl.multiple_of(place % features, 128), chunk)
        w1 = w1_ref[:, lanes]
        w2 = w2_ref[lanes, :]
        pre = nn(s2[...], w1) + vec_ref[row, row_lanes]
        back = nt(cot_ref[...], w2)
        area = 0.5 * (1.0 + lax.erf(pre * (0.5**0.5)))
        bell = jnp.exp(-0.5 * pre * pre) * (1.0 / (2.0 * jnp.pi) ** 0.5)
        hidden = (pre * area).astype(bf16)
        grad = ((area + pre * bell) * back).astype(bf16)
        acc[...] += nn(hidden, w2)
        gsec[...] += nt(grad, w1)
        row_ref[row, row_lanes] = column_sum(grad.astype(f32))
        rows_s[...] = nn(hidden.T, cot_ref[...]).astype(bf16)
        for side, ref in ((0, sk_ref), (1, ss_ref)):
            first = jnp.where(own == side, 0, wide)
            for h, at in ((0, i), (1, table[5 * half + i])):
                start = pl.multiple_of(first + h * (wide // 2), 16)
                ref[h, at] = rows_s[pl.ds(start, wide // 2), :]
        ek_ref[:, lanes] = nn(s2t[: features // 2, :], grad).astype(bf16)
        es_ref[:, lanes] = nn(s2t[features // 2 :, :], grad).astype(bf16)
        return carry

    lax.fori_loop(0, half, step, 0)
    out_ref[...] = (middle_s[...] + acc[...] + vec_ref[7:8, :]).astype(bf16)
    unit, scale = unit_rows(middle_s[...])
    grad = gsec[...]
    cot = cot_ref[...].astype(f32)
    row_ref[0:1, :] = column_sum(grad * unit)
    row_ref[1:2, :] = column_sum(grad)
    grad_middle = cot + norm_back(grad, unit, scale, vec_ref[2:3, :])
    gm_ref[...] = grad_middle
    branch = grad_middle.astype(bf16)
    row_ref[2:3, :] = column_sum(branch.astype(f32))
    row_ref[3:4, :] = column_sum(cot)
    ga_ref[...] = nt(branch, wo_ref[...]).astype(bf16)
    ek_ref[:, inner:] = nn(ot[: features // 2, :], branch).astype(bf16)
    es_ref[:, inner:] = nn(ot[features // 2 :, :], branch).astype(bf16)


def attend_back_kernel(
    g,
    bounds,
    q_ref,
    kv_ref,
    o_ref,
    g_ref,
    lse_ref,
    qid_ref,
    kid_ref,
    dq_ref,
    dk_ref,
    dv_ref,
    row_ref,
    acc,
    qm,
    gm,
    q_stack,
    g_stack,
    sc,
    dp,
    p_wide,
    g_wide,
    rows_s,
):
    width, features = q_ref.shape
    slots = kv_ref.shape[0]
    barred = mask_rows(qid_ref[...].astype(f32), width)
    nothing = jnp.zeros((64, width), bf16)
    upper = lane_half(width, 1)

    def blank(s, carry):
        dk_ref[s] = jnp.zeros(dk_ref.shape[1:], dk_ref.dtype)
        dv_ref[s] = jnp.zeros(dv_ref.shape[1:], dv_ref.dtype)
        return carry

    lax.fori_loop(0, bounds[0], blank, 0)
    lax.fori_loop(bounds[1], slots, blank, 0)

    base = g * GROUP * HEAD_WIDTH
    lanes_g = slice(base, base + GROUP * HEAD_WIDTH)
    lanes_v = slice(features + base, features + base + GROUP * HEAD_WIDTH)
    acc[...] = jnp.zeros_like(acc)
    q_all, g_all = q_ref[:, lanes_g], g_ref[:, lanes_g]
    product = (g_all.astype(f32) * o_ref[:, lanes_g].astype(f32)).T
    q_t, g_t = q_all.T, g_all.T
    for h in range(GROUP):
        lanes = slice(128 * (h // 2), 128 * (h // 2) + 128)
        rows = slice(64 * h, 64 * h + 64)
        odd = h % 2
        qm[h, 0:64, :] = barred if odd else q_t[rows, :]
        qm[h, 64:128, :] = q_t[rows, :] if odd else barred
        gm[h, 0:64, :] = nothing if odd else g_t[rows, :]
        gm[h, 64:128, :] = g_t[rows, :] if odd else nothing
        half = lane_half(width, odd)
        place = slice(width * odd, width * odd + width)
        pair = q_all[:, lanes]
        q_stack[h // 2, place, :] = jnp.where(half, pair, jnp.zeros_like(pair))
        pair = g_all[:, lanes]
        g_stack[h // 2, place, :] = jnp.where(half, pair, jnp.zeros_like(pair))
        rows_s[h : h + 1, :] = column_sum(product[rows, :])
    rows_s[8:9, :] = jnp.zeros((1, GROUP * HEAD_WIDTH), f32)

    def step(s, carry):
        keys = kv_ref[s, :, lanes_g]
        values = kv_ref[s, :, lanes_v]
        keys_t = keys.T
        marks = key_marks(kid_ref[s], width)
        for h in range(GROUP):
            lanes = slice(128 * (h // 2), 128 * (h // 2) + 128)
            pair = keys[:, lanes]
            marked = jnp.where(upper, pair, marks) if h % 2 else jnp.where(upper, marks, pair)
            sc[h] = nn(marked, qm[h])
            dp[h] = nn(values[:, lanes], gm[h])
        for h in range(GROUP):
            place = slice(width * (h % 2), width * (h % 2) + width)
            prob = jnp.exp(sc[h] - lse_ref[g, h : h + 1, :])
            p_wide[h // 2, :, place] = prob.astype(bf16)
            g_wide[h // 2, :, place] = (prob * (dp[h] - rows_s[h : h + 1, :])).astype(bf16)
        for h in range(GROUP):
            place = slice(width * (h % 2), width * (h % 2) + width)
            rows = slice(64 * h, 64 * h + 64)
            acc[rows, :] += nn(keys_t[rows, :], g_wide[h // 2, :, place])
        key_parts, value_parts = [], []
        for j in range(GROUP // 2):
            value_parts.append(nn(p_wide[j], g_stack[j]))
            key_parts.append(nn(g_wide[j], q_stack[j]))
        value_all = jnp.concatenate(value_parts, axis=1)
        dk_ref[s] = jnp.concatenate(key_parts, axis=1).astype(bf16)
        dv_ref[s] = value_all.astype(bf16)
        rows_s[8:9, :] += column_sum(value_all)
        return carry

    lax.fori_loop(bounds[0], bounds[1], step, 0)
    dq = (acc[...].T.astype(bf16).astype(f32) * score_scale).astype(bf16)
    dq_ref[...] = dq
    row_ref[0:1, :] = column_sum(dq.astype(f32))
    row_ref[1:2, :] = rows_s[8:9, :]


def parts_kernel(reach, bounds, *refs):
    groups = (len(refs) - 3) // 3
    dqs, dks, dvs = (refs[k * groups : (k + 1) * groups] for k in range(3))
    w_ref, p_ref, own_ref = refs[3 * groups :]
    features = p_ref.shape[2]
    size = features // groups

    def part(s):
        total = None
        for g in range(groups):
            for ref, base in ((dks[g], features), (dvs[g], 2 * features)):
                now = nt(ref[s], w_ref[:, base + g * size : base + (g + 1) * size])
                total = now if total is None else total + now
        return total

    def one(s, to):
        active = (s >= bounds[0]) & (s < bounds[1])

        @pl.when(active)
        def _():
            p_ref[to] = part(s).astype(bf16)

        @pl.when(jnp.logical_not(active))
        def _():
            p_ref[to] = jnp.zeros(p_ref.shape[1:], p_ref.dtype)

    def some(i, carry):
        one(jnp.where(i < reach, i, i + 1), i)
        return carry

    lax.fori_loop(0, 2 * reach, some, 0)
    total = part(reach)
    for g in range(groups):
        total = total + nt(dqs[g][...], w_ref[:, g * size : (g + 1) * size])
    own_ref[...] = total


def weight_kernel(reach, half, groups, table, *refs):
    slots = 2 * reach + 1
    xs, bounds = refs[:slots], refs[slots]
    refs = refs[slots + 1 :]
    dqs, dks, dvs = (refs[k * groups : (k + 1) * groups] for k in range(3))
    keep_ref, send_ref, xt, plain = refs[3 * groups :]
    width, size = dqs[0].shape
    features = size * groups
    few = min(3, slots)
    small = bounds[1] - bounds[0] <= few
    start = jnp.minimum(bounds[0], slots - few)

    for s in range(slots):

        @pl.when(jnp.logical_not(small) | ((s >= start) & (s < start + few)))
        def _(s=s):
            plain[...] = xs[s][0:width, :].T.astype(f32)
            spread_rows(table, plain, xt, slice(width * s, width * s + width), half)

    def put(tokens, right, base):
        lanes = slice(base, base + size)
        keep_ref[:, lanes] = nn(xt[: features // 2, tokens], right).astype(bf16)
        send_ref[:, lanes] = nn(xt[features // 2 :, tokens], right).astype(bf16)

    for g in range(groups):
        put(slice(width * reach, width * reach + width), dqs[g][...], g * size)

    def over(start, count):
        tokens = pl.ds(pl.multiple_of(start * width, 128), count * width)
        for base, group in ((features, dks), (2 * features, dvs)):
            for g in range(groups):
                rows = group[g][pl.ds(start, count)].reshape(count * width, size)
                put(tokens, rows, base + g * size)

    @pl.when(small)
    def _():
        over(start, few)

    @pl.when(jnp.logical_not(small))
    def _():
        over(0, slots)


def leave_kernel(
    table,
    raw_ref,
    mean_ref,
    std_ref,
    vec_ref,
    gm_ref,
    own_ref,
    left_ref,
    right_ref,
    ffn_rows,
    *refs,
):
    attend_rows, (gn_ref, row_ref) = refs[:-2], refs[-2:]
    features = raw_ref.shape[1]
    centred = raw_ref[...] - mean_ref[...]
    unit, scale = unit_rows(centred * std_ref[...])
    grad = own_ref[...] + left_ref[...].astype(f32) + right_ref[...].astype(f32)
    row_ref[0:1, :] = column_sum(grad * unit)
    row_ref[1:2, :] = column_sum(grad)
    row_ref[2:4, :] = ffn_rows[0:2, :]
    size = features // len(attend_rows)
    for g, ref in enumerate(attend_rows):
        row_ref[4:6, g * size : (g + 1) * size] = ref[...]
    row_ref[6:8, :] = ffn_rows[2:4, :]
    row_ref[8:12, :] = ffn_rows[8:12, :]
    whole_grad = gm_ref[...] + norm_back(grad, unit, scale, vec_ref[0:1, :])
    gn_ref[...] = whole_grad
    row_ref[12:13, :] = column_sum(whole_grad)
    row_ref[13:14, :] = column_sum(whole_grad * centred)
    row_ref[14:16, :] = jnp.zeros((2, features), f32)


def adam_rule(master, moment, square, gradient, step_value, step_rate, weight_decay):
    moment_new = beta_one * moment + (1.0 - beta_one) * gradient
    square_new = beta_two * square + (1.0 - beta_two) * gradient * gradient
    fix_first = 1.0 - jnp.power(beta_one, step_value)
    fix_second = 1.0 - jnp.power(beta_two, step_value)
    planned = step_rate * jnp.minimum(1.0, step_value / warmup_length)
    direction = moment_new / fix_first / (jnp.sqrt(square_new / fix_second) + adam_epsilon)
    weight_new = master - planned * (direction + weight_decay * master)
    return (weight_new, moment_new, square_new, weight_new.astype(bf16))


def per_device(
    raw_input,
    cotangent,
    segment_ids,
    step_count,
    inlet_copy,
    inlet_master,
    inlet_moment,
    inlet_square,
    outlet_copy,
    outlet_master,
    outlet_moment,
    outlet_square,
    expand_copy,
    expand_master,
    expand_moment,
    expand_square,
    shrink_copy,
    shrink_master,
    shrink_moment,
    shrink_square,
    vector_copy,
    vector_master,
    vector_moment,
    vector_square,
):
    sequences, block_length, features = raw_input.shape
    assert sequences == 1
    width = block_length
    group_size = lax.axis_size("blk")
    group_index = lax.axis_index("blk")
    owners = lax.axis_size("dp")
    owner = lax.axis_index("dp")
    half = owners // 2
    total_tokens = owners * group_size * block_length
    reach = group_size // 2
    slots = 2 * reach + 1
    inner = expand_copy.shape[1]
    chunk = inner // half
    vectors = vector_copy.astype(f32)
    raw = raw_input.reshape(width, features)
    cot = cotangent.reshape(width, features)
    own_ids = segment_ids
    count = owners.bit_length() - 1
    scalar = pl.BlockSpec(memory_space=pltpu.SMEM)
    vmem = pltpu.VMEM

    def reversed_bits(value):
        return int(format(value, f"0{count - 1}b")[::-1], 2) if count > 1 else 0

    straight = [reversed_bits(p) for p in range(half)]
    other_way = list(range(half))
    relative = jnp.array(
        [2 * v for v in straight]
        + [2 * v for v in straight]
        + [2 * v + 1 for v in straight]
        + [2 * v for v in other_way]
        + [2 * v + 1 for v in other_way],
        jnp.int32,
    ) ^ owner
    inside = [group_index >= d for d in range(1, reach + 1)]
    inside += [group_index + d < group_size for d in range(1, reach + 1)]
    table = jnp.concatenate(
        [
            relative[:half] // 2,
            relative[half:],
            jnp.array(straight, jnp.int32),
            jnp.stack([flag for pair in zip(inside[:reach], inside[reach:]) for flag in pair]).astype(jnp.int32),
        ]
    )
    lows = [(group_index // bit) % 2 == 0 for bit in bits_of("blk")]
    column_count = vector_master.shape[1]
    column_start = owner * column_count
    step_value = step_count[0].astype(f32)

    tokens, row = (width, features), (1, features)
    wkv = 3 * features
    lanes = GROUP * HEAD_WIDTH
    steps = features // lanes

    (totals,) = call(
        totals_kernel, "totals", jnp.zeros((1,), jnp.int32), [raw], [struct((2, features), f32)], mib=2
    )
    rounds = SmallSum(totals)
    rounds.send()
    rounds.take()
    rounds.send()
    tied = together(*rounds.arrived, table, column_start, vectors, *lows)
    ways = len(rounds.arrived)
    rounds.arrived = list(tied[:ways])
    table, column_start, vectors = tied[ways : ways + 3]
    lows = list(tied[ways + 3 :])
    rounds.take()
    while rounds.left():
        rounds.send()
        rounds.take()
    totals = rounds.block
    packed = width + 16
    x, mean_row, inverse_row = call(
        functools.partial(enter_kernel, total_tokens),
        "enter",
        table,
        [raw, totals, vectors, own_ids],
        [struct((packed, features), bf16), struct(row, f32), struct(row, f32)],
        mib=6,
    )

    xs = [None] * slots
    xs[reach] = x
    ahead, behind = moved(x, "blk", 1), moved(x, "blk", -1)
    queries, pairs, columns = call(
        project_own_kernel,
        "project_own",
        table,
        [x, inlet_copy, vectors],
        [
            struct(tokens, bf16),
            struct((slots, width, 2 * features), bf16),
            struct((slots, width, 128), f32),
        ],
        mib=6,
    )
    ahead, behind, queries = together(ahead, behind, queries)
    for d in range(1, reach + 1):
        if d > 1:
            ahead, behind = moved(ahead, "blk", 1), moved(behind, "blk", -1)
            ahead, behind, pairs = together(ahead, behind, pairs)
        xs[reach - d], xs[reach + d] = ahead, behind
        pairs, columns = call(
            functools.partial(project_pair_kernel, d, 6 * half + 2 * (d - 1)),
            "project_pair",
            table,
            [ahead, behind, x, inlet_copy, vectors, pairs, columns],
            [struct(pairs.shape, bf16), struct(columns.shape, f32)],
            mib=6,
        )

    attended, lse, bounds = call(
        functools.partial(attend_kernel, reach),
        "attend",
        table,
        [queries, pairs, own_ids, columns],
        [struct(tokens, bf16), struct((steps, GROUP, width), f32), struct((2,), jnp.int32)],
        [
            vmem((80 * GROUP, width), f32),
            vmem((8, width), f32),
            vmem((GROUP, 128, width), bf16),
            vmem((GROUP, width, width), f32),
        ],
        mib=6,
    )

    owned_wide, owned = inner // owners, features // owners
    kept_shrink = struct((2, half, owned_wide // 2, features), bf16)
    kept_expand = struct((features // 2, inner + features), bf16)
    layer_output, grad_middle, grad_attended, shrink_keep, shrink_send, expand_keep, expand_send, ffn_rows = call(
        functools.partial(ffn_kernel, half),
        "ffn",
        table,
        [attended, outlet_copy, raw, mean_row, inverse_row, vectors, cot, expand_copy, shrink_copy],
        [
            struct(tokens, bf16),
            struct(tokens, f32),
            struct(tokens, bf16),
            kept_shrink,
            kept_shrink,
            kept_expand,
            kept_expand,
            struct((12, features), f32),
        ],
        [
            vmem(tokens, f32),
            vmem(tokens, f32),
            vmem(tokens, bf16),
            vmem((features, width), bf16),
            vmem((features, width), bf16),
            vmem((features, width), f32),
            vmem((chunk, features), bf16),
            vmem(tokens, f32),
        ],
        mib=14,
    )
    bits = bits_of("dp")
    orders = (bits[1:], bits[:0:-1])

    def scatters(keep, arrived, rows):
        shape = (2,) + (2,) * (count - 1) + (rows // 2, keep.shape[-1])
        keep, arrived = keep.reshape(shape), arrived.reshape(shape)
        return [Scatter([keep[h], arrived[h]], orders[h]) for h in range(2)]

    token = [grad_attended]

    def after(*values):
        tied = together(*values, *token)[: len(values)]
        token[:] = tied
        return tied

    def launch(pair):
        for one in pair:
            one.prepare()
        token[:] = [one.sent for one in pair]
        for one in pair:
            one.send()

    def advance(pair):
        for one, value in zip(pair, after(*[one.arrived for one in pair])):
            one.arrived = value
            one.take()
        if pair[0].order:
            launch(pair)

    def follow(line, stage):
        (line.arrived,) = after(line.arrived)
        stage(line)
        token[:] = [line.keep]

    def begin(pair):
        line = Line(*pair, lows)
        token[:] = [line.sent]
        line.scatter()
        return line

    def next_round():
        rounds.take(after)
        token[:] = [rounds.block]
        if rounds.left():
            rounds.send()

    shrink_in = flipped(shrink_send, "dp", 1)
    expand_in = flipped(expand_send, "dp", 1)
    spread = struct((slots, width, lanes), bf16)
    back = []
    for g in range(steps):
        (grad_attended,) = after(grad_attended)
        back.append(
            call(
                functools.partial(attend_back_kernel, g),
                "attend_back",
                bounds,
                [queries, pairs, attended, grad_attended, lse, own_ids, columns],
                [struct((width, lanes), bf16), spread, spread, struct((2, lanes), f32)],
                [
                    vmem((lanes, width), f32),
                    vmem((GROUP, 128, width), bf16),
                    vmem((GROUP, 128, width), bf16),
                    vmem((GROUP // 2, 2 * width, 128), bf16),
                    vmem((GROUP // 2, 2 * width, 128), bf16),
                    vmem((GROUP, width, width), f32),
                    vmem((GROUP, width, width), f32),
                    vmem((GROUP // 2, width, 2 * width), bf16),
                    vmem((GROUP // 2, width, 2 * width), bf16),
                    vmem((16, width), f32),
                ],
                mib=8,
            )
        )
        token[:] = [back[-1][0]]
        if g == 0:
            (shrink_in,) = after(shrink_in)
            first = scatters(shrink_keep, shrink_in, owned_wide)
            launch(first)
    query_low, key_low, value_low, attend_rows = zip(*back)
    grads = [*query_low, *key_low, *value_low]
    (expand_in,) = after(expand_in)

    grads = after(*grads)
    parts, own_part = call(
        functools.partial(parts_kernel, reach),
        "parts",
        bounds,
        [*grads, inlet_copy],
        [struct((2 * reach, width, features), bf16), struct(tokens, f32)],
        mib=6,
    )
    to_left, to_right = parts[0], parts[2 * reach - 1]
    token[:] = [to_left, to_right]
    from_right, from_left = moved(to_left, "blk", -1), moved(to_right, "blk", 1)
    advance(first)

    kept_inlet = struct((features // 2, wkv), bf16)
    grads = after(*grads)
    inlet_keep, inlet_send = call(
        functools.partial(weight_kernel, reach, half, steps),
        "weights",
        table,
        xs + [(scalar, bounds), *grads],
        [kept_inlet, kept_inlet],
        [vmem((features, slots * width), bf16), vmem((features, width), f32)],
        mib=8,
    )
    token[:] = [inlet_keep]
    inlet_in = flipped(inlet_send, "dp", 1)
    while first[0].order:
        advance(first)
    advance(first)
    (expand_in,) = after(expand_in)
    second = scatters(expand_keep, expand_in, owned)
    launch(second)
    for d in range(reach - 1, 0, -1):
        from_right, from_left = after(from_right, from_left)
        to_left = added(parts[reach - d], from_right)
        to_right = added(parts[reach + d - 1], from_left)
        token[:] = [to_left, to_right]
        from_right, from_left = moved(to_left, "blk", -1), moved(to_right, "blk", 1)
    line_one = begin(first)
    from_right, from_left = after(from_right, from_left)
    grad_normed, small = call(
        leave_kernel,
        "leave",
        table,
        [
            raw,
            mean_row,
            inverse_row,
            vectors,
            grad_middle,
            own_part,
            from_left,
            from_right,
            ffn_rows,
            *attend_rows,
        ],
        [struct(tokens, f32), struct((16, features), f32)],
        mib=8,
    )
    token[:] = [small]
    rounds = SmallSum(small, paired=False)
    rounds.send()
    advance(second)
    (inlet_in,) = after(inlet_in)
    third = scatters(inlet_keep, inlet_in, owned)
    launch(third)
    next_round()
    follow(line_one, Line.exchange)
    while second[0].order:
        advance(second)
    advance(second)
    line_two = begin(second)
    next_round()
    advance(third)
    follow(line_two, Line.exchange)
    follow(line_one, Line.gather)
    next_round()
    while third[0].order:
        advance(third)
    advance(third)
    line_three = begin(third)
    while rounds.left():
        next_round()
    follow(line_three, Line.exchange)
    (line_one.arrived,) = after(line_one.arrived)
    shrink_share = line_one.result()
    token[:] = [shrink_share]
    follow(line_two, Line.gather)
    next_round()
    small = rounds.block
    follow(line_three, Line.gather)
    (line_two.arrived,) = after(line_two.arrived)
    expand_share = line_two.result()
    token[:] = [expand_share]
    inlet_share = line_three.result()

    band_mean = totals[0] / total_tokens
    band_variance = totals[1] / total_tokens - band_mean * band_mean
    inverse = lax.rsqrt(band_variance + stat_epsilon)
    back_totals = small[12:14]
    grad_variance = -0.5 * back_totals[1] * inverse * inverse * inverse
    grad_centre = -inverse * back_totals[0] - 2.0 * band_mean * grad_variance
    input_gradient = (
        grad_normed * inverse
        + grad_centre / total_tokens
        + 2.0 * grad_variance * raw / total_tokens
    ).reshape(sequences, block_length, features)
    vector_share = lax.dynamic_slice(
        small[:12], (0, column_start), (12, column_count), allow_negative_indices=False
    )

    updates = []
    for master, moment, square, share in (
        (inlet_master, inlet_moment, inlet_square, inlet_share),
        (outlet_master, outlet_moment, outlet_square, expand_share[:, inner:]),
        (expand_master, expand_moment, expand_square, expand_share[:, :inner]),
        (shrink_master, shrink_moment, shrink_square, shrink_share),
    ):
        updates.extend(
            adam_rule(
                master, moment, square, share.astype(f32), step_value, rate_matrix, decay_matrix
            )
        )
    updates.extend(
        adam_rule(
            vector_master, vector_moment, vector_square, vector_share, step_value, rate_vector, 0.0
        )
    )
    layer_output = layer_output.reshape(sequences, block_length, features)
    return (layer_output, input_gradient, band_mean, band_variance, *updates)


def solution(mesh):
    tokens = P("dp", "blk", None)
    rows = P("dp", None)
    columns = P(None, "dp")
    matrix = (P(), rows, rows, rows)
    return jax.shard_map(
        per_device,
        mesh=mesh,
        in_specs=(tokens, tokens, P("dp", "blk"), P())
        + matrix * 4
        + (P(), columns, columns, columns),
        out_specs=(tokens, tokens, P(), P()) + (rows,) * 16 + (columns,) * 4,
        check_vma=False,
    )
```

```python
import functools

import jax
import jax.numpy as jnp
from jax import lax
from jax.experimental import pallas as pl
from jax.experimental.pallas import tpu as pltpu
from jax.sharding import PartitionSpec as P

HEADS = 12
HEAD_WIDTH = 64
GROUP = 4

ln_epsilon = 1e-05
stat_epsilon = 1e-06
beta_one = 0.5
beta_two = 0.6
rate_matrix = 0.04
rate_vector = 0.8
warmup_length = 20.0
decay_matrix = 0.05
adam_epsilon = 1e-08
score_scale = 0.125
masked_score = -1e30

f32 = jnp.float32
bf16 = jnp.bfloat16


def nn(a, b):
    return lax.dot_general(a, b, (((1,), (0,)), ((), ())), preferred_element_type=f32)


def nt(a, b):
    return lax.dot_general(a, b, (((1,), (1,)), ((), ())), preferred_element_type=f32)


def tn(a, b):
    return lax.dot_general(a, b, (((0,), (0,)), ((), ())), preferred_element_type=f32)


def flipped(block, axis, bit):
    size = lax.axis_size(axis)
    return lax.ppermute(block, axis, [(i, i ^ bit) for i in range(size)])


def moved(block, axis, distance):
    size = lax.axis_size(axis)
    route = [(i, i + distance) for i in range(size) if 0 <= i + distance < size]
    return lax.ppermute(block, axis, route)


def bits_of(axis):
    size = lax.axis_size(axis)
    return [1 << i for i in range(size.bit_length() - 1)]


class SmallSum:
    def __init__(self, block, paired=True):
        self.block, self.rounds = block, []
        if not paired:
            self.rounds = [(axis, [bit]) for axis in ("blk", "dp") for bit in bits_of(axis)]
            return
        for axis in ("dp", "blk"):
            bits = bits_of(axis)
            odd = len(bits) % 2
            parts = [bits[:odd]] * odd + [bits[i : i + 2] for i in range(odd, len(bits), 2)]
            self.rounds += [(axis, part) for part in parts]

    def left(self):
        return len(self.rounds)

    def send(self):
        axis, part = self.rounds.pop(0)
        ways = part if len(part) == 1 else [part[0], part[1], part[0] | part[1]]
        self.arrived = [flipped(self.block, axis, way) for way in ways]

    def take(self, tie=lambda *values: values):
        others = tie(*self.arrived)
        if len(others) == 1:
            self.block = self.block + others[0]
        else:
            self.block = (self.block + others[0]) + (others[1] + others[2])


def added(kept, arrived):
    return (kept.astype(f32) + arrived.astype(f32)).astype(bf16)


def summed(addends):
    total = addends[0].astype(f32)
    for addend in addends[1:]:
        total = total + addend.astype(f32)
    return total.astype(bf16)


class Scatter:
    def __init__(self, addends, order):
        self.addends, self.order = list(addends), list(order)

    def prepare(self):
        self.sent = summed([addend[1] for addend in self.addends])

    def send(self):
        self.arrived = flipped(self.sent, "dp", self.order.pop(0))

    def take(self):
        self.addends = [addend[0] for addend in self.addends] + [self.arrived]


class Line:
    def __init__(self, first, second, lows):
        self.bits, self.lows = bits_of("blk"), lows
        first, second = summed(first.addends), summed(second.addends)
        self.keep = jnp.where(lows[0], first, second)
        self.sent = jnp.where(lows[0], second, first)

    def scatter(self):
        self.arrived = flipped(self.sent, "blk", 1)

    def exchange(self):
        share = added(self.keep, self.arrived)
        for bit, low in zip(self.bits[1:-1], self.lows[1:]):
            middle = share.shape[0] // 2
            keep = jnp.where(low, share[:middle], share[middle:])
            sent = jnp.where(low, share[middle:], share[:middle])
            share = added(keep, flipped(sent, "blk", bit))
        self.keep = share
        self.arrived = flipped(share, "blk", self.bits[-1])

    def joined(self, low):
        mine, other = self.keep, self.arrived
        return jnp.concatenate(
            [jnp.where(low, mine, other), jnp.where(low, other, mine)], axis=0
        )

    def gather(self):
        share = added(self.keep, self.arrived)
        for bit, low in reversed(list(zip(self.bits[1:-1], self.lows[1:]))):
            self.keep, self.arrived = share, flipped(share, "blk", bit)
            share = self.joined(low)
        self.keep = share
        self.arrived = flipped(share, "blk", 1)

    def result(self):
        return self.joined(self.lows[0])


def together(*values):
    return lax.optimization_barrier(values)


def whole(shape):
    return pl.BlockSpec(shape, lambda *a: (0,) * len(shape))


def call(kernel, name, table, operands, outs, scratch=(), mib=8):
    scalar = pl.BlockSpec(memory_space=pltpu.SMEM)
    return pl.pallas_call(
        kernel,
        grid_spec=pltpu.PrefetchScalarGridSpec(
            num_scalar_prefetch=1,
            grid=(1,),
            in_specs=[
                spec if isinstance(spec, pl.BlockSpec) else whole(spec.shape)
                for spec in (o[0] if isinstance(o, tuple) else o for o in operands)
            ],
            out_specs=[scalar if o.shape == (2,) else whole(o.shape) for o in outs],
            scratch_shapes=list(scratch),
        ),
        out_shape=outs,
        cost_estimate=pl.CostEstimate(flops=1 << 20, bytes_accessed=1 << 16, transcendentals=0),
        compiler_params=pltpu.CompilerParams(vmem_limit_bytes=mib << 20),
        name=name,
    )(table, *[o[1] if isinstance(o, tuple) else o for o in operands])


def struct(shape, dtype):
    return jax.ShapeDtypeStruct(shape, dtype)


def unit_rows(rows):
    centred = rows - jnp.mean(rows, axis=-1, keepdims=True)
    scale = lax.rsqrt(jnp.mean(centred * centred, axis=-1, keepdims=True) + ln_epsilon)
    return centred * scale, scale


def norm_back(grad, unit, scale, gain):
    inner = grad * gain
    return scale * (
        inner
        - jnp.mean(inner, axis=-1, keepdims=True)
        - unit * jnp.mean(inner * unit, axis=-1, keepdims=True)
    )


def column_sum(rows):
    return jnp.sum(rows, axis=0, keepdims=True)


def totals_kernel(table, raw_ref, out_ref):
    raw = raw_ref[...]
    out_ref[0:1, :] = column_sum(raw)
    out_ref[1:2, :] = column_sum(raw * raw)


def enter_kernel(total_tokens, table, raw_ref, sum_ref, vec_ref, id_ref, x_ref, mean_ref, std_ref):
    width = raw_ref.shape[0]
    mean = sum_ref[0:1, :] / total_tokens
    variance = sum_ref[1:2, :] / total_tokens - mean * mean
    inverse = lax.rsqrt(variance + stat_epsilon)
    mean_ref[...] = mean
    std_ref[...] = inverse
    unit, _ = unit_rows((raw_ref[...] - mean) * inverse)
    x_ref[0:width, :] = (unit * vec_ref[0:1, :] + vec_ref[1:2, :]).astype(bf16)
    x_ref[width:, :] = jnp.zeros((x_ref.shape[0] - width, x_ref.shape[1]), bf16)
    ids = jnp.broadcast_to(id_ref[...], (16, width)).astype(f32).astype(bf16)
    x_ref[width:, 0:width] = ids


def id_columns(ids, width):
    return jnp.broadcast_to(ids, (128, width)).T


def id_row(rows):
    return rows.astype(f32)[0:1]


def project_own_kernel(table, x_ref, w_ref, vec_ref, q_ref, kv_ref, id_ref):
    width = q_ref.shape[0]
    features = q_ref.shape[1]
    slot = kv_ref.shape[0] // 2
    x = x_ref[0:width, :]
    q_ref[...] = ((nn(x, w_ref[:, :features]) + vec_ref[4:5, :]) * score_scale).astype(bf16)
    kv_ref[slot, :, :features] = nn(x, w_ref[:, features : 2 * features]).astype(bf16)
    kv_ref[slot, :, features:] = (nn(x, w_ref[:, 2 * features :]) + vec_ref[5:6, :]).astype(bf16)
    id_ref[slot] = id_columns(id_row(x_ref[width : width + 8, 0:width]), width)


def project_pair_kernel(
    d, inside_at, table, xa_ref, xb_ref, x_ref, w_ref, vec_ref, kv_in, id_in, kv_ref, id_ref, both
):
    width = kv_ref.shape[1]
    features = kv_ref.shape[2] // 2
    reach = kv_ref.shape[0] // 2
    done = slice(reach - d + 1, reach + d)
    kv_ref[done] = kv_in[done]
    id_ref[done] = id_in[done]
    both[0], both[1] = xa_ref[...], xb_ref[...]
    own = id_row(x_ref[width : width + 8, 0:width])
    low, high = jnp.min(own), jnp.max(own)

    def one(i, carry):
        slot = reach - d + 2 * d * i
        ids = id_row(both[i, width : width + 8, 0:width])
        near = (table[inside_at + i] > 0) & (jnp.max(ids) >= low) & (jnp.min(ids) <= high)
        id_ref[slot] = jnp.full((width, 128), -1.0, f32)

        @pl.when(near)
        def _():
            x = both[i, 0:width, :]
            kv_ref[slot, :, :features] = nn(x, w_ref[:, features : 2 * features]).astype(bf16)
            kv_ref[slot, :, features:] = (
                nn(x, w_ref[:, 2 * features :]) + vec_ref[5:6, :]
            ).astype(bf16)
            id_ref[slot] = id_columns(ids, width)

        return carry

    lax.fori_loop(0, 2, one, 0)


def lane_half(rows, which):
    lanes = lax.broadcasted_iota(jnp.int32, (rows, 128), 1)
    return (lanes >= 64) if which else (lanes < 64)


def mask_rows(own_row, width):
    ids = lax.broadcasted_iota(jnp.int32, (64, width), 0).astype(f32)
    return jnp.where(ids == own_row, 0.0, masked_score).astype(bf16)


def key_marks(column, width):
    lane_ids = (lax.broadcasted_iota(jnp.int32, (width, 128), 1) % 64).astype(f32)
    return (column == lane_ids).astype(f32).astype(bf16)


def lane_group(g):
    return pl.ds(pl.multiple_of(g * GROUP * HEAD_WIDTH, 128), GROUP * HEAD_WIDTH)


def attend_kernel(reach, table, q_ref, kv_ref, qid_ref, kid_ref, o_ref, lse_ref, bound_ref, acc, top, qm, sc):
    width, features = q_ref.shape
    slots = kv_ref.shape[0]
    steps = features // (GROUP * HEAD_WIDTH)
    low = kid_ref[reach, 0:1, :]
    high = kid_ref[reach, width - 1 : width, :]
    start = jnp.full_like(low, float(reach))
    end = jnp.full_like(low, float(reach))
    for s in range(slots):
        active = (kid_ref[s, width - 1 : width, :] >= low) & (kid_ref[s, 0:1, :] <= high)
        start = jnp.where(active, jnp.minimum(start, float(s)), start)
        end = jnp.where(active, jnp.maximum(end, float(s)), end)
    bound_ref[0] = jnp.min(start).astype(jnp.int32)
    bound_ref[1] = jnp.max(end).astype(jnp.int32) + 1
    barred = mask_rows(qid_ref[...].astype(f32), width)
    upper = lane_half(width, 1)
    one_rows = (lax.broadcasted_iota(jnp.int32, (16, width), 0) == 0).astype(f32).astype(bf16)

    def group(g, carry):
        lanes_g = lane_group(g)
        lanes_v = pl.ds(pl.multiple_of(features + g * GROUP * HEAD_WIDTH, 128), GROUP * HEAD_WIDTH)
        top[...] = jnp.full_like(top, masked_score)
        acc[...] = jnp.zeros_like(acc)
        q_t = q_ref[:, lanes_g].T
        for h in range(GROUP):
            head = q_t[64 * h : 64 * h + 64, :]
            qm[h, 0:64, :] = barred if h % 2 else head
            qm[h, 64:128, :] = head if h % 2 else barred

        def step(s, carry):
            keys = kv_ref[s, :, lanes_g]
            values_t = kv_ref[s, :, lanes_v].T
            marks = key_marks(kid_ref[s], width)
            for h in range(GROUP):
                lanes = slice(128 * (h // 2), 128 * (h // 2) + 128)
                pair = keys[:, lanes]
                marked = jnp.where(upper, pair, marks) if h % 2 else jnp.where(upper, marks, pair)
                sc[h] = nn(marked, qm[h])
            for h in range(GROUP):
                score = sc[h]
                old = top[h : h + 1, :]
                new = jnp.maximum(old, jnp.max(score, axis=0, keepdims=True))
                fade = jnp.exp(old - new)
                weight = jnp.exp(score - new).astype(bf16)
                top[h : h + 1, :] = new
                rows = slice(80 * h, 80 * h + 80)
                left = jnp.concatenate([values_t[64 * h : 64 * h + 64, :], one_rows], axis=0)
                acc[rows, :] = acc[rows, :] * fade + nn(left, weight)
            return carry

        lax.fori_loop(bound_ref[0], bound_ref[1], step, 0)
        outs, lses = [], []
        for h in range(GROUP):
            total = acc[80 * h + 64 : 80 * h + 65, :]
            outs.append(acc[80 * h : 80 * h + 64, :] / total)
            lses.append(top[h : h + 1, :] + jnp.log(total))
        o_ref[:, lanes_g] = jnp.concatenate(outs, axis=0).T.astype(bf16)
        lse_ref[g] = jnp.concatenate(lses, axis=0)
        return carry

    lax.fori_loop(0, steps, group, 0)


def spread_rows(table, plain, target, lanes, half):
    part = plain.shape[0] // (4 * half)
    for side in range(2):
        for h in range(2):
            for p in range(half):
                owner = table[half * (1 + 2 * h + side) + p]
                place = pl.multiple_of((2 * owner + h) * part, 8)
                to = ((side * 2 + h) * half + p) * part
                target[to : to + part, lanes] = plain[pl.ds(place, part), :].astype(bf16)


def ffn_kernel(
    half,
    table,
    o_ref,
    wo_ref,
    raw_ref,
    mean_ref,
    std_ref,
    vec_ref,
    cot_ref,
    w1_ref,
    w2_ref,
    out_ref,
    gm_ref,
    ga_ref,
    sk_ref,
    ss_ref,
    ek_ref,
    es_ref,
    row_ref,
    middle_s,
    gsec,
    s2,
    s2t,
    ot,
    plain,
    rows_s,
    acc,
):
    features = gm_ref.shape[1]
    inner = w1_ref.shape[1]
    chunk = inner // half
    wide = chunk // 2
    normed = (raw_ref[...] - mean_ref[...]) * std_ref[...]
    middle = normed + nn(o_ref[...], wo_ref[...]) + vec_ref[6:7, :]
    middle_s[...] = middle
    unit, _ = unit_rows(middle)
    second = unit * vec_ref[2:3, :] + vec_ref[3:4, :]
    s2[...] = second.astype(bf16)
    plain[...] = second.T
    spread_rows(table, plain, s2t, slice(None), half)
    plain[...] = o_ref[...].T.astype(f32)
    spread_rows(table, plain, ot, slice(None), half)
    acc[...] = jnp.zeros_like(acc)
    gsec[...] = jnp.zeros_like(gsec)
    own = table[half] % 2

    def step(i, carry):
        place = table[i] * chunk
        lanes = pl.ds(pl.multiple_of(place, 128), chunk)
        row = pl.ds(8 + place // features, 1)
        row_lanes = pl.ds(pl.multiple_of(place % features, 128), chunk)
        w1 = w1_ref[:, lanes]
        w2 = w2_ref[lanes, :]
        pre = nn(s2[...], w1) + vec_ref[row, row_lanes]
        back = nt(cot_ref[...], w2)
        area = 0.5 * (1.0 + lax.erf(pre * (0.5**0.5)))
        bell = jnp.exp(-0.5 * pre * pre) * (1.0 / (2.0 * jnp.pi) ** 0.5)
        hidden = (pre * area).astype(bf16)
        grad = ((area + pre * bell) * back).astype(bf16)
        acc[...] += nn(hidden, w2)
        gsec[...] += nt(grad, w1)
        row_ref[row, row_lanes] = column_sum(grad.astype(f32))
        rows_s[...] = nn(hidden.T, cot_ref[...]).astype(bf16)
        for side, ref in ((0, sk_ref), (1, ss_ref)):
            first = jnp.where(own == side, 0, wide)
            for h, at in ((0, i), (1, table[5 * half + i])):
                start = pl.multiple_of(first + h * (wide // 2), 16)
                ref[h, at] = rows_s[pl.ds(start, wide // 2), :]
        ek_ref[:, lanes] = nn(s2t[: features // 2, :], grad).astype(bf16)
        es_ref[:, lanes] = nn(s2t[features // 2 :, :], grad).astype(bf16)
        return carry

    lax.fori_loop(0, half, step, 0, unroll=True)
    out_ref[...] = (middle_s[...] + acc[...] + vec_ref[7:8, :]).astype(bf16)
    unit, scale = unit_rows(middle_s[...])
    grad = gsec[...]
    cot = cot_ref[...].astype(f32)
    row_ref[0:1, :] = column_sum(grad * unit)
    row_ref[1:2, :] = column_sum(grad)
    grad_middle = cot + norm_back(grad, unit, scale, vec_ref[2:3, :])
    gm_ref[...] = grad_middle
    branch = grad_middle.astype(bf16)
    row_ref[2:3, :] = column_sum(branch.astype(f32))
    row_ref[3:4, :] = column_sum(cot)
    ga_ref[...] = nt(branch, wo_ref[...]).astype(bf16)
    ek_ref[:, inner:] = nn(ot[: features // 2, :], branch).astype(bf16)
    es_ref[:, inner:] = nn(ot[features // 2 :, :], branch).astype(bf16)


def attend_back_kernel(
    g,
    bounds,
    q_ref,
    kv_ref,
    o_ref,
    g_ref,
    lse_ref,
    qid_ref,
    kid_ref,
    dq_ref,
    dk_ref,
    dv_ref,
    row_ref,
    acc,
    qm,
    gm,
    q_stack,
    g_stack,
    sc,
    dp,
    p_wide,
    g_wide,
    rows_s,
):
    width, features = q_ref.shape
    slots = kv_ref.shape[0]
    barred = mask_rows(qid_ref[...].astype(f32), width)
    nothing = jnp.zeros((64, width), bf16)
    upper = lane_half(width, 1)

    def blank(s, carry):
        dk_ref[s] = jnp.zeros(dk_ref.shape[1:], dk_ref.dtype)
        dv_ref[s] = jnp.zeros(dv_ref.shape[1:], dv_ref.dtype)
        return carry

    lax.fori_loop(0, bounds[0], blank, 0)
    lax.fori_loop(bounds[1], slots, blank, 0)

    base = g * GROUP * HEAD_WIDTH
    lanes_g = slice(base, base + GROUP * HEAD_WIDTH)
    lanes_v = slice(features + base, features + base + GROUP * HEAD_WIDTH)
    acc[...] = jnp.zeros_like(acc)
    q_all, g_all = q_ref[:, lanes_g], g_ref[:, lanes_g]
    product = (g_all.astype(f32) * o_ref[:, lanes_g].astype(f32)).T
    q_t, g_t = q_all.T, g_all.T
    for h in range(GROUP):
        lanes = slice(128 * (h // 2), 128 * (h // 2) + 128)
        rows = slice(64 * h, 64 * h + 64)
        odd = h % 2
        qm[h, 0:64, :] = barred if odd else q_t[rows, :]
        qm[h, 64:128, :] = q_t[rows, :] if odd else barred
        gm[h, 0:64, :] = nothing if odd else g_t[rows, :]
        gm[h, 64:128, :] = g_t[rows, :] if odd else nothing
        half = lane_half(width, odd)
        place = slice(width * odd, width * odd + width)
        pair = q_all[:, lanes]
        q_stack[h // 2, place, :] = jnp.where(half, pair, jnp.zeros_like(pair))
        pair = g_all[:, lanes]
        g_stack[h // 2, place, :] = jnp.where(half, pair, jnp.zeros_like(pair))
        rows_s[h : h + 1, :] = column_sum(product[rows, :])
    rows_s[8:9, :] = jnp.zeros((1, GROUP * HEAD_WIDTH), f32)

    def step(s, carry):
        keys = kv_ref[s, :, lanes_g]
        values = kv_ref[s, :, lanes_v]
        keys_t = keys.T
        marks = key_marks(kid_ref[s], width)
        for h in range(GROUP):
            lanes = slice(128 * (h // 2), 128 * (h // 2) + 128)
            pair = keys[:, lanes]
            marked = jnp.where(upper, pair, marks) if h % 2 else jnp.where(upper, marks, pair)
            sc[h] = nn(marked, qm[h])
            dp[h] = nn(values[:, lanes], gm[h])
        for h in range(GROUP):
            place = slice(width * (h % 2), width * (h % 2) + width)
            prob = jnp.exp(sc[h] - lse_ref[g, h : h + 1, :])
            p_wide[h // 2, :, place] = prob.astype(bf16)
            g_wide[h // 2, :, place] = (prob * (dp[h] - rows_s[h : h + 1, :])).astype(bf16)
        for h in range(GROUP):
            place = slice(width * (h % 2), width * (h % 2) + width)
            rows = slice(64 * h, 64 * h + 64)
            acc[rows, :] += nn(keys_t[rows, :], g_wide[h // 2, :, place])
        key_parts, value_parts = [], []
        for j in range(GROUP // 2):
            value_parts.append(nn(p_wide[j], g_stack[j]))
            key_parts.append(nn(g_wide[j], q_stack[j]))
        value_all = jnp.concatenate(value_parts, axis=1)
        dk_ref[s] = jnp.concatenate(key_parts, axis=1).astype(bf16)
        dv_ref[s] = value_all.astype(bf16)
        rows_s[8:9, :] += column_sum(value_all)
        return carry

    lax.fori_loop(bounds[0], bounds[1], step, 0)
    dq = (acc[...].T.astype(bf16).astype(f32) * score_scale).astype(bf16)
    dq_ref[...] = dq
    row_ref[0:1, :] = column_sum(dq.astype(f32))
    row_ref[1:2, :] = rows_s[8:9, :]


def parts_kernel(reach, bounds, *refs):
    groups = (len(refs) - 3) // 3
    dqs, dks, dvs = (refs[k * groups : (k + 1) * groups] for k in range(3))
    w_ref, p_ref, own_ref = refs[3 * groups :]
    features = p_ref.shape[2]
    size = features // groups

    def part(s):
        total = None
        for g in range(groups):
            for ref, base in ((dks[g], features), (dvs[g], 2 * features)):
                now = nt(ref[s], w_ref[:, base + g * size : base + (g + 1) * size])
                total = now if total is None else total + now
        return total

    def one(s, to):
        active = (s >= bounds[0]) & (s < bounds[1])

        @pl.when(active)
        def _():
            p_ref[to] = part(s).astype(bf16)

        @pl.when(jnp.logical_not(active))
        def _():
            p_ref[to] = jnp.zeros(p_ref.shape[1:], p_ref.dtype)

    def some(i, carry):
        one(jnp.where(i < reach, i, i + 1), i)
        return carry

    lax.fori_loop(0, 2 * reach, some, 0)
    total = part(reach)
    for g in range(groups):
        total = total + nt(dqs[g][...], w_ref[:, g * size : (g + 1) * size])
    own_ref[...] = total


def weight_kernel(reach, half, groups, table, *refs):
    slots = 2 * reach + 1
    xs, bounds = refs[:slots], refs[slots]
    refs = refs[slots + 1 :]
    dqs, dks, dvs = (refs[k * groups : (k + 1) * groups] for k in range(3))
    keep_ref, send_ref, xt, plain = refs[3 * groups :]
    width, size = dqs[0].shape
    features = size * groups
    few = min(3, slots)
    small = bounds[1] - bounds[0] <= few
    start = jnp.minimum(bounds[0], slots - few)

    for s in range(slots):

        @pl.when(jnp.logical_not(small) | ((s >= start) & (s < start + few)))
        def _(s=s):
            plain[...] = xs[s][0:width, :].T.astype(f32)
            spread_rows(table, plain, xt, slice(width * s, width * s + width), half)

    def put(tokens, right, base):
        lanes = slice(base, base + size)
        keep_ref[:, lanes] = nn(xt[: features // 2, tokens], right).astype(bf16)
        send_ref[:, lanes] = nn(xt[features // 2 :, tokens], right).astype(bf16)

    for g in range(groups):
        put(slice(width * reach, width * reach + width), dqs[g][...], g * size)

    def over(start, count):
        tokens = pl.ds(pl.multiple_of(start * width, 128), count * width)
        for base, group in ((features, dks), (2 * features, dvs)):
            for g in range(groups):
                rows = group[g][pl.ds(start, count)].reshape(count * width, size)
                put(tokens, rows, base + g * size)

    @pl.when(small)
    def _():
        over(start, few)

    @pl.when(jnp.logical_not(small))
    def _():
        over(0, slots)


def leave_kernel(
    table,
    raw_ref,
    mean_ref,
    std_ref,
    vec_ref,
    gm_ref,
    own_ref,
    left_ref,
    right_ref,
    ffn_rows,
    *refs,
):
    attend_rows, (gn_ref, row_ref) = refs[:-2], refs[-2:]
    features = raw_ref.shape[1]
    centred = raw_ref[...] - mean_ref[...]
    unit, scale = unit_rows(centred * std_ref[...])
    grad = own_ref[...] + left_ref[...].astype(f32) + right_ref[...].astype(f32)
    row_ref[0:1, :] = column_sum(grad * unit)
    row_ref[1:2, :] = column_sum(grad)
    row_ref[2:4, :] = ffn_rows[0:2, :]
    size = features // len(attend_rows)
    for g, ref in enumerate(attend_rows):
        row_ref[4:6, g * size : (g + 1) * size] = ref[...]
    row_ref[6:8, :] = ffn_rows[2:4, :]
    row_ref[8:12, :] = ffn_rows[8:12, :]
    whole_grad = gm_ref[...] + norm_back(grad, unit, scale, vec_ref[0:1, :])
    gn_ref[...] = whole_grad
    row_ref[12:13, :] = column_sum(whole_grad)
    row_ref[13:14, :] = column_sum(whole_grad * centred)
    row_ref[14:16, :] = jnp.zeros((2, features), f32)


def adam_rule(master, moment, square, gradient, step_value, step_rate, weight_decay):
    moment_new = beta_one * moment + (1.0 - beta_one) * gradient
    square_new = beta_two * square + (1.0 - beta_two) * gradient * gradient
    fix_first = 1.0 - jnp.power(beta_one, step_value)
    fix_second = 1.0 - jnp.power(beta_two, step_value)
    planned = step_rate * jnp.minimum(1.0, step_value / warmup_length)
    direction = moment_new / fix_first / (jnp.sqrt(square_new / fix_second) + adam_epsilon)
    weight_new = master - planned * (direction + weight_decay * master)
    return (weight_new, moment_new, square_new, weight_new.astype(bf16))


def per_device(
    raw_input,
    cotangent,
    segment_ids,
    step_count,
    inlet_copy,
    inlet_master,
    inlet_moment,
    inlet_square,
    outlet_copy,
    outlet_master,
    outlet_moment,
    outlet_square,
    expand_copy,
    expand_master,
    expand_moment,
    expand_square,
    shrink_copy,
    shrink_master,
    shrink_moment,
    shrink_square,
    vector_copy,
    vector_master,
    vector_moment,
    vector_square,
):
    sequences, block_length, features = raw_input.shape
    assert sequences == 1
    width = block_length
    group_size = lax.axis_size("blk")
    group_index = lax.axis_index("blk")
    owners = lax.axis_size("dp")
    owner = lax.axis_index("dp")
    half = owners // 2
    total_tokens = owners * group_size * block_length
    reach = group_size // 2
    slots = 2 * reach + 1
    inner = expand_copy.shape[1]
    chunk = inner // half
    vectors = vector_copy.astype(f32)
    raw = raw_input.reshape(width, features)
    cot = cotangent.reshape(width, features)
    own_ids = segment_ids
    count = owners.bit_length() - 1
    scalar = pl.BlockSpec(memory_space=pltpu.SMEM)
    vmem = pltpu.VMEM

    def reversed_bits(value):
        return int(format(value, f"0{count - 1}b")[::-1], 2) if count > 1 else 0

    straight = [reversed_bits(p) for p in range(half)]
    other_way = list(range(half))
    relative = jnp.array(
        [2 * v for v in straight]
        + [2 * v for v in straight]
        + [2 * v + 1 for v in straight]
        + [2 * v for v in other_way]
        + [2 * v + 1 for v in other_way],
        jnp.int32,
    ) ^ owner
    inside = [group_index >= d for d in range(1, reach + 1)]
    inside += [group_index + d < group_size for d in range(1, reach + 1)]
    table = jnp.concatenate(
        [
            relative[:half] // 2,
            relative[half:],
            jnp.array(straight, jnp.int32),
            jnp.stack([flag for pair in zip(inside[:reach], inside[reach:]) for flag in pair]).astype(jnp.int32),
        ]
    )
    lows = [(group_index // bit) % 2 == 0 for bit in bits_of("blk")]
    column_count = vector_master.shape[1]
    column_start = owner * column_count
    step_value = step_count[0].astype(f32)

    tokens, row = (width, features), (1, features)
    wkv = 3 * features
    lanes = GROUP * HEAD_WIDTH
    steps = features // lanes

    (totals,) = call(
        totals_kernel, "totals", jnp.zeros((1,), jnp.int32), [raw], [struct((2, features), f32)], mib=2
    )
    rounds = SmallSum(totals)
    rounds.send()
    rounds.take()
    rounds.send()
    tied = together(*rounds.arrived, table, column_start, vectors, *lows)
    ways = len(rounds.arrived)
    rounds.arrived = list(tied[:ways])
    table, column_start, vectors = tied[ways : ways + 3]
    lows = list(tied[ways + 3 :])
    rounds.take()
    while rounds.left():
        rounds.send()
        rounds.take()
    totals = rounds.block
    packed = width + 16
    x, mean_row, inverse_row = call(
        functools.partial(enter_kernel, total_tokens),
        "enter",
        table,
        [raw, totals, vectors, own_ids],
        [struct((packed, features), bf16), struct(row, f32), struct(row, f32)],
        mib=6,
    )

    xs = [None] * slots
    xs[reach] = x
    ahead, behind = moved(x, "blk", 1), moved(x, "blk", -1)
    queries, pairs, columns = call(
        project_own_kernel,
        "project_own",
        table,
        [x, inlet_copy, vectors],
        [
            struct(tokens, bf16),
            struct((slots, width, 2 * features), bf16),
            struct((slots, width, 128), f32),
        ],
        mib=6,
    )
    ahead, behind, queries = together(ahead, behind, queries)
    for d in range(1, reach + 1):
        if d > 1:
            ahead, behind = moved(ahead, "blk", 1), moved(behind, "blk", -1)
            ahead, behind, pairs = together(ahead, behind, pairs)
        xs[reach - d], xs[reach + d] = ahead, behind
        pairs, columns = call(
            functools.partial(project_pair_kernel, d, 6 * half + 2 * (d - 1)),
            "project_pair",
            table,
            [ahead, behind, x, inlet_copy, vectors, pairs, columns],
            [struct(pairs.shape, bf16), struct(columns.shape, f32)],
            [vmem((2, packed, features), bf16)],
            mib=6,
        )

    attended, lse, bounds = call(
        functools.partial(attend_kernel, reach),
        "attend",
        table,
        [queries, pairs, own_ids, columns],
        [struct(tokens, bf16), struct((steps, GROUP, width), f32), struct((2,), jnp.int32)],
        [
            vmem((80 * GROUP, width), f32),
            vmem((8, width), f32),
            vmem((GROUP, 128, width), bf16),
            vmem((GROUP, width, width), f32),
        ],
        mib=6,
    )

    owned_wide, owned = inner // owners, features // owners
    kept_shrink = struct((2, half, owned_wide // 2, features), bf16)
    kept_expand = struct((features // 2, inner + features), bf16)
    layer_output, grad_middle, grad_attended, shrink_keep, shrink_send, expand_keep, expand_send, ffn_rows = call(
        functools.partial(ffn_kernel, half),
        "ffn",
        table,
        [attended, outlet_copy, raw, mean_row, inverse_row, vectors, cot, expand_copy, shrink_copy],
        [
            struct(tokens, bf16),
            struct(tokens, f32),
            struct(tokens, bf16),
            kept_shrink,
            kept_shrink,
            kept_expand,
            kept_expand,
            struct((12, features), f32),
        ],
        [
            vmem(tokens, f32),
            vmem(tokens, f32),
            vmem(tokens, bf16),
            vmem((features, width), bf16),
            vmem((features, width), bf16),
            vmem((features, width), f32),
            vmem((chunk, features), bf16),
            vmem(tokens, f32),
        ],
        mib=14,
    )
    bits = bits_of("dp")
    orders = (bits[1:], bits[:0:-1])

    def scatters(keep, arrived, rows):
        shape = (2,) + (2,) * (count - 1) + (rows // 2, keep.shape[-1])
        keep, arrived = keep.reshape(shape), arrived.reshape(shape)
        return [Scatter([keep[h], arrived[h]], orders[h]) for h in range(2)]

    token = [grad_attended]

    def after(*values):
        tied = together(*values, *token)[: len(values)]
        token[:] = tied
        return tied

    def launch(pair):
        for one in pair:
            one.prepare()
        token[:] = [one.sent for one in pair]
        for one in pair:
            one.send()

    def advance(pair):
        for one, value in zip(pair, after(*[one.arrived for one in pair])):
            one.arrived = value
            one.take()
        if pair[0].order:
            launch(pair)

    def follow(line, stage):
        (line.arrived,) = after(line.arrived)
        stage(line)
        token[:] = [line.keep]

    def begin(pair):
        line = Line(*pair, lows)
        token[:] = [line.sent]
        line.scatter()
        return line

    def next_round():
        rounds.take(after)
        token[:] = [rounds.block]
        if rounds.left():
            rounds.send()

    shrink_in = flipped(shrink_send, "dp", 1)
    expand_in = flipped(expand_send, "dp", 1)
    spread = struct((slots, width, lanes), bf16)
    back = []
    for g in range(steps):
        (grad_attended,) = after(grad_attended)
        back.append(
            call(
                functools.partial(attend_back_kernel, g),
                "attend_back",
                bounds,
                [queries, pairs, attended, grad_attended, lse, own_ids, columns],
                [struct((width, lanes), bf16), spread, spread, struct((2, lanes), f32)],
                [
                    vmem((lanes, width), f32),
                    vmem((GROUP, 128, width), bf16),
                    vmem((GROUP, 128, width), bf16),
                    vmem((GROUP // 2, 2 * width, 128), bf16),
                    vmem((GROUP // 2, 2 * width, 128), bf16),
                    vmem((GROUP, width, width), f32),
                    vmem((GROUP, width, width), f32),
                    vmem((GROUP // 2, width, 2 * width), bf16),
                    vmem((GROUP // 2, width, 2 * width), bf16),
                    vmem((16, width), f32),
                ],
                mib=8,
            )
        )
        token[:] = [back[-1][0]]
        if g == 0:
            (shrink_in,) = after(shrink_in)
            first = scatters(shrink_keep, shrink_in, owned_wide)
            launch(first)
    query_low, key_low, value_low, attend_rows = zip(*back)
    grads = [*query_low, *key_low, *value_low]
    (expand_in,) = after(expand_in)

    grads = after(*grads)
    parts, own_part = call(
        functools.partial(parts_kernel, reach),
        "parts",
        bounds,
        [*grads, inlet_copy],
        [struct((2 * reach, width, features), bf16), struct(tokens, f32)],
        mib=6,
    )
    to_left, to_right = parts[0], parts[2 * reach - 1]
    token[:] = [to_left, to_right]
    from_right, from_left = moved(to_left, "blk", -1), moved(to_right, "blk", 1)
    advance(first)

    kept_inlet = struct((features // 2, wkv), bf16)
    grads = after(*grads)
    inlet_keep, inlet_send = call(
        functools.partial(weight_kernel, reach, half, steps),
        "weights",
        table,
        xs + [(scalar, bounds), *grads],
        [kept_inlet, kept_inlet],
        [vmem((features, slots * width), bf16), vmem((features, width), f32)],
        mib=8,
    )
    token[:] = [inlet_keep]
    inlet_in = flipped(inlet_send, "dp", 1)
    while first[0].order:
        advance(first)
    advance(first)
    (expand_in,) = after(expand_in)
    second = scatters(expand_keep, expand_in, owned)
    launch(second)
    for d in range(reach - 1, 0, -1):
        from_right, from_left = after(from_right, from_left)
        to_left = added(parts[reach - d], from_right)
        to_right = added(parts[reach + d - 1], from_left)
        token[:] = [to_left, to_right]
        from_right, from_left = moved(to_left, "blk", -1), moved(to_right, "blk", 1)
    line_one = begin(first)
    from_right, from_left = after(from_right, from_left)
    grad_normed, small = call(
        leave_kernel,
        "leave",
        table,
        [
            raw,
            mean_row,
            inverse_row,
            vectors,
            grad_middle,
            own_part,
            from_left,
            from_right,
            ffn_rows,
            *attend_rows,
        ],
        [struct(tokens, f32), struct((16, features), f32)],
        mib=8,
    )
    token[:] = [small]
    rounds = SmallSum(small, paired=False)
    rounds.send()
    advance(second)
    (inlet_in,) = after(inlet_in)
    third = scatters(inlet_keep, inlet_in, owned)
    launch(third)
    next_round()
    follow(line_one, Line.exchange)
    while second[0].order:
        advance(second)
    advance(second)
    line_two = begin(second)
    next_round()
    advance(third)
    follow(line_two, Line.exchange)
    follow(line_one, Line.gather)
    next_round()
    while third[0].order:
        advance(third)
    advance(third)
    line_three = begin(third)
    while rounds.left():
        next_round()
    (line_two.arrived, line_three.arrived) = after(line_two.arrived, line_three.arrived)
    line_three.exchange()
    line_two.gather()
    *rounds.arrived, line_three.keep = together(*rounds.arrived, line_three.keep)
    rounds.take()
    small = rounds.block
    line_one.arrived, line_three.keep = together(line_one.arrived, line_three.keep)
    shrink_share = line_one.result()
    line_three.gather()
    expand_share = line_two.result()
    inlet_share = line_three.result()

    band_mean = totals[0] / total_tokens
    band_variance = totals[1] / total_tokens - band_mean * band_mean
    inverse = lax.rsqrt(band_variance + stat_epsilon)
    back_totals = small[12:14]
    grad_variance = -0.5 * back_totals[1] * inverse * inverse * inverse
    grad_centre = -inverse * back_totals[0] - 2.0 * band_mean * grad_variance
    input_gradient = (
        grad_normed * inverse
        + grad_centre / total_tokens
        + 2.0 * grad_variance * raw / total_tokens
    ).reshape(sequences, block_length, features)
    vector_share = lax.dynamic_slice(
        small[:12], (0, column_start), (12, column_count), allow_negative_indices=False
    )

    updates = []
    for master, moment, square, share in (
        (inlet_master, inlet_moment, inlet_square, inlet_share),
        (outlet_master, outlet_moment, outlet_square, expand_share[:, inner:]),
        (expand_master, expand_moment, expand_square, expand_share[:, :inner]),
        (shrink_master, shrink_moment, shrink_square, shrink_share),
    ):
        updates.extend(
            adam_rule(
                master, moment, square, share.astype(f32), step_value, rate_matrix, decay_matrix
            )
        )
    updates.extend(
        adam_rule(
            vector_master, vector_moment, vector_square, vector_share, step_value, rate_vector, 0.0
        )
    )
    layer_output = layer_output.reshape(sequences, block_length, features)
    return (layer_output, input_gradient, band_mean, band_variance, *updates)


def solution(mesh):
    tokens = P("dp", "blk", None)
    rows = P("dp", None)
    columns = P(None, "dp")
    matrix = (P(), rows, rows, rows)
    return jax.shard_map(
        per_device,
        mesh=mesh,
        in_specs=(tokens, tokens, P("dp", "blk"), P())
        + matrix * 4
        + (P(), columns, columns, columns),
        out_specs=(tokens, tokens, P(), P()) + (rows,) * 16 + (columns,) * 4,
        check_vma=False,
    )
```

```python
import functools

import jax
import jax.numpy as jnp
from jax import lax
from jax.experimental import pallas as pl
from jax.experimental.pallas import tpu as pltpu
from jax.sharding import PartitionSpec as P

HEADS = 12
HEAD_WIDTH = 64
GROUP = 4

ln_epsilon = 1e-05
stat_epsilon = 1e-06
beta_one = 0.5
beta_two = 0.6
rate_matrix = 0.04
rate_vector = 0.8
warmup_length = 20.0
decay_matrix = 0.05
adam_epsilon = 1e-08
score_scale = 0.125
masked_score = -1e30

f32 = jnp.float32
bf16 = jnp.bfloat16


def nn(a, b):
    return lax.dot_general(a, b, (((1,), (0,)), ((), ())), preferred_element_type=f32)


def nt(a, b):
    return lax.dot_general(a, b, (((1,), (1,)), ((), ())), preferred_element_type=f32)


def tn(a, b):
    return lax.dot_general(a, b, (((0,), (0,)), ((), ())), preferred_element_type=f32)


def flipped(block, axis, bit):
    size = lax.axis_size(axis)
    return lax.ppermute(block, axis, [(i, i ^ bit) for i in range(size)])


def moved(block, axis, distance):
    size = lax.axis_size(axis)
    route = [(i, i + distance) for i in range(size) if 0 <= i + distance < size]
    return lax.ppermute(block, axis, route)


def bits_of(axis):
    size = lax.axis_size(axis)
    return [1 << i for i in range(size.bit_length() - 1)]


class SmallSum:
    def __init__(self, block, paired=True):
        self.block, self.rounds = block, []
        if not paired:
            self.rounds = [(axis, [bit]) for axis in ("blk", "dp") for bit in bits_of(axis)]
            return
        for axis in ("dp", "blk"):
            bits = bits_of(axis)
            odd = len(bits) % 2
            parts = [bits[:odd]] * odd + [bits[i : i + 2] for i in range(odd, len(bits), 2)]
            self.rounds += [(axis, part) for part in parts]

    def left(self):
        return len(self.rounds)

    def send(self):
        axis, part = self.rounds.pop(0)
        ways = part if len(part) == 1 else [part[0], part[1], part[0] | part[1]]
        self.arrived = [flipped(self.block, axis, way) for way in ways]

    def take(self, tie=lambda *values: values):
        others = tie(*self.arrived)
        if len(others) == 1:
            self.block = self.block + others[0]
        else:
            self.block = (self.block + others[0]) + (others[1] + others[2])


def added(kept, arrived):
    return (kept.astype(f32) + arrived.astype(f32)).astype(bf16)


def summed(addends):
    total = addends[0].astype(f32)
    for addend in addends[1:]:
        total = total + addend.astype(f32)
    return total.astype(bf16)


class Scatter:
    def __init__(self, addends, order):
        self.addends, self.order = list(addends), list(order)

    def prepare(self):
        self.sent = summed([addend[1] for addend in self.addends])

    def send(self):
        self.arrived = flipped(self.sent, "dp", self.order.pop(0))

    def take(self):
        self.addends = [addend[0] for addend in self.addends] + [self.arrived]


class Line:
    def __init__(self, first, second, lows):
        self.bits, self.lows = bits_of("blk"), lows
        first, second = summed(first.addends), summed(second.addends)
        self.keep = jnp.where(lows[0], first, second)
        self.sent = jnp.where(lows[0], second, first)

    def scatter(self):
        self.arrived = flipped(self.sent, "blk", 1)

    def exchange(self):
        share = added(self.keep, self.arrived)
        for bit, low in zip(self.bits[1:-1], self.lows[1:]):
            middle = share.shape[0] // 2
            keep = jnp.where(low, share[:middle], share[middle:])
            sent = jnp.where(low, share[middle:], share[:middle])
            share = added(keep, flipped(sent, "blk", bit))
        self.keep = share
        self.arrived = flipped(share, "blk", self.bits[-1])

    def joined(self, low):
        mine, other = self.keep, self.arrived
        return jnp.concatenate(
            [jnp.where(low, mine, other), jnp.where(low, other, mine)], axis=0
        )

    def gather(self):
        share = added(self.keep, self.arrived)
        for bit, low in reversed(list(zip(self.bits[1:-1], self.lows[1:]))):
            self.keep, self.arrived = share, flipped(share, "blk", bit)
            share = self.joined(low)
        self.keep = share
        self.arrived = flipped(share, "blk", 1)

    def result(self):
        return self.joined(self.lows[0])


def together(*values):
    return lax.optimization_barrier(values)


def whole(shape):
    return pl.BlockSpec(shape, lambda *a: (0,) * len(shape))


def call(kernel, name, table, operands, outs, scratch=(), mib=8):
    scalar = pl.BlockSpec(memory_space=pltpu.SMEM)
    return pl.pallas_call(
        kernel,
        grid_spec=pltpu.PrefetchScalarGridSpec(
            num_scalar_prefetch=1,
            grid=(1,),
            in_specs=[
                spec if isinstance(spec, pl.BlockSpec) else whole(spec.shape)
                for spec in (o[0] if isinstance(o, tuple) else o for o in operands)
            ],
            out_specs=[scalar if o.shape == (2,) else whole(o.shape) for o in outs],
            scratch_shapes=list(scratch),
        ),
        out_shape=outs,
        cost_estimate=pl.CostEstimate(flops=1 << 20, bytes_accessed=1 << 16, transcendentals=0),
        compiler_params=pltpu.CompilerParams(vmem_limit_bytes=mib << 20),
        name=name,
    )(table, *[o[1] if isinstance(o, tuple) else o for o in operands])


def struct(shape, dtype):
    return jax.ShapeDtypeStruct(shape, dtype)


def unit_rows(rows):
    centred = rows - jnp.mean(rows, axis=-1, keepdims=True)
    scale = lax.rsqrt(jnp.mean(centred * centred, axis=-1, keepdims=True) + ln_epsilon)
    return centred * scale, scale


def norm_back(grad, unit, scale, gain):
    inner = grad * gain
    return scale * (
        inner
        - jnp.mean(inner, axis=-1, keepdims=True)
        - unit * jnp.mean(inner * unit, axis=-1, keepdims=True)
    )


def column_sum(rows):
    return jnp.sum(rows, axis=0, keepdims=True)


def totals_kernel(table, raw_ref, out_ref):
    raw = raw_ref[...]
    out_ref[0:1, :] = column_sum(raw)
    out_ref[1:2, :] = column_sum(raw * raw)


def enter_kernel(total_tokens, table, raw_ref, sum_ref, vec_ref, id_ref, x_ref, mean_ref, std_ref):
    width = raw_ref.shape[0]
    mean = sum_ref[0:1, :] / total_tokens
    variance = sum_ref[1:2, :] / total_tokens - mean * mean
    inverse = lax.rsqrt(variance + stat_epsilon)
    mean_ref[...] = mean
    std_ref[...] = inverse
    unit, _ = unit_rows((raw_ref[...] - mean) * inverse)
    x_ref[0:width, :] = (unit * vec_ref[0:1, :] + vec_ref[1:2, :]).astype(bf16)
    x_ref[width:, :] = jnp.zeros((x_ref.shape[0] - width, x_ref.shape[1]), bf16)
    ids = jnp.broadcast_to(id_ref[...], (16, width)).astype(f32).astype(bf16)
    x_ref[width:, 0:width] = ids


def id_columns(ids, width):
    return jnp.broadcast_to(ids, (128, width)).T


def id_row(rows):
    return rows.astype(f32)[0:1]


def project_own_kernel(table, x_ref, w_ref, vec_ref, q_ref, kv_ref, id_ref):
    width = q_ref.shape[0]
    features = q_ref.shape[1]
    slot = kv_ref.shape[0] // 2
    x = x_ref[0:width, :]
    q_ref[...] = ((nn(x, w_ref[:, :features]) + vec_ref[4:5, :]) * score_scale).astype(bf16)
    kv_ref[slot, :, :features] = nn(x, w_ref[:, features : 2 * features]).astype(bf16)
    kv_ref[slot, :, features:] = (nn(x, w_ref[:, 2 * features :]) + vec_ref[5:6, :]).astype(bf16)
    id_ref[slot] = id_columns(id_row(x_ref[width : width + 8, 0:width]), width)


def project_pair_kernel(
    d, inside_at, table, xa_ref, xb_ref, x_ref, w_ref, vec_ref, kv_in, id_in, kv_ref, id_ref, both
):
    width = kv_ref.shape[1]
    features = kv_ref.shape[2] // 2
    reach = kv_ref.shape[0] // 2
    done = slice(reach - d + 1, reach + d)
    kv_ref[done] = kv_in[done]
    id_ref[done] = id_in[done]
    both[0], both[1] = xa_ref[...], xb_ref[...]
    own = id_row(x_ref[width : width + 8, 0:width])
    low, high = jnp.min(own), jnp.max(own)

    def one(i, carry):
        slot = reach - d + 2 * d * i
        ids = id_row(both[i, width : width + 8, 0:width])
        near = (table[inside_at + i] > 0) & (jnp.max(ids) >= low) & (jnp.min(ids) <= high)
        id_ref[slot] = jnp.full((width, 128), -1.0, f32)

        @pl.when(near)
        def _():
            x = both[i, 0:width, :]
            kv_ref[slot, :, :features] = nn(x, w_ref[:, features : 2 * features]).astype(bf16)
            kv_ref[slot, :, features:] = (
                nn(x, w_ref[:, 2 * features :]) + vec_ref[5:6, :]
            ).astype(bf16)
            id_ref[slot] = id_columns(ids, width)

        return carry

    lax.fori_loop(0, 2, one, 0)


def lane_half(rows, which):
    lanes = lax.broadcasted_iota(jnp.int32, (rows, 128), 1)
    return (lanes >= 64) if which else (lanes < 64)


def mask_rows(own_row, width):
    ids = lax.broadcasted_iota(jnp.int32, (64, width), 0).astype(f32)
    return jnp.where(ids == own_row, 0.0, masked_score).astype(bf16)


def key_marks(column, width):
    lane_ids = (lax.broadcasted_iota(jnp.int32, (width, 128), 1) % 64).astype(f32)
    return (column == lane_ids).astype(f32).astype(bf16)


def lane_group(g):
    return pl.ds(pl.multiple_of(g * GROUP * HEAD_WIDTH, 128), GROUP * HEAD_WIDTH)


def attend_kernel(reach, table, q_ref, kv_ref, qid_ref, kid_ref, o_ref, lse_ref, bound_ref, acc, top, qm, sc):
    width, features = q_ref.shape
    slots = kv_ref.shape[0]
    steps = features // (GROUP * HEAD_WIDTH)
    low = kid_ref[reach, 0:1, :]
    high = kid_ref[reach, width - 1 : width, :]
    start = jnp.full_like(low, float(reach))
    end = jnp.full_like(low, float(reach))
    for s in range(slots):
        active = (kid_ref[s, width - 1 : width, :] >= low) & (kid_ref[s, 0:1, :] <= high)
        start = jnp.where(active, jnp.minimum(start, float(s)), start)
        end = jnp.where(active, jnp.maximum(end, float(s)), end)
    bound_ref[0] = jnp.min(start).astype(jnp.int32)
    bound_ref[1] = jnp.max(end).astype(jnp.int32) + 1
    barred = mask_rows(qid_ref[...].astype(f32), width)
    upper = lane_half(width, 1)
    one_rows = (lax.broadcasted_iota(jnp.int32, (16, width), 0) == 0).astype(f32).astype(bf16)

    def group(g, carry):
        lanes_g = lane_group(g)
        lanes_v = pl.ds(pl.multiple_of(features + g * GROUP * HEAD_WIDTH, 128), GROUP * HEAD_WIDTH)
        top[...] = jnp.full_like(top, masked_score)
        acc[...] = jnp.zeros_like(acc)
        q_t = q_ref[:, lanes_g].T
        for h in range(GROUP):
            head = q_t[64 * h : 64 * h + 64, :]
            qm[h, 0:64, :] = barred if h % 2 else head
            qm[h, 64:128, :] = head if h % 2 else barred

        def step(s, carry):
            keys = kv_ref[s, :, lanes_g]
            values_t = kv_ref[s, :, lanes_v].T
            marks = key_marks(kid_ref[s], width)
            for h in range(GROUP):
                lanes = slice(128 * (h // 2), 128 * (h // 2) + 128)
                pair = keys[:, lanes]
                marked = jnp.where(upper, pair, marks) if h % 2 else jnp.where(upper, marks, pair)
                sc[h] = nn(marked, qm[h])
            for h in range(GROUP):
                score = sc[h]
                old = top[h : h + 1, :]
                new = jnp.maximum(old, jnp.max(score, axis=0, keepdims=True))
                fade = jnp.exp(old - new)
                weight = jnp.exp(score - new).astype(bf16)
                top[h : h + 1, :] = new
                rows = slice(80 * h, 80 * h + 80)
                left = jnp.concatenate([values_t[64 * h : 64 * h + 64, :], one_rows], axis=0)
                acc[rows, :] = acc[rows, :] * fade + nn(left, weight)
            return carry

        lax.fori_loop(bound_ref[0], bound_ref[1], step, 0)
        outs, lses = [], []
        for h in range(GROUP):
            total = acc[80 * h + 64 : 80 * h + 65, :]
            outs.append(acc[80 * h : 80 * h + 64, :] / total)
            lses.append(top[h : h + 1, :] + jnp.log(total))
        o_ref[:, lanes_g] = jnp.concatenate(outs, axis=0).T.astype(bf16)
        lse_ref[g] = jnp.concatenate(lses, axis=0)
        return carry

    lax.fori_loop(0, steps, group, 0)


def spread_rows(table, plain, target, lanes, half):
    part = plain.shape[0] // (4 * half)
    for side in range(2):
        for h in range(2):
            for p in range(half):
                owner = table[half * (1 + 2 * h + side) + p]
                place = pl.multiple_of((2 * owner + h) * part, 8)
                to = ((side * 2 + h) * half + p) * part
                target[to : to + part, lanes] = plain[pl.ds(place, part), :].astype(bf16)


def ffn_kernel(
    half,
    table,
    o_ref,
    wo_ref,
    raw_ref,
    mean_ref,
    std_ref,
    vec_ref,
    cot_ref,
    w1_ref,
    w2_ref,
    out_ref,
    gm_ref,
    ga_ref,
    sk_ref,
    ss_ref,
    ek_ref,
    es_ref,
    row_ref,
    middle_s,
    gsec,
    s2,
    s2t,
    ot,
    plain,
    rows_s,
    acc,
):
    features = gm_ref.shape[1]
    inner = w1_ref.shape[1]
    chunk = inner // half
    wide = chunk // 2
    normed = (raw_ref[...] - mean_ref[...]) * std_ref[...]
    middle = normed + nn(o_ref[...], wo_ref[...]) + vec_ref[6:7, :]
    middle_s[...] = middle
    unit, _ = unit_rows(middle)
    second = unit * vec_ref[2:3, :] + vec_ref[3:4, :]
    s2[...] = second.astype(bf16)
    plain[...] = second.T
    spread_rows(table, plain, s2t, slice(None), half)
    plain[...] = o_ref[...].T.astype(f32)
    spread_rows(table, plain, ot, slice(None), half)
    acc[...] = jnp.zeros_like(acc)
    gsec[...] = jnp.zeros_like(gsec)
    own = table[half] % 2

    def step(i, carry):
        place = table[i] * chunk
        lanes = pl.ds(pl.multiple_of(place, 128), chunk)
        row = pl.ds(8 + place // features, 1)
        row_lanes = pl.ds(pl.multiple_of(place % features, 128), chunk)
        w1 = w1_ref[:, lanes]
        w2 = w2_ref[lanes, :]
        pre = nn(s2[...], w1) + vec_ref[row, row_lanes]
        back = nt(cot_ref[...], w2)
        area = 0.5 * (1.0 + lax.erf(pre * (0.5**0.5)))
        bell = jnp.exp(-0.5 * pre * pre) * (1.0 / (2.0 * jnp.pi) ** 0.5)
        hidden = (pre * area).astype(bf16)
        grad = ((area + pre * bell) * back).astype(bf16)
        acc[...] += nn(hidden, w2)
        gsec[...] += nt(grad, w1)
        row_ref[row, row_lanes] = column_sum(grad.astype(f32))
        rows_s[...] = nn(hidden.T, cot_ref[...]).astype(bf16)
        for side, ref in ((0, sk_ref), (1, ss_ref)):
            first = jnp.where(own == side, 0, wide)
            for h, at in ((0, i), (1, table[5 * half + i])):
                start = pl.multiple_of(first + h * (wide // 2), 16)
                ref[h, at] = rows_s[pl.ds(start, wide // 2), :]
        ek_ref[:, lanes] = nn(s2t[: features // 2, :], grad).astype(bf16)
        es_ref[:, lanes] = nn(s2t[features // 2 :, :], grad).astype(bf16)
        return carry

    lax.fori_loop(0, half, step, 0, unroll=True)
    out_ref[...] = (middle_s[...] + acc[...] + vec_ref[7:8, :]).astype(bf16)
    unit, scale = unit_rows(middle_s[...])
    grad = gsec[...]
    cot = cot_ref[...].astype(f32)
    row_ref[0:1, :] = column_sum(grad * unit)
    row_ref[1:2, :] = column_sum(grad)
    grad_middle = cot + norm_back(grad, unit, scale, vec_ref[2:3, :])
    gm_ref[...] = grad_middle
    branch = grad_middle.astype(bf16)
    row_ref[2:3, :] = column_sum(branch.astype(f32))
    row_ref[3:4, :] = column_sum(cot)
    ga_ref[...] = nt(branch, wo_ref[...]).astype(bf16)
    ek_ref[:, inner:] = nn(ot[: features // 2, :], branch).astype(bf16)
    es_ref[:, inner:] = nn(ot[features // 2 :, :], branch).astype(bf16)


def attend_back_kernel(
    g,
    bounds,
    q_ref,
    kv_ref,
    o_ref,
    g_ref,
    lse_ref,
    qid_ref,
    kid_ref,
    dq_ref,
    dk_ref,
    dv_ref,
    row_ref,
    acc,
    qm,
    gm,
    q_stack,
    g_stack,
    sc,
    dp,
    p_wide,
    g_wide,
    rows_s,
):
    width, features = q_ref.shape
    slots = kv_ref.shape[0]
    barred = mask_rows(qid_ref[...].astype(f32), width)
    nothing = jnp.zeros((64, width), bf16)
    upper = lane_half(width, 1)

    def blank(s, carry):
        dk_ref[s] = jnp.zeros(dk_ref.shape[1:], dk_ref.dtype)
        dv_ref[s] = jnp.zeros(dv_ref.shape[1:], dv_ref.dtype)
        return carry

    lax.fori_loop(0, bounds[0], blank, 0)
    lax.fori_loop(bounds[1], slots, blank, 0)

    base = g * GROUP * HEAD_WIDTH
    lanes_g = slice(base, base + GROUP * HEAD_WIDTH)
    lanes_v = slice(features + base, features + base + GROUP * HEAD_WIDTH)
    acc[...] = jnp.zeros_like(acc)
    q_all, g_all = q_ref[:, lanes_g], g_ref[:, lanes_g]
    product = (g_all.astype(f32) * o_ref[:, lanes_g].astype(f32)).T
    q_t, g_t = q_all.T, g_all.T
    for h in range(GROUP):
        lanes = slice(128 * (h // 2), 128 * (h // 2) + 128)
        rows = slice(64 * h, 64 * h + 64)
        odd = h % 2
        qm[h, 0:64, :] = barred if odd else q_t[rows, :]
        qm[h, 64:128, :] = q_t[rows, :] if odd else barred
        gm[h, 0:64, :] = nothing if odd else g_t[rows, :]
        gm[h, 64:128, :] = g_t[rows, :] if odd else nothing
        half = lane_half(width, odd)
        place = slice(width * odd, width * odd + width)
        pair = q_all[:, lanes]
        q_stack[h // 2, place, :] = jnp.where(half, pair, jnp.zeros_like(pair))
        pair = g_all[:, lanes]
        g_stack[h // 2, place, :] = jnp.where(half, pair, jnp.zeros_like(pair))
        rows_s[h : h + 1, :] = column_sum(product[rows, :])
    rows_s[8:9, :] = jnp.zeros((1, GROUP * HEAD_WIDTH), f32)

    def step(s, carry):
        keys = kv_ref[s, :, lanes_g]
        values = kv_ref[s, :, lanes_v]
        keys_t = keys.T
        marks = key_marks(kid_ref[s], width)
        for h in range(GROUP):
            lanes = slice(128 * (h // 2), 128 * (h // 2) + 128)
            pair = keys[:, lanes]
            marked = jnp.where(upper, pair, marks) if h % 2 else jnp.where(upper, marks, pair)
            sc[h] = nn(marked, qm[h])
            dp[h] = nn(values[:, lanes], gm[h])
        for h in range(GROUP):
            place = slice(width * (h % 2), width * (h % 2) + width)
            prob = jnp.exp(sc[h] - lse_ref[g, h : h + 1, :])
            p_wide[h // 2, :, place] = prob.astype(bf16)
            g_wide[h // 2, :, place] = (prob * (dp[h] - rows_s[h : h + 1, :])).astype(bf16)
        for h in range(GROUP):
            place = slice(width * (h % 2), width * (h % 2) + width)
            rows = slice(64 * h, 64 * h + 64)
            acc[rows, :] += nn(keys_t[rows, :], g_wide[h // 2, :, place])
        key_parts, value_parts = [], []
        for j in range(GROUP // 2):
            value_parts.append(nn(p_wide[j], g_stack[j]))
            key_parts.append(nn(g_wide[j], q_stack[j]))
        value_all = jnp.concatenate(value_parts, axis=1)
        dk_ref[s] = jnp.concatenate(key_parts, axis=1).astype(bf16)
        dv_ref[s] = value_all.astype(bf16)
        rows_s[8:9, :] += column_sum(value_all)
        return carry

    lax.fori_loop(bounds[0], bounds[1], step, 0)
    dq = (acc[...].T.astype(bf16).astype(f32) * score_scale).astype(bf16)
    dq_ref[...] = dq
    row_ref[0:1, :] = column_sum(dq.astype(f32))
    row_ref[1:2, :] = rows_s[8:9, :]


def parts_kernel(reach, bounds, *refs):
    groups = (len(refs) - 3) // 3
    dqs, dks, dvs = (refs[k * groups : (k + 1) * groups] for k in range(3))
    w_ref, p_ref, own_ref = refs[3 * groups :]
    features = p_ref.shape[2]
    size = features // groups

    def part(s):
        total = None
        for g in range(groups):
            for ref, base in ((dks[g], features), (dvs[g], 2 * features)):
                now = nt(ref[s], w_ref[:, base + g * size : base + (g + 1) * size])
                total = now if total is None else total + now
        return total

    def one(s, to):
        active = (s >= bounds[0]) & (s < bounds[1])

        @pl.when(active)
        def _():
            p_ref[to] = part(s).astype(bf16)

        @pl.when(jnp.logical_not(active))
        def _():
            p_ref[to] = jnp.zeros(p_ref.shape[1:], p_ref.dtype)

    def some(i, carry):
        one(jnp.where(i < reach, i, i + 1), i)
        return carry

    lax.fori_loop(0, 2 * reach, some, 0)
    total = part(reach)
    for g in range(groups):
        total = total + nt(dqs[g][...], w_ref[:, g * size : (g + 1) * size])
    own_ref[...] = total


def weight_kernel(reach, half, groups, table, *refs):
    slots = 2 * reach + 1
    xs, bounds = refs[:slots], refs[slots]
    refs = refs[slots + 1 :]
    dqs, dks, dvs = (refs[k * groups : (k + 1) * groups] for k in range(3))
    keep_ref, send_ref, xt, plain = refs[3 * groups :]
    width, size = dqs[0].shape
    features = size * groups
    few = min(3, slots)
    small = bounds[1] - bounds[0] <= few
    start = jnp.minimum(bounds[0], slots - few)

    for s in range(slots):

        @pl.when(jnp.logical_not(small) | ((s >= start) & (s < start + few)))
        def _(s=s):
            plain[...] = xs[s][0:width, :].T.astype(f32)
            spread_rows(table, plain, xt, slice(width * s, width * s + width), half)

    def put(tokens, right, base):
        lanes = slice(base, base + size)
        keep_ref[:, lanes] = nn(xt[: features // 2, tokens], right).astype(bf16)
        send_ref[:, lanes] = nn(xt[features // 2 :, tokens], right).astype(bf16)

    for g in range(groups):
        put(slice(width * reach, width * reach + width), dqs[g][...], g * size)

    def over(start, count):
        tokens = pl.ds(pl.multiple_of(start * width, 128), count * width)
        for base, group in ((features, dks), (2 * features, dvs)):
            for g in range(groups):
                rows = group[g][pl.ds(start, count)].reshape(count * width, size)
                put(tokens, rows, base + g * size)

    @pl.when(small)
    def _():
        over(start, few)

    @pl.when(jnp.logical_not(small))
    def _():
        over(0, slots)


def leave_kernel(
    table,
    raw_ref,
    mean_ref,
    std_ref,
    vec_ref,
    gm_ref,
    own_ref,
    left_ref,
    right_ref,
    ffn_rows,
    *refs,
):
    attend_rows, (gn_ref, row_ref) = refs[:-2], refs[-2:]
    features = raw_ref.shape[1]
    centred = raw_ref[...] - mean_ref[...]
    unit, scale = unit_rows(centred * std_ref[...])
    grad = own_ref[...] + left_ref[...].astype(f32) + right_ref[...].astype(f32)
    row_ref[0:1, :] = column_sum(grad * unit)
    row_ref[1:2, :] = column_sum(grad)
    row_ref[2:4, :] = ffn_rows[0:2, :]
    size = features // len(attend_rows)
    for g, ref in enumerate(attend_rows):
        row_ref[4:6, g * size : (g + 1) * size] = ref[...]
    row_ref[6:8, :] = ffn_rows[2:4, :]
    row_ref[8:12, :] = ffn_rows[8:12, :]
    whole_grad = gm_ref[...] + norm_back(grad, unit, scale, vec_ref[0:1, :])
    gn_ref[...] = whole_grad
    row_ref[12:13, :] = column_sum(whole_grad)
    row_ref[13:14, :] = column_sum(whole_grad * centred)
    row_ref[14:16, :] = jnp.zeros((2, features), f32)


def adam_rule(master, moment, square, gradient, step_value, step_rate, weight_decay):
    moment_new = beta_one * moment + (1.0 - beta_one) * gradient
    square_new = beta_two * square + (1.0 - beta_two) * gradient * gradient
    fix_first = 1.0 - jnp.power(beta_one, step_value)
    fix_second = 1.0 - jnp.power(beta_two, step_value)
    planned = step_rate * jnp.minimum(1.0, step_value / warmup_length)
    direction = moment_new / fix_first / (jnp.sqrt(square_new / fix_second) + adam_epsilon)
    weight_new = master - planned * (direction + weight_decay * master)
    return (weight_new, moment_new, square_new, weight_new.astype(bf16))


def per_device(
    raw_input,
    cotangent,
    segment_ids,
    step_count,
    inlet_copy,
    inlet_master,
    inlet_moment,
    inlet_square,
    outlet_copy,
    outlet_master,
    outlet_moment,
    outlet_square,
    expand_copy,
    expand_master,
    expand_moment,
    expand_square,
    shrink_copy,
    shrink_master,
    shrink_moment,
    shrink_square,
    vector_copy,
    vector_master,
    vector_moment,
    vector_square,
):
    sequences, block_length, features = raw_input.shape
    assert sequences == 1
    width = block_length
    group_size = lax.axis_size("blk")
    group_index = lax.axis_index("blk")
    owners = lax.axis_size("dp")
    owner = lax.axis_index("dp")
    half = owners // 2
    total_tokens = owners * group_size * block_length
    reach = group_size // 2
    slots = 2 * reach + 1
    inner = expand_copy.shape[1]
    chunk = inner // half
    vectors = vector_copy.astype(f32)
    raw = raw_input.reshape(width, features)
    cot = cotangent.reshape(width, features)
    own_ids = segment_ids
    count = owners.bit_length() - 1
    scalar = pl.BlockSpec(memory_space=pltpu.SMEM)
    vmem = pltpu.VMEM

    def reversed_bits(value):
        return int(format(value, f"0{count - 1}b")[::-1], 2) if count > 1 else 0

    straight = [reversed_bits(p) for p in range(half)]
    other_way = list(range(half))
    relative = jnp.array(
        [2 * v for v in straight]
        + [2 * v for v in straight]
        + [2 * v + 1 for v in straight]
        + [2 * v for v in other_way]
        + [2 * v + 1 for v in other_way],
        jnp.int32,
    ) ^ owner
    inside = [group_index >= d for d in range(1, reach + 1)]
    inside += [group_index + d < group_size for d in range(1, reach + 1)]
    table = jnp.concatenate(
        [
            relative[:half] // 2,
            relative[half:],
            jnp.array(straight, jnp.int32),
            jnp.stack([flag for pair in zip(inside[:reach], inside[reach:]) for flag in pair]).astype(jnp.int32),
        ]
    )
    lows = [(group_index // bit) % 2 == 0 for bit in bits_of("blk")]
    column_count = vector_master.shape[1]
    column_start = owner * column_count
    step_value = step_count[0].astype(f32)

    tokens, row = (width, features), (1, features)
    wkv = 3 * features
    lanes = GROUP * HEAD_WIDTH
    steps = features // lanes

    (totals,) = call(
        totals_kernel, "totals", jnp.zeros((1,), jnp.int32), [raw], [struct((2, features), f32)], mib=2
    )
    rounds = SmallSum(totals)
    rounds.send()
    rounds.take()
    rounds.send()
    tied = together(*rounds.arrived, table, column_start, vectors, *lows)
    ways = len(rounds.arrived)
    rounds.arrived = list(tied[:ways])
    table, column_start, vectors = tied[ways : ways + 3]
    lows = list(tied[ways + 3 :])
    rounds.take()
    while rounds.left():
        rounds.send()
        rounds.take()
    totals = rounds.block
    packed = width + 16
    x, mean_row, inverse_row = call(
        functools.partial(enter_kernel, total_tokens),
        "enter",
        table,
        [raw, totals, vectors, own_ids],
        [struct((packed, features), bf16), struct(row, f32), struct(row, f32)],
        mib=6,
    )

    xs = [None] * slots
    xs[reach] = x
    ahead, behind = moved(x, "blk", 1), moved(x, "blk", -1)
    queries, pairs, columns = call(
        project_own_kernel,
        "project_own",
        table,
        [x, inlet_copy, vectors],
        [
            struct(tokens, bf16),
            struct((slots, width, 2 * features), bf16),
            struct((slots, width, 128), f32),
        ],
        mib=6,
    )
    ahead, behind, queries = together(ahead, behind, queries)
    for d in range(1, reach + 1):
        if d > 1:
            ahead, behind = moved(ahead, "blk", 1), moved(behind, "blk", -1)
            ahead, behind, pairs = together(ahead, behind, pairs)
        xs[reach - d], xs[reach + d] = ahead, behind
        pairs, columns = call(
            functools.partial(project_pair_kernel, d, 6 * half + 2 * (d - 1)),
            "project_pair",
            table,
            [ahead, behind, x, inlet_copy, vectors, pairs, columns],
            [struct(pairs.shape, bf16), struct(columns.shape, f32)],
            [vmem((2, packed, features), bf16)],
            mib=6,
        )

    attended, lse, bounds = call(
        functools.partial(attend_kernel, reach),
        "attend",
        table,
        [queries, pairs, own_ids, columns],
        [struct(tokens, bf16), struct((steps, GROUP, width), f32), struct((2,), jnp.int32)],
        [
            vmem((80 * GROUP, width), f32),
            vmem((8, width), f32),
            vmem((GROUP, 128, width), bf16),
            vmem((GROUP, width, width), f32),
        ],
        mib=6,
    )

    owned_wide, owned = inner // owners, features // owners
    kept_shrink = struct((2, half, owned_wide // 2, features), bf16)
    kept_expand = struct((features // 2, inner + features), bf16)
    layer_output, grad_middle, grad_attended, shrink_keep, shrink_send, expand_keep, expand_send, ffn_rows = call(
        functools.partial(ffn_kernel, half),
        "ffn",
        table,
        [attended, outlet_copy, raw, mean_row, inverse_row, vectors, cot, expand_copy, shrink_copy],
        [
            struct(tokens, bf16),
            struct(tokens, f32),
            struct(tokens, bf16),
            kept_shrink,
            kept_shrink,
            kept_expand,
            kept_expand,
            struct((12, features), f32),
        ],
        [
            vmem(tokens, f32),
            vmem(tokens, f32),
            vmem(tokens, bf16),
            vmem((features, width), bf16),
            vmem((features, width), bf16),
            vmem((features, width), f32),
            vmem((chunk, features), bf16),
            vmem(tokens, f32),
        ],
        mib=14,
    )
    bits = bits_of("dp")
    orders = (bits[1:], bits[:0:-1])

    def scatters(keep, arrived, rows):
        shape = (2,) + (2,) * (count - 1) + (rows // 2, keep.shape[-1])
        keep, arrived = keep.reshape(shape), arrived.reshape(shape)
        return [Scatter([keep[h], arrived[h]], orders[h]) for h in range(2)]

    token = [grad_attended]

    def after(*values):
        tied = together(*values, *token)[: len(values)]
        token[:] = tied
        return tied

    def launch(pair):
        for one in pair:
            one.prepare()
        token[:] = [one.sent for one in pair]
        for one in pair:
            one.send()

    def advance(pair):
        for one, value in zip(pair, after(*[one.arrived for one in pair])):
            one.arrived = value
            one.take()
        if pair[0].order:
            launch(pair)

    def follow(line, stage):
        (line.arrived,) = after(line.arrived)
        stage(line)
        token[:] = [line.keep]

    def begin(pair):
        line = Line(*pair, lows)
        token[:] = [line.sent]
        line.scatter()
        return line

    def next_round():
        rounds.take(after)
        token[:] = [rounds.block]
        if rounds.left():
            rounds.send()

    shrink_in = flipped(shrink_send, "dp", 1)
    expand_in = flipped(expand_send, "dp", 1)
    spread = struct((slots, width, lanes), bf16)
    back = []
    for g in range(steps):
        (grad_attended,) = after(grad_attended)
        back.append(
            call(
                functools.partial(attend_back_kernel, g),
                "attend_back",
                bounds,
                [queries, pairs, attended, grad_attended, lse, own_ids, columns],
                [struct((width, lanes), bf16), spread, spread, struct((2, lanes), f32)],
                [
                    vmem((lanes, width), f32),
                    vmem((GROUP, 128, width), bf16),
                    vmem((GROUP, 128, width), bf16),
                    vmem((GROUP // 2, 2 * width, 128), bf16),
                    vmem((GROUP // 2, 2 * width, 128), bf16),
                    vmem((GROUP, width, width), f32),
                    vmem((GROUP, width, width), f32),
                    vmem((GROUP // 2, width, 2 * width), bf16),
                    vmem((GROUP // 2, width, 2 * width), bf16),
                    vmem((16, width), f32),
                ],
                mib=8,
            )
        )
        token[:] = [back[-1][0]]
        if g == 0:
            (shrink_in,) = after(shrink_in)
            first = scatters(shrink_keep, shrink_in, owned_wide)
            launch(first)
    query_low, key_low, value_low, attend_rows = zip(*back)
    grads = [*query_low, *key_low, *value_low]
    (expand_in,) = after(expand_in)

    grads = after(*grads)
    parts, own_part = call(
        functools.partial(parts_kernel, reach),
        "parts",
        bounds,
        [*grads, inlet_copy],
        [struct((2 * reach, width, features), bf16), struct(tokens, f32)],
        mib=6,
    )
    to_left, to_right = parts[0], parts[2 * reach - 1]
    token[:] = [to_left, to_right]
    from_right, from_left = moved(to_left, "blk", -1), moved(to_right, "blk", 1)
    advance(first)

    kept_inlet = struct((features // 2, wkv), bf16)
    grads = after(*grads)
    inlet_keep, inlet_send = call(
        functools.partial(weight_kernel, reach, half, steps),
        "weights",
        table,
        xs + [(scalar, bounds), *grads],
        [kept_inlet, kept_inlet],
        [vmem((features, slots * width), bf16), vmem((features, width), f32)],
        mib=8,
    )
    token[:] = [inlet_keep]
    inlet_in = flipped(inlet_send, "dp", 1)
    while first[0].order:
        advance(first)
    advance(first)
    (expand_in,) = after(expand_in)
    from_right, from_left, expand_in = together(from_right, from_left, expand_in)
    second = scatters(expand_keep, expand_in, owned)
    launch(second)
    for d in range(reach - 1, 0, -1):
        from_right, from_left = after(from_right, from_left)
        to_left = added(parts[reach - d], from_right)
        to_right = added(parts[reach + d - 1], from_left)
        token[:] = [to_left, to_right]
        from_right, from_left = moved(to_left, "blk", -1), moved(to_right, "blk", 1)
    advance(second)
    from_right, from_left = after(from_right, from_left)
    grad_normed, small = call(
        leave_kernel,
        "leave",
        table,
        [
            raw,
            mean_row,
            inverse_row,
            vectors,
            grad_middle,
            own_part,
            from_left,
            from_right,
            ffn_rows,
            *attend_rows,
        ],
        [struct(tokens, f32), struct((16, features), f32)],
        mib=8,
    )
    token[:] = [small]
    rounds = SmallSum(small, paired=False)
    (inlet_in,) = after(inlet_in)
    third = scatters(inlet_keep, inlet_in, owned)
    launch(third)
    line_one = begin(first)
    rounds.send()
    while second[0].order:
        advance(second)
    advance(second)
    line_two = begin(second)
    next_round()
    follow(line_one, Line.exchange)
    advance(third)
    follow(line_two, Line.exchange)
    next_round()
    follow(line_one, Line.gather)
    while third[0].order:
        advance(third)
    advance(third)
    line_three = begin(third)
    while rounds.left():
        next_round()
    (line_two.arrived, line_three.arrived) = after(line_two.arrived, line_three.arrived)
    line_three.exchange()
    line_two.gather()
    *rounds.arrived, line_three.keep = together(*rounds.arrived, line_three.keep)
    rounds.take()
    small = rounds.block
    line_one.arrived, line_three.keep = together(line_one.arrived, line_three.keep)
    shrink_share = line_one.result()
    line_three.gather()
    expand_share = line_two.result()
    inlet_share = line_three.result()

    band_mean = totals[0] / total_tokens
    band_variance = totals[1] / total_tokens - band_mean * band_mean
    inverse = lax.rsqrt(band_variance + stat_epsilon)
    back_totals = small[12:14]
    grad_variance = -0.5 * back_totals[1] * inverse * inverse * inverse
    grad_centre = -inverse * back_totals[0] - 2.0 * band_mean * grad_variance
    input_gradient = (
        grad_normed * inverse
        + grad_centre / total_tokens
        + 2.0 * grad_variance * raw / total_tokens
    ).reshape(sequences, block_length, features)
    vector_share = lax.dynamic_slice(
        small[:12], (0, column_start), (12, column_count), allow_negative_indices=False
    )

    updates = []
    for master, moment, square, share in (
        (inlet_master, inlet_moment, inlet_square, inlet_share),
        (outlet_master, outlet_moment, outlet_square, expand_share[:, inner:]),
        (expand_master, expand_moment, expand_square, expand_share[:, :inner]),
        (shrink_master, shrink_moment, shrink_square, shrink_share),
    ):
        updates.extend(
            adam_rule(
                master, moment, square, share.astype(f32), step_value, rate_matrix, decay_matrix
            )
        )
    updates.extend(
        adam_rule(
            vector_master, vector_moment, vector_square, vector_share, step_value, rate_vector, 0.0
        )
    )
    layer_output = layer_output.reshape(sequences, block_length, features)
    return (layer_output, input_gradient, band_mean, band_variance, *updates)


def solution(mesh):
    tokens = P("dp", "blk", None)
    rows = P("dp", None)
    columns = P(None, "dp")
    matrix = (P(), rows, rows, rows)
    return jax.shard_map(
        per_device,
        mesh=mesh,
        in_specs=(tokens, tokens, P("dp", "blk"), P())
        + matrix * 4
        + (P(), columns, columns, columns),
        out_specs=(tokens, tokens, P(), P()) + (rows,) * 16 + (columns,) * 4,
        check_vma=False,
    )
```

```python
import functools

import jax
import jax.numpy as jnp
from jax import lax
from jax.experimental import pallas as pl
from jax.experimental.pallas import tpu as pltpu
from jax.sharding import PartitionSpec as P

HEADS = 12
HEAD_WIDTH = 64
GROUP = 4

ln_epsilon = 1e-05
stat_epsilon = 1e-06
beta_one = 0.5
beta_two = 0.6
rate_matrix = 0.04
rate_vector = 0.8
warmup_length = 20.0
decay_matrix = 0.05
adam_epsilon = 1e-08
score_scale = 0.125
masked_score = -1e30

f32 = jnp.float32
bf16 = jnp.bfloat16


def nn(a, b):
    return lax.dot_general(a, b, (((1,), (0,)), ((), ())), preferred_element_type=f32)


def nt(a, b):
    return lax.dot_general(a, b, (((1,), (1,)), ((), ())), preferred_element_type=f32)


def tn(a, b):
    return lax.dot_general(a, b, (((0,), (0,)), ((), ())), preferred_element_type=f32)


def flipped(block, axis, bit):
    size = lax.axis_size(axis)
    return lax.ppermute(block, axis, [(i, i ^ bit) for i in range(size)])


def moved(block, axis, distance):
    size = lax.axis_size(axis)
    route = [(i, i + distance) for i in range(size) if 0 <= i + distance < size]
    return lax.ppermute(block, axis, route)


def bits_of(axis):
    size = lax.axis_size(axis)
    return [1 << i for i in range(size.bit_length() - 1)]


class SmallSum:
    def __init__(self, block, paired=True):
        self.block, self.rounds = block, []
        if not paired:
            self.rounds = [(axis, [bit]) for axis in ("blk", "dp") for bit in bits_of(axis)]
            return
        for axis in ("dp", "blk"):
            bits = bits_of(axis)
            odd = len(bits) % 2
            parts = [bits[:odd]] * odd + [bits[i : i + 2] for i in range(odd, len(bits), 2)]
            self.rounds += [(axis, part) for part in parts]

    def left(self):
        return len(self.rounds)

    def send(self):
        axis, part = self.rounds.pop(0)
        ways = part if len(part) == 1 else [part[0], part[1], part[0] | part[1]]
        self.arrived = [flipped(self.block, axis, way) for way in ways]

    def take(self, tie=lambda *values: values):
        others = tie(*self.arrived)
        if len(others) == 1:
            self.block = self.block + others[0]
        else:
            self.block = (self.block + others[0]) + (others[1] + others[2])


def added(kept, arrived):
    return (kept.astype(f32) + arrived.astype(f32)).astype(bf16)


def summed(addends):
    total = addends[0].astype(f32)
    for addend in addends[1:]:
        total = total + addend.astype(f32)
    return total.astype(bf16)


class Scatter:
    def __init__(self, addends, order):
        self.addends, self.order = list(addends), list(order)

    def prepare(self):
        self.sent = summed([addend[1] for addend in self.addends])

    def send(self):
        self.arrived = flipped(self.sent, "dp", self.order.pop(0))

    def take(self):
        self.addends = [addend[0] for addend in self.addends] + [self.arrived]


class Line:
    def __init__(self, first, second, lows):
        self.bits, self.lows = bits_of("blk"), lows
        first, second = summed(first.addends), summed(second.addends)
        self.keep = jnp.where(lows[0], first, second)
        self.sent = jnp.where(lows[0], second, first)

    def scatter(self):
        self.arrived = flipped(self.sent, "blk", 1)

    def exchange(self):
        share = added(self.keep, self.arrived)
        for bit, low in zip(self.bits[1:-1], self.lows[1:]):
            middle = share.shape[0] // 2
            keep = jnp.where(low, share[:middle], share[middle:])
            sent = jnp.where(low, share[middle:], share[:middle])
            share = added(keep, flipped(sent, "blk", bit))
        self.keep = share
        self.arrived = flipped(share, "blk", self.bits[-1])

    def joined(self, low):
        mine, other = self.keep, self.arrived
        return jnp.concatenate(
            [jnp.where(low, mine, other), jnp.where(low, other, mine)], axis=0
        )

    def gather(self):
        share = added(self.keep, self.arrived)
        for bit, low in reversed(list(zip(self.bits[1:-1], self.lows[1:]))):
            self.keep, self.arrived = share, flipped(share, "blk", bit)
            share = self.joined(low)
        self.keep = share
        self.arrived = flipped(share, "blk", 1)

    def result(self):
        return self.joined(self.lows[0])


def together(*values):
    return lax.optimization_barrier(values)


def whole(shape):
    return pl.BlockSpec(shape, lambda *a: (0,) * len(shape))


def call(kernel, name, table, operands, outs, scratch=(), mib=8):
    scalar = pl.BlockSpec(memory_space=pltpu.SMEM)
    return pl.pallas_call(
        kernel,
        grid_spec=pltpu.PrefetchScalarGridSpec(
            num_scalar_prefetch=1,
            grid=(1,),
            in_specs=[
                spec if isinstance(spec, pl.BlockSpec) else whole(spec.shape)
                for spec in (o[0] if isinstance(o, tuple) else o for o in operands)
            ],
            out_specs=[scalar if o.shape == (2,) else whole(o.shape) for o in outs],
            scratch_shapes=list(scratch),
        ),
        out_shape=outs,
        cost_estimate=pl.CostEstimate(flops=1 << 20, bytes_accessed=1 << 16, transcendentals=0),
        compiler_params=pltpu.CompilerParams(vmem_limit_bytes=mib << 20),
        name=name,
    )(table, *[o[1] if isinstance(o, tuple) else o for o in operands])


def struct(shape, dtype):
    return jax.ShapeDtypeStruct(shape, dtype)


def unit_rows(rows):
    centred = rows - jnp.mean(rows, axis=-1, keepdims=True)
    scale = lax.rsqrt(jnp.mean(centred * centred, axis=-1, keepdims=True) + ln_epsilon)
    return centred * scale, scale


def norm_back(grad, unit, scale, gain):
    inner = grad * gain
    return scale * (
        inner
        - jnp.mean(inner, axis=-1, keepdims=True)
        - unit * jnp.mean(inner * unit, axis=-1, keepdims=True)
    )


def column_sum(rows):
    return jnp.sum(rows, axis=0, keepdims=True)


def totals_kernel(table, raw_ref, out_ref):
    raw = raw_ref[...]
    out_ref[0:1, :] = column_sum(raw)
    out_ref[1:2, :] = column_sum(raw * raw)


def enter_kernel(total_tokens, table, raw_ref, sum_ref, vec_ref, id_ref, x_ref, mean_ref, std_ref):
    width = raw_ref.shape[0]
    mean = sum_ref[0:1, :] / total_tokens
    variance = sum_ref[1:2, :] / total_tokens - mean * mean
    inverse = lax.rsqrt(variance + stat_epsilon)
    mean_ref[...] = mean
    std_ref[...] = inverse
    unit, _ = unit_rows((raw_ref[...] - mean) * inverse)
    x_ref[0:width, :] = (unit * vec_ref[0:1, :] + vec_ref[1:2, :]).astype(bf16)
    x_ref[width:, :] = jnp.zeros((x_ref.shape[0] - width, x_ref.shape[1]), bf16)
    ids = jnp.broadcast_to(id_ref[...], (16, width)).astype(f32).astype(bf16)
    x_ref[width:, 0:width] = ids


def id_columns(ids, width):
    return jnp.broadcast_to(ids, (128, width)).T


def id_row(rows):
    return rows.astype(f32)[0:1]


def project_own_kernel(table, x_ref, w_ref, vec_ref, q_ref, kv_ref, id_ref):
    width = q_ref.shape[0]
    features = q_ref.shape[1]
    slot = kv_ref.shape[0] // 2
    x = x_ref[0:width, :]
    q_ref[...] = ((nn(x, w_ref[:, :features]) + vec_ref[4:5, :]) * score_scale).astype(bf16)
    kv_ref[slot, :, :features] = nn(x, w_ref[:, features : 2 * features]).astype(bf16)
    kv_ref[slot, :, features:] = (nn(x, w_ref[:, 2 * features :]) + vec_ref[5:6, :]).astype(bf16)
    id_ref[slot] = id_columns(id_row(x_ref[width : width + 8, 0:width]), width)


def project_pair_kernel(
    d, inside_at, table, xa_ref, xb_ref, x_ref, w_ref, vec_ref, kv_in, id_in, kv_ref, id_ref, both
):
    width = kv_ref.shape[1]
    features = kv_ref.shape[2] // 2
    reach = kv_ref.shape[0] // 2
    done = slice(reach - d + 1, reach + d)
    kv_ref[done] = kv_in[done]
    id_ref[done] = id_in[done]
    both[0], both[1] = xa_ref[...], xb_ref[...]
    own = id_row(x_ref[width : width + 8, 0:width])
    low, high = jnp.min(own), jnp.max(own)

    def one(i, carry):
        slot = reach - d + 2 * d * i
        ids = id_row(both[i, width : width + 8, 0:width])
        near = (table[inside_at + i] > 0) & (jnp.max(ids) >= low) & (jnp.min(ids) <= high)
        id_ref[slot] = jnp.full((width, 128), -1.0, f32)

        @pl.when(near)
        def _():
            x = both[i, 0:width, :]
            kv_ref[slot, :, :features] = nn(x, w_ref[:, features : 2 * features]).astype(bf16)
            kv_ref[slot, :, features:] = (
                nn(x, w_ref[:, 2 * features :]) + vec_ref[5:6, :]
            ).astype(bf16)
            id_ref[slot] = id_columns(ids, width)

        return carry

    lax.fori_loop(0, 2, one, 0)


def lane_half(rows, which):
    lanes = lax.broadcasted_iota(jnp.int32, (rows, 128), 1)
    return (lanes >= 64) if which else (lanes < 64)


def mask_rows(own_row, width):
    ids = lax.broadcasted_iota(jnp.int32, (64, width), 0).astype(f32)
    return jnp.where(ids == own_row, 0.0, masked_score).astype(bf16)


def key_marks(column, width):
    lane_ids = (lax.broadcasted_iota(jnp.int32, (width, 128), 1) % 64).astype(f32)
    return (column == lane_ids).astype(f32).astype(bf16)


def lane_group(g):
    return pl.ds(pl.multiple_of(g * GROUP * HEAD_WIDTH, 128), GROUP * HEAD_WIDTH)


def attend_kernel(reach, table, q_ref, kv_ref, qid_ref, kid_ref, o_ref, lse_ref, bound_ref, acc, top, qm, sc):
    width, features = q_ref.shape
    slots = kv_ref.shape[0]
    steps = features // (GROUP * HEAD_WIDTH)
    low = kid_ref[reach, 0:1, :]
    high = kid_ref[reach, width - 1 : width, :]
    start = jnp.full_like(low, float(reach))
    end = jnp.full_like(low, float(reach))
    for s in range(slots):
        active = (kid_ref[s, width - 1 : width, :] >= low) & (kid_ref[s, 0:1, :] <= high)
        start = jnp.where(active, jnp.minimum(start, float(s)), start)
        end = jnp.where(active, jnp.maximum(end, float(s)), end)
    bound_ref[0] = jnp.min(start).astype(jnp.int32)
    bound_ref[1] = jnp.max(end).astype(jnp.int32) + 1
    barred = mask_rows(qid_ref[...].astype(f32), width)
    upper = lane_half(width, 1)
    one_rows = (lax.broadcasted_iota(jnp.int32, (16, width), 0) == 0).astype(f32).astype(bf16)

    def group(g, carry):
        lanes_g = lane_group(g)
        lanes_v = pl.ds(pl.multiple_of(features + g * GROUP * HEAD_WIDTH, 128), GROUP * HEAD_WIDTH)
        top[...] = jnp.full_like(top, masked_score)
        acc[...] = jnp.zeros_like(acc)
        q_t = q_ref[:, lanes_g].T
        for h in range(GROUP):
            head = q_t[64 * h : 64 * h + 64, :]
            qm[h, 0:64, :] = barred if h % 2 else head
            qm[h, 64:128, :] = head if h % 2 else barred

        def step(s, carry):
            keys = kv_ref[s, :, lanes_g]
            values_t = kv_ref[s, :, lanes_v].T
            marks = key_marks(kid_ref[s], width)
            for h in range(GROUP):
                lanes = slice(128 * (h // 2), 128 * (h // 2) + 128)
                pair = keys[:, lanes]
                marked = jnp.where(upper, pair, marks) if h % 2 else jnp.where(upper, marks, pair)
                sc[h] = nn(marked, qm[h])
            for h in range(GROUP):
                score = sc[h]
                old = top[h : h + 1, :]
                new = jnp.maximum(old, jnp.max(score, axis=0, keepdims=True))
                fade = jnp.exp(old - new)
                weight = jnp.exp(score - new).astype(bf16)
                top[h : h + 1, :] = new
                rows = slice(80 * h, 80 * h + 80)
                left = jnp.concatenate([values_t[64 * h : 64 * h + 64, :], one_rows], axis=0)
                acc[rows, :] = acc[rows, :] * fade + nn(left, weight)
            return carry

        lax.fori_loop(bound_ref[0], bound_ref[1], step, 0)
        outs, lses = [], []
        for h in range(GROUP):
            total = acc[80 * h + 64 : 80 * h + 65, :]
            outs.append(acc[80 * h : 80 * h + 64, :] / total)
            lses.append(top[h : h + 1, :] + jnp.log(total))
        o_ref[:, lanes_g] = jnp.concatenate(outs, axis=0).T.astype(bf16)
        lse_ref[g] = jnp.concatenate(lses, axis=0)
        return carry

    lax.fori_loop(0, steps, group, 0)


def spread_rows(table, plain, target, lanes, half):
    part = plain.shape[0] // (4 * half)
    for side in range(2):
        for h in range(2):
            for p in range(half):
                owner = table[half * (1 + 2 * h + side) + p]
                place = pl.multiple_of((2 * owner + h) * part, 8)
                to = ((side * 2 + h) * half + p) * part
                target[to : to + part, lanes] = plain[pl.ds(place, part), :].astype(bf16)


def ffn_kernel(
    half,
    table,
    o_ref,
    wo_ref,
    raw_ref,
    mean_ref,
    std_ref,
    vec_ref,
    cot_ref,
    w1_ref,
    w2_ref,
    out_ref,
    gm_ref,
    ga_ref,
    sk_ref,
    ss_ref,
    ek_ref,
    es_ref,
    row_ref,
    middle_s,
    gsec,
    s2,
    s2t,
    ot,
    plain,
    rows_s,
    acc,
):
    features = gm_ref.shape[1]
    inner = w1_ref.shape[1]
    chunk = inner // half
    wide = chunk // 2
    normed = (raw_ref[...] - mean_ref[...]) * std_ref[...]
    middle = normed + nn(o_ref[...], wo_ref[...]) + vec_ref[6:7, :]
    middle_s[...] = middle
    unit, _ = unit_rows(middle)
    second = unit * vec_ref[2:3, :] + vec_ref[3:4, :]
    s2[...] = second.astype(bf16)
    plain[...] = second.T
    spread_rows(table, plain, s2t, slice(None), half)
    plain[...] = o_ref[...].T.astype(f32)
    spread_rows(table, plain, ot, slice(None), half)
    acc[...] = jnp.zeros_like(acc)
    gsec[...] = jnp.zeros_like(gsec)
    own = table[half] % 2

    def step(i, carry):
        place = table[i] * chunk
        lanes = pl.ds(pl.multiple_of(place, 128), chunk)
        row = pl.ds(8 + place // features, 1)
        row_lanes = pl.ds(pl.multiple_of(place % features, 128), chunk)
        w1 = w1_ref[:, lanes]
        w2 = w2_ref[lanes, :]
        pre = nn(s2[...], w1) + vec_ref[row, row_lanes]
        back = nt(cot_ref[...], w2)
        area = 0.5 * (1.0 + lax.erf(pre * (0.5**0.5)))
        bell = jnp.exp(-0.5 * pre * pre) * (1.0 / (2.0 * jnp.pi) ** 0.5)
        hidden = (pre * area).astype(bf16)
        grad = ((area + pre * bell) * back).astype(bf16)
        acc[...] += nn(hidden, w2)
        gsec[...] += nt(grad, w1)
        row_ref[row, row_lanes] = column_sum(grad.astype(f32))
        rows_s[...] = nn(hidden.T, cot_ref[...]).astype(bf16)
        for side, ref in ((0, sk_ref), (1, ss_ref)):
            first = jnp.where(own == side, 0, wide)
            for h, at in ((0, i), (1, table[5 * half + i])):
                start = pl.multiple_of(first + h * (wide // 2), 16)
                ref[h, at] = rows_s[pl.ds(start, wide // 2), :]
        ek_ref[:, lanes] = nn(s2t[: features // 2, :], grad).astype(bf16)
        es_ref[:, lanes] = nn(s2t[features // 2 :, :], grad).astype(bf16)
        return carry

    lax.fori_loop(0, half, step, 0, unroll=True)
    out_ref[...] = (middle_s[...] + acc[...] + vec_ref[7:8, :]).astype(bf16)
    unit, scale = unit_rows(middle_s[...])
    grad = gsec[...]
    cot = cot_ref[...].astype(f32)
    row_ref[0:1, :] = column_sum(grad * unit)
    row_ref[1:2, :] = column_sum(grad)
    grad_middle = cot + norm_back(grad, unit, scale, vec_ref[2:3, :])
    gm_ref[...] = grad_middle
    branch = grad_middle.astype(bf16)
    row_ref[2:3, :] = column_sum(branch.astype(f32))
    row_ref[3:4, :] = column_sum(cot)
    ga_ref[...] = nt(branch, wo_ref[...]).astype(bf16)
    ek_ref[:, inner:] = nn(ot[: features // 2, :], branch).astype(bf16)
    es_ref[:, inner:] = nn(ot[features // 2 :, :], branch).astype(bf16)


def attend_back_kernel(
    g,
    bounds,
    q_ref,
    kv_ref,
    o_ref,
    g_ref,
    lse_ref,
    qid_ref,
    kid_ref,
    dq_ref,
    dk_ref,
    dv_ref,
    row_ref,
    acc,
    qm,
    gm,
    q_stack,
    g_stack,
    sc,
    dp,
    p_wide,
    g_wide,
    rows_s,
):
    width, features = q_ref.shape
    slots = kv_ref.shape[0]
    barred = mask_rows(qid_ref[...].astype(f32), width)
    nothing = jnp.zeros((64, width), bf16)
    upper = lane_half(width, 1)

    def blank(s, carry):
        dk_ref[s] = jnp.zeros(dk_ref.shape[1:], dk_ref.dtype)
        dv_ref[s] = jnp.zeros(dv_ref.shape[1:], dv_ref.dtype)
        return carry

    lax.fori_loop(0, bounds[0], blank, 0)
    lax.fori_loop(bounds[1], slots, blank, 0)

    base = g * GROUP * HEAD_WIDTH
    lanes_g = slice(base, base + GROUP * HEAD_WIDTH)
    lanes_v = slice(features + base, features + base + GROUP * HEAD_WIDTH)
    acc[...] = jnp.zeros_like(acc)
    q_all, g_all = q_ref[:, lanes_g], g_ref[:, lanes_g]
    product = (g_all.astype(f32) * o_ref[:, lanes_g].astype(f32)).T
    q_t, g_t = q_all.T, g_all.T
    for h in range(GROUP):
        lanes = slice(128 * (h // 2), 128 * (h // 2) + 128)
        rows = slice(64 * h, 64 * h + 64)
        odd = h % 2
        qm[h, 0:64, :] = barred if odd else q_t[rows, :]
        qm[h, 64:128, :] = q_t[rows, :] if odd else barred
        gm[h, 0:64, :] = nothing if odd else g_t[rows, :]
        gm[h, 64:128, :] = g_t[rows, :] if odd else nothing
        half = lane_half(width, odd)
        place = slice(width * odd, width * odd + width)
        pair = q_all[:, lanes]
        q_stack[h // 2, place, :] = jnp.where(half, pair, jnp.zeros_like(pair))
        pair = g_all[:, lanes]
        g_stack[h // 2, place, :] = jnp.where(half, pair, jnp.zeros_like(pair))
        rows_s[h : h + 1, :] = column_sum(product[rows, :])
    rows_s[8:9, :] = jnp.zeros((1, GROUP * HEAD_WIDTH), f32)

    def step(s, carry):
        keys = kv_ref[s, :, lanes_g]
        values = kv_ref[s, :, lanes_v]
        keys_t = keys.T
        marks = key_marks(kid_ref[s], width)
        for h in range(GROUP):
            lanes = slice(128 * (h // 2), 128 * (h // 2) + 128)
            pair = keys[:, lanes]
            marked = jnp.where(upper, pair, marks) if h % 2 else jnp.where(upper, marks, pair)
            sc[h] = nn(marked, qm[h])
            dp[h] = nn(values[:, lanes], gm[h])
        for h in range(GROUP):
            place = slice(width * (h % 2), width * (h % 2) + width)
            prob = jnp.exp(sc[h] - lse_ref[g, h : h + 1, :])
            p_wide[h // 2, :, place] = prob.astype(bf16)
            g_wide[h // 2, :, place] = (prob * (dp[h] - rows_s[h : h + 1, :])).astype(bf16)
        for h in range(GROUP):
            place = slice(width * (h % 2), width * (h % 2) + width)
            rows = slice(64 * h, 64 * h + 64)
            acc[rows, :] += nn(keys_t[rows, :], g_wide[h // 2, :, place])
        key_parts, value_parts = [], []
        for j in range(GROUP // 2):
            value_parts.append(nn(p_wide[j], g_stack[j]))
            key_parts.append(nn(g_wide[j], q_stack[j]))
        value_all = jnp.concatenate(value_parts, axis=1)
        dk_ref[s] = jnp.concatenate(key_parts, axis=1).astype(bf16)
        dv_ref[s] = value_all.astype(bf16)
        rows_s[8:9, :] += column_sum(value_all)
        return carry

    lax.fori_loop(bounds[0], bounds[1], step, 0)
    dq = (acc[...].T.astype(bf16).astype(f32) * score_scale).astype(bf16)
    dq_ref[...] = dq
    row_ref[0:1, :] = column_sum(dq.astype(f32))
    row_ref[1:2, :] = rows_s[8:9, :]


def parts_kernel(reach, bounds, *refs):
    groups = (len(refs) - 3) // 3
    dqs, dks, dvs = (refs[k * groups : (k + 1) * groups] for k in range(3))
    w_ref, p_ref, own_ref = refs[3 * groups :]
    features = p_ref.shape[2]
    size = features // groups

    def part(s):
        total = None
        for g in range(groups):
            for ref, base in ((dks[g], features), (dvs[g], 2 * features)):
                now = nt(ref[s], w_ref[:, base + g * size : base + (g + 1) * size])
                total = now if total is None else total + now
        return total

    def one(s, to):
        active = (s >= bounds[0]) & (s < bounds[1])

        @pl.when(active)
        def _():
            p_ref[to] = part(s).astype(bf16)

        @pl.when(jnp.logical_not(active))
        def _():
            p_ref[to] = jnp.zeros(p_ref.shape[1:], p_ref.dtype)

    def some(i, carry):
        one(jnp.where(i < reach, i, i + 1), i)
        return carry

    lax.fori_loop(0, 2 * reach, some, 0)
    total = part(reach)
    for g in range(groups):
        total = total + nt(dqs[g][...], w_ref[:, g * size : (g + 1) * size])
    own_ref[...] = total


def weight_kernel(reach, half, groups, table, *refs):
    slots = 2 * reach + 1
    xs, bounds = refs[:slots], refs[slots]
    refs = refs[slots + 1 :]
    dqs, dks, dvs = (refs[k * groups : (k + 1) * groups] for k in range(3))
    keep_ref, send_ref, xt, plain = refs[-4:]
    width, size = dqs[0].shape
    features = size * groups
    few = min(3, slots)
    small = bounds[1] - bounds[0] <= few
    start = jnp.minimum(bounds[0], slots - few)

    for s in range(slots):

        @pl.when(jnp.logical_not(small) | ((s >= start) & (s < start + few)))
        def _(s=s):
            plain[...] = xs[s][0:width, :].T.astype(f32)
            spread_rows(table, plain, xt, slice(width * s, width * s + width), half)

    def put(tokens, right, base):
        lanes = slice(base, base + size)
        keep_ref[:, lanes] = nn(xt[: features // 2, tokens], right).astype(bf16)
        send_ref[:, lanes] = nn(xt[features // 2 :, tokens], right).astype(bf16)

    for g in range(groups):
        put(slice(width * reach, width * reach + width), dqs[g][...], g * size)

    def over(start, count):
        tokens = pl.ds(pl.multiple_of(start * width, 128), count * width)
        for base, group in ((features, dks), (2 * features, dvs)):
            for g in range(groups):
                rows = group[g][pl.ds(start, count)].reshape(count * width, size)
                put(tokens, rows, base + g * size)

    @pl.when(small)
    def _():
        over(start, few)

    @pl.when(jnp.logical_not(small))
    def _():
        over(0, slots)


def leave_kernel(
    table,
    raw_ref,
    mean_ref,
    std_ref,
    vec_ref,
    gm_ref,
    own_ref,
    left_ref,
    right_ref,
    ffn_rows,
    *refs,
):
    attend_rows, (gn_ref, row_ref) = refs[:-2], refs[-2:]
    features = raw_ref.shape[1]
    centred = raw_ref[...] - mean_ref[...]
    unit, scale = unit_rows(centred * std_ref[...])
    grad = own_ref[...] + left_ref[...].astype(f32) + right_ref[...].astype(f32)
    row_ref[0:1, :] = column_sum(grad * unit)
    row_ref[1:2, :] = column_sum(grad)
    row_ref[2:4, :] = ffn_rows[0:2, :]
    size = features // len(attend_rows)
    for g, ref in enumerate(attend_rows):
        row_ref[4:6, g * size : (g + 1) * size] = ref[...]
    row_ref[6:8, :] = ffn_rows[2:4, :]
    row_ref[8:12, :] = ffn_rows[8:12, :]
    whole_grad = gm_ref[...] + norm_back(grad, unit, scale, vec_ref[0:1, :])
    gn_ref[...] = whole_grad
    row_ref[12:13, :] = column_sum(whole_grad)
    row_ref[13:14, :] = column_sum(whole_grad * centred)
    row_ref[14:16, :] = jnp.zeros((2, features), f32)


def adam_rule(master, moment, square, gradient, step_value, step_rate, weight_decay):
    moment_new = beta_one * moment + (1.0 - beta_one) * gradient
    square_new = beta_two * square + (1.0 - beta_two) * gradient * gradient
    fix_first = 1.0 - jnp.power(beta_one, step_value)
    fix_second = 1.0 - jnp.power(beta_two, step_value)
    planned = step_rate * jnp.minimum(1.0, step_value / warmup_length)
    direction = moment_new / fix_first / (jnp.sqrt(square_new / fix_second) + adam_epsilon)
    weight_new = master - planned * (direction + weight_decay * master)
    return (weight_new, moment_new, square_new, weight_new.astype(bf16))


def per_device(
    raw_input,
    cotangent,
    segment_ids,
    step_count,
    inlet_copy,
    inlet_master,
    inlet_moment,
    inlet_square,
    outlet_copy,
    outlet_master,
    outlet_moment,
    outlet_square,
    expand_copy,
    expand_master,
    expand_moment,
    expand_square,
    shrink_copy,
    shrink_master,
    shrink_moment,
    shrink_square,
    vector_copy,
    vector_master,
    vector_moment,
    vector_square,
):
    sequences, block_length, features = raw_input.shape
    assert sequences == 1
    width = block_length
    group_size = lax.axis_size("blk")
    group_index = lax.axis_index("blk")
    owners = lax.axis_size("dp")
    owner = lax.axis_index("dp")
    half = owners // 2
    total_tokens = owners * group_size * block_length
    reach = group_size // 2
    slots = 2 * reach + 1
    inner = expand_copy.shape[1]
    chunk = inner // half
    vectors = vector_copy.astype(f32)
    raw = raw_input.reshape(width, features)
    cot = cotangent.reshape(width, features)
    own_ids = segment_ids
    count = owners.bit_length() - 1
    scalar = pl.BlockSpec(memory_space=pltpu.SMEM)
    vmem = pltpu.VMEM

    def reversed_bits(value):
        return int(format(value, f"0{count - 1}b")[::-1], 2) if count > 1 else 0

    straight = [reversed_bits(p) for p in range(half)]
    other_way = list(range(half))
    relative = jnp.array(
        [2 * v for v in straight]
        + [2 * v for v in straight]
        + [2 * v + 1 for v in straight]
        + [2 * v for v in other_way]
        + [2 * v + 1 for v in other_way],
        jnp.int32,
    ) ^ owner
    inside = [group_index >= d for d in range(1, reach + 1)]
    inside += [group_index + d < group_size for d in range(1, reach + 1)]
    table = jnp.concatenate(
        [
            relative[:half] // 2,
            relative[half:],
            jnp.array(straight, jnp.int32),
            jnp.stack([flag for pair in zip(inside[:reach], inside[reach:]) for flag in pair]).astype(jnp.int32),
        ]
    )
    lows = [(group_index // bit) % 2 == 0 for bit in bits_of("blk")]
    column_count = vector_master.shape[1]
    column_start = owner * column_count
    step_value = step_count[0].astype(f32)

    tokens, row = (width, features), (1, features)
    wkv = 3 * features
    lanes = GROUP * HEAD_WIDTH
    steps = features // lanes

    (totals,) = call(
        totals_kernel, "totals", jnp.zeros((1,), jnp.int32), [raw], [struct((2, features), f32)], mib=2
    )
    rounds = SmallSum(totals)
    rounds.send()
    rounds.take()
    rounds.send()
    tied = together(*rounds.arrived, table, column_start, vectors, *lows)
    ways = len(rounds.arrived)
    rounds.arrived = list(tied[:ways])
    table, column_start, vectors = tied[ways : ways + 3]
    lows = list(tied[ways + 3 :])
    rounds.take()
    while rounds.left():
        rounds.send()
        rounds.take()
    totals = rounds.block
    packed = width + 16
    x, mean_row, inverse_row = call(
        functools.partial(enter_kernel, total_tokens),
        "enter",
        table,
        [raw, totals, vectors, own_ids],
        [struct((packed, features), bf16), struct(row, f32), struct(row, f32)],
        mib=6,
    )

    xs = [None] * slots
    xs[reach] = x
    ahead, behind = moved(x, "blk", 1), moved(x, "blk", -1)
    queries, pairs, columns = call(
        project_own_kernel,
        "project_own",
        table,
        [x, inlet_copy, vectors],
        [
            struct(tokens, bf16),
            struct((slots, width, 2 * features), bf16),
            struct((slots, width, 128), f32),
        ],
        mib=6,
    )
    ahead, behind, queries = together(ahead, behind, queries)
    for d in range(1, reach + 1):
        if d > 1:
            ahead, behind = moved(ahead, "blk", 1), moved(behind, "blk", -1)
            ahead, behind, pairs = together(ahead, behind, pairs)
        xs[reach - d], xs[reach + d] = ahead, behind
        pairs, columns = call(
            functools.partial(project_pair_kernel, d, 6 * half + 2 * (d - 1)),
            "project_pair",
            table,
            [ahead, behind, x, inlet_copy, vectors, pairs, columns],
            [struct(pairs.shape, bf16), struct(columns.shape, f32)],
            [vmem((2, packed, features), bf16)],
            mib=6,
        )

    attended, lse, bounds = call(
        functools.partial(attend_kernel, reach),
        "attend",
        table,
        [queries, pairs, own_ids, columns],
        [struct(tokens, bf16), struct((steps, GROUP, width), f32), struct((2,), jnp.int32)],
        [
            vmem((80 * GROUP, width), f32),
            vmem((8, width), f32),
            vmem((GROUP, 128, width), bf16),
            vmem((GROUP, width, width), f32),
        ],
        mib=6,
    )

    owned_wide, owned = inner // owners, features // owners
    kept_shrink = struct((2, half, owned_wide // 2, features), bf16)
    kept_expand = struct((features // 2, inner + features), bf16)
    layer_output, grad_middle, grad_attended, shrink_keep, shrink_send, expand_keep, expand_send, ffn_rows = call(
        functools.partial(ffn_kernel, half),
        "ffn",
        table,
        [attended, outlet_copy, raw, mean_row, inverse_row, vectors, cot, expand_copy, shrink_copy],
        [
            struct(tokens, bf16),
            struct(tokens, f32),
            struct(tokens, bf16),
            kept_shrink,
            kept_shrink,
            kept_expand,
            kept_expand,
            struct((12, features), f32),
        ],
        [
            vmem(tokens, f32),
            vmem(tokens, f32),
            vmem(tokens, bf16),
            vmem((features, width), bf16),
            vmem((features, width), bf16),
            vmem((features, width), f32),
            vmem((chunk, features), bf16),
            vmem(tokens, f32),
        ],
        mib=14,
    )
    bits = bits_of("dp")
    orders = (bits[1:], bits[:0:-1])

    def scatters(keep, arrived, rows):
        shape = (2,) + (2,) * (count - 1) + (rows // 2, keep.shape[-1])
        keep, arrived = keep.reshape(shape), arrived.reshape(shape)
        return [Scatter([keep[h], arrived[h]], orders[h]) for h in range(2)]

    token = [grad_attended]

    def after(*values):
        tied = together(*values, *token)[: len(values)]
        token[:] = tied
        return tied

    def launch(pair):
        for one in pair:
            one.prepare()
        token[:] = [one.sent for one in pair]
        for one in pair:
            one.send()

    def advance(pair):
        for one, value in zip(pair, after(*[one.arrived for one in pair])):
            one.arrived = value
            one.take()
        if pair[0].order:
            launch(pair)

    def follow(line, stage):
        (line.arrived,) = after(line.arrived)
        stage(line)
        token[:] = [line.keep]

    def begin(pair):
        line = Line(*pair, lows)
        token[:] = [line.sent]
        line.scatter()
        return line

    def next_round():
        rounds.take(after)
        token[:] = [rounds.block]
        if rounds.left():
            rounds.send()

    shrink_in = flipped(shrink_send, "dp", 1)
    expand_in = flipped(expand_send, "dp", 1)
    spread = struct((slots, width, lanes), bf16)
    back = []
    for g in range(steps):
        (grad_attended,) = after(grad_attended)
        back.append(
            call(
                functools.partial(attend_back_kernel, g),
                "attend_back",
                bounds,
                [queries, pairs, attended, grad_attended, lse, own_ids, columns],
                [struct((width, lanes), bf16), spread, spread, struct((2, lanes), f32)],
                [
                    vmem((lanes, width), f32),
                    vmem((GROUP, 128, width), bf16),
                    vmem((GROUP, 128, width), bf16),
                    vmem((GROUP // 2, 2 * width, 128), bf16),
                    vmem((GROUP // 2, 2 * width, 128), bf16),
                    vmem((GROUP, width, width), f32),
                    vmem((GROUP, width, width), f32),
                    vmem((GROUP // 2, width, 2 * width), bf16),
                    vmem((GROUP // 2, width, 2 * width), bf16),
                    vmem((16, width), f32),
                ],
                mib=8,
            )
        )
        token[:] = [back[-1][0]]
        if g == 0:
            (shrink_in,) = after(shrink_in)
            first = scatters(shrink_keep, shrink_in, owned_wide)
            launch(first)
    query_low, key_low, value_low, attend_rows = zip(*back)
    grads = [*query_low, *key_low, *value_low]
    (expand_in,) = after(expand_in)

    grads = after(*grads)
    parts, own_part = call(
        functools.partial(parts_kernel, reach),
        "parts",
        bounds,
        [*grads, inlet_copy],
        [struct((2 * reach, width, features), bf16), struct(tokens, f32)],
        mib=6,
    )
    to_left, to_right = parts[0], parts[2 * reach - 1]
    back_one = together(*[one.arrived for one in first], expand_in, to_left)
    for one, value in zip(first, back_one):
        one.arrived = value
        one.take()
    expand_in, to_left = back_one[-2:]
    second = scatters(expand_keep, expand_in, owned)
    for one in first + second:
        if one.order:
            one.prepare()

    kept_inlet = struct((features // 2, wkv), bf16)
    inlet_keep, inlet_send = call(
        functools.partial(weight_kernel, reach, half, steps),
        "weights",
        table,
        xs
        + [(scalar, bounds), *grads]
        + [(pl.BlockSpec(memory_space=pl.ANY), one.sent) for one in first + second if one.order],
        [kept_inlet, kept_inlet],
        [vmem((features, slots * width), bf16), vmem((features, width), f32)],
        mib=8,
    )
    for one in first + second:
        if one.order:
            one.send()
    inlet_in = flipped(inlet_send, "dp", 1)
    tied = together(*[one.arrived for one in second], inlet_keep)
    for one, value in zip(second, tied):
        one.arrived = value
        one.take()
    inlet_keep = tied[-1]
    if second[0].order:
        launch(second)
    while True:
        tied = together(
            *[one.arrived for one in first],
            to_left,
            to_right,
            *[one.addends[-1] for one in second],
        )
        for one, value in zip(first, tied):
            one.arrived = value
            one.take()
        to_left, to_right = tied[2:4]
        for one, value in zip(second, tied[4:]):
            one.addends[-1] = value
        if not first[0].order:
            break
        for one in first:
            one.prepare()
            one.send()
    from_right, from_left = moved(to_left, "blk", -1), moved(to_right, "blk", 1)
    token[:] = [inlet_keep]
    line_one = begin(first)
    while second[0].order:
        advance(second)
    from_right, from_left, inlet_in, *arrived = together(
        from_right, from_left, inlet_in, *[one.arrived for one in second]
    )
    for one, value in zip(second, arrived):
        one.arrived = value
        one.take()
    third = scatters(inlet_keep, inlet_in, owned)
    launch(third)
    for d in range(reach - 1, 0, -1):
        from_right, from_left = after(from_right, from_left)
        to_left = added(parts[reach - d], from_right)
        to_right = added(parts[reach + d - 1], from_left)
        token[:] = [to_left, to_right]
        from_right, from_left = moved(to_left, "blk", -1), moved(to_right, "blk", 1)
    line_two = begin(second)
    follow(line_one, Line.exchange)
    from_right, from_left = after(from_right, from_left)
    grad_normed, small = call(
        leave_kernel,
        "leave",
        table,
        [
            raw,
            mean_row,
            inverse_row,
            vectors,
            grad_middle,
            own_part,
            from_left,
            from_right,
            ffn_rows,
            *attend_rows,
        ],
        [struct(tokens, f32), struct((16, features), f32)],
        mib=8,
    )
    token[:] = [small]
    rounds = SmallSum(small, paired=False)
    rounds.send()
    advance(third)
    follow(line_two, Line.exchange)
    next_round()
    while third[0].order:
        advance(third)
    advance(third)
    line_three = begin(third)
    follow(line_one, Line.gather)
    while rounds.left():
        next_round()
    (line_two.arrived, line_three.arrived) = after(line_two.arrived, line_three.arrived)
    line_three.exchange()
    line_two.gather()
    *rounds.arrived, line_three.keep = together(*rounds.arrived, line_three.keep)
    rounds.take()
    small = rounds.block
    line_one.arrived, line_three.keep = together(line_one.arrived, line_three.keep)
    shrink_share = line_one.result()
    line_three.gather()
    expand_share = line_two.result()
    inlet_share = line_three.result()

    band_mean = totals[0] / total_tokens
    band_variance = totals[1] / total_tokens - band_mean * band_mean
    inverse = lax.rsqrt(band_variance + stat_epsilon)
    back_totals = small[12:14]
    grad_variance = -0.5 * back_totals[1] * inverse * inverse * inverse
    grad_centre = -inverse * back_totals[0] - 2.0 * band_mean * grad_variance
    input_gradient = (
        grad_normed * inverse
        + grad_centre / total_tokens
        + 2.0 * grad_variance * raw / total_tokens
    ).reshape(sequences, block_length, features)
    vector_share = lax.dynamic_slice(
        small[:12], (0, column_start), (12, column_count), allow_negative_indices=False
    )

    updates = []
    for master, moment, square, share in (
        (inlet_master, inlet_moment, inlet_square, inlet_share),
        (outlet_master, outlet_moment, outlet_square, expand_share[:, inner:]),
        (expand_master, expand_moment, expand_square, expand_share[:, :inner]),
        (shrink_master, shrink_moment, shrink_square, shrink_share),
    ):
        updates.extend(
            adam_rule(
                master, moment, square, share.astype(f32), step_value, rate_matrix, decay_matrix
            )
        )
    updates.extend(
        adam_rule(
            vector_master, vector_moment, vector_square, vector_share, step_value, rate_vector, 0.0
        )
    )
    layer_output = layer_output.reshape(sequences, block_length, features)
    return (layer_output, input_gradient, band_mean, band_variance, *updates)


def solution(mesh):
    tokens = P("dp", "blk", None)
    rows = P("dp", None)
    columns = P(None, "dp")
    matrix = (P(), rows, rows, rows)
    return jax.shard_map(
        per_device,
        mesh=mesh,
        in_specs=(tokens, tokens, P("dp", "blk"), P())
        + matrix * 4
        + (P(), columns, columns, columns),
        out_specs=(tokens, tokens, P(), P()) + (rows,) * 16 + (columns,) * 4,
        check_vma=False,
    )
```

```python
import functools

import jax
import jax.numpy as jnp
from jax import lax
from jax.experimental import pallas as pl
from jax.experimental.pallas import tpu as pltpu
from jax.sharding import PartitionSpec as P

HEADS = 12
HEAD_WIDTH = 64
GROUP = 4

ln_epsilon = 1e-05
stat_epsilon = 1e-06
beta_one = 0.5
beta_two = 0.6
rate_matrix = 0.04
rate_vector = 0.8
warmup_length = 20.0
decay_matrix = 0.05
adam_epsilon = 1e-08
score_scale = 0.125
masked_score = -1e30

f32 = jnp.float32
bf16 = jnp.bfloat16


def nn(a, b):
    return lax.dot_general(a, b, (((1,), (0,)), ((), ())), preferred_element_type=f32)


def nt(a, b):
    return lax.dot_general(a, b, (((1,), (1,)), ((), ())), preferred_element_type=f32)


def tn(a, b):
    return lax.dot_general(a, b, (((0,), (0,)), ((), ())), preferred_element_type=f32)


def flipped(block, axis, bit):
    size = lax.axis_size(axis)
    return lax.ppermute(block, axis, [(i, i ^ bit) for i in range(size)])


def moved(block, axis, distance):
    size = lax.axis_size(axis)
    route = [(i, i + distance) for i in range(size) if 0 <= i + distance < size]
    return lax.ppermute(block, axis, route)


def bits_of(axis):
    size = lax.axis_size(axis)
    return [1 << i for i in range(size.bit_length() - 1)]


class SmallSum:
    def __init__(self, block, paired=True):
        self.block, self.rounds = block, []
        if not paired:
            self.rounds = [(axis, [bit]) for axis in ("dp", "blk") for bit in bits_of(axis)]
            return
        for axis in ("dp", "blk"):
            bits = bits_of(axis)
            odd = len(bits) % 2
            parts = [bits[:odd]] * odd + [bits[i : i + 2] for i in range(odd, len(bits), 2)]
            self.rounds += [(axis, part) for part in parts]

    def left(self):
        return len(self.rounds)

    def send(self):
        axis, part = self.rounds.pop(0)
        ways = part if len(part) == 1 else [part[0], part[1], part[0] | part[1]]
        self.arrived = [flipped(self.block, axis, way) for way in ways]

    def take(self, tie=lambda *values: values):
        others = tie(*self.arrived)
        if len(others) == 1:
            self.block = self.block + others[0]
        else:
            self.block = (self.block + others[0]) + (others[1] + others[2])


def added(kept, arrived):
    return (kept.astype(f32) + arrived.astype(f32)).astype(bf16)


def summed(addends):
    total = addends[0].astype(f32)
    for addend in addends[1:]:
        total = total + addend.astype(f32)
    return total.astype(bf16)


class Scatter:
    def __init__(self, addends, order):
        self.addends, self.order = list(addends), list(order)

    def prepare(self):
        self.sent = summed([addend[1] for addend in self.addends])

    def send(self):
        self.arrived = flipped(self.sent, "dp", self.order.pop(0))

    def take(self):
        self.addends = [addend[0] for addend in self.addends] + [self.arrived]


class Line:
    def __init__(self, first, second, lows):
        self.bits, self.lows = bits_of("blk"), lows
        first, second = summed(first.addends), summed(second.addends)
        self.keep = jnp.where(lows[0], first, second)
        self.sent = jnp.where(lows[0], second, first)

    def scatter(self):
        self.arrived = flipped(self.sent, "blk", 1)

    def exchange(self):
        share = added(self.keep, self.arrived)
        for bit, low in zip(self.bits[1:-1], self.lows[1:]):
            middle = share.shape[0] // 2
            keep = jnp.where(low, share[:middle], share[middle:])
            sent = jnp.where(low, share[middle:], share[:middle])
            share = added(keep, flipped(sent, "blk", bit))
        self.keep = share
        self.arrived = flipped(share, "blk", self.bits[-1])

    def joined(self, low):
        mine, other = self.keep, self.arrived
        return jnp.concatenate(
            [jnp.where(low, mine, other), jnp.where(low, other, mine)], axis=0
        )

    def gather(self):
        share = added(self.keep, self.arrived)
        for bit, low in reversed(list(zip(self.bits[1:-1], self.lows[1:]))):
            self.keep, self.arrived = share, flipped(share, "blk", bit)
            share = self.joined(low)
        self.keep = share
        self.arrived = flipped(share, "blk", 1)

    def result(self):
        return self.joined(self.lows[0])


def together(*values):
    return lax.optimization_barrier(values)


def whole(shape):
    return pl.BlockSpec(shape, lambda *a: (0,) * len(shape))


def call(kernel, name, table, operands, outs, scratch=(), mib=8):
    scalar = pl.BlockSpec(memory_space=pltpu.SMEM)
    return pl.pallas_call(
        kernel,
        grid_spec=pltpu.PrefetchScalarGridSpec(
            num_scalar_prefetch=1,
            grid=(1,),
            in_specs=[
                spec if isinstance(spec, pl.BlockSpec) else whole(spec.shape)
                for spec in (o[0] if isinstance(o, tuple) else o for o in operands)
            ],
            out_specs=[scalar if o.shape == (2,) else whole(o.shape) for o in outs],
            scratch_shapes=list(scratch),
        ),
        out_shape=outs,
        cost_estimate=pl.CostEstimate(flops=1 << 20, bytes_accessed=1 << 16, transcendentals=0),
        compiler_params=pltpu.CompilerParams(vmem_limit_bytes=mib << 20),
        name=name,
    )(table, *[o[1] if isinstance(o, tuple) else o for o in operands])


def struct(shape, dtype):
    return jax.ShapeDtypeStruct(shape, dtype)


def unit_rows(rows):
    centred = rows - jnp.mean(rows, axis=-1, keepdims=True)
    scale = lax.rsqrt(jnp.mean(centred * centred, axis=-1, keepdims=True) + ln_epsilon)
    return centred * scale, scale


def norm_back(grad, unit, scale, gain):
    inner = grad * gain
    return scale * (
        inner
        - jnp.mean(inner, axis=-1, keepdims=True)
        - unit * jnp.mean(inner * unit, axis=-1, keepdims=True)
    )


def column_sum(rows):
    return jnp.sum(rows, axis=0, keepdims=True)


def totals_kernel(table, raw_ref, out_ref):
    raw = raw_ref[...]
    out_ref[0:1, :] = column_sum(raw)
    out_ref[1:2, :] = column_sum(raw * raw)


def enter_kernel(total_tokens, table, raw_ref, sum_ref, vec_ref, id_ref, x_ref, mean_ref, std_ref):
    width = raw_ref.shape[0]
    mean = sum_ref[0:1, :] / total_tokens
    variance = sum_ref[1:2, :] / total_tokens - mean * mean
    inverse = lax.rsqrt(variance + stat_epsilon)
    mean_ref[...] = mean
    std_ref[...] = inverse
    unit, _ = unit_rows((raw_ref[...] - mean) * inverse)
    x_ref[0:width, :] = (unit * vec_ref[0:1, :] + vec_ref[1:2, :]).astype(bf16)
    x_ref[width:, :] = jnp.zeros((x_ref.shape[0] - width, x_ref.shape[1]), bf16)
    ids = jnp.broadcast_to(id_ref[...], (16, width)).astype(f32).astype(bf16)
    x_ref[width:, 0:width] = ids


def id_columns(ids, width):
    return jnp.broadcast_to(ids, (128, width)).T


def id_row(rows):
    return rows.astype(f32)[0:1]


def project_own_kernel(table, x_ref, w_ref, vec_ref, q_ref, kv_ref, id_ref):
    width = q_ref.shape[0]
    features = q_ref.shape[1]
    slot = kv_ref.shape[0] // 2
    x = x_ref[0:width, :]
    q_ref[...] = ((nn(x, w_ref[:, :features]) + vec_ref[4:5, :]) * score_scale).astype(bf16)
    kv_ref[slot, :, :features] = nn(x, w_ref[:, features : 2 * features]).astype(bf16)
    kv_ref[slot, :, features:] = (nn(x, w_ref[:, 2 * features :]) + vec_ref[5:6, :]).astype(bf16)
    id_ref[slot] = id_columns(id_row(x_ref[width : width + 8, 0:width]), width)


def project_pair_kernel(
    d, inside_at, table, xa_ref, xb_ref, x_ref, w_ref, vec_ref, kv_in, id_in, kv_ref, id_ref, both
):
    width = kv_ref.shape[1]
    features = kv_ref.shape[2] // 2
    reach = kv_ref.shape[0] // 2
    done = slice(reach - d + 1, reach + d)
    kv_ref[done] = kv_in[done]
    id_ref[done] = id_in[done]
    both[0], both[1] = xa_ref[...], xb_ref[...]
    own = id_row(x_ref[width : width + 8, 0:width])
    low, high = jnp.min(own), jnp.max(own)

    def one(i, carry):
        slot = reach - d + 2 * d * i
        ids = id_row(both[i, width : width + 8, 0:width])
        near = (table[inside_at + i] > 0) & (jnp.max(ids) >= low) & (jnp.min(ids) <= high)
        id_ref[slot] = jnp.full((width, 128), -1.0, f32)

        @pl.when(near)
        def _():
            x = both[i, 0:width, :]
            kv_ref[slot, :, :features] = nn(x, w_ref[:, features : 2 * features]).astype(bf16)
            kv_ref[slot, :, features:] = (
                nn(x, w_ref[:, 2 * features :]) + vec_ref[5:6, :]
            ).astype(bf16)
            id_ref[slot] = id_columns(ids, width)

        return carry

    lax.fori_loop(0, 2, one, 0)


def lane_half(rows, which):
    lanes = lax.broadcasted_iota(jnp.int32, (rows, 128), 1)
    return (lanes >= 64) if which else (lanes < 64)


def mask_rows(own_row, width):
    ids = lax.broadcasted_iota(jnp.int32, (64, width), 0).astype(f32)
    return jnp.where(ids == own_row, 0.0, masked_score).astype(bf16)


def key_marks(column, width):
    lane_ids = (lax.broadcasted_iota(jnp.int32, (width, 128), 1) % 64).astype(f32)
    return (column == lane_ids).astype(f32).astype(bf16)


def lane_group(g):
    return pl.ds(pl.multiple_of(g * GROUP * HEAD_WIDTH, 128), GROUP * HEAD_WIDTH)


def attend_kernel(reach, table, q_ref, kv_ref, qid_ref, kid_ref, o_ref, lse_ref, bound_ref, acc, top, qm, sc):
    width, features = q_ref.shape
    slots = kv_ref.shape[0]
    steps = features // (GROUP * HEAD_WIDTH)
    low = kid_ref[reach, 0:1, :]
    high = kid_ref[reach, width - 1 : width, :]
    start = jnp.full_like(low, float(reach))
    end = jnp.full_like(low, float(reach))
    for s in range(slots):
        active = (kid_ref[s, width - 1 : width, :] >= low) & (kid_ref[s, 0:1, :] <= high)
        start = jnp.where(active, jnp.minimum(start, float(s)), start)
        end = jnp.where(active, jnp.maximum(end, float(s)), end)
    bound_ref[0] = jnp.min(start).astype(jnp.int32)
    bound_ref[1] = jnp.max(end).astype(jnp.int32) + 1
    barred = mask_rows(qid_ref[...].astype(f32), width)
    upper = lane_half(width, 1)
    one_rows = (lax.broadcasted_iota(jnp.int32, (16, width), 0) == 0).astype(f32).astype(bf16)

    def group(g, carry):
        lanes_g = lane_group(g)
        lanes_v = pl.ds(pl.multiple_of(features + g * GROUP * HEAD_WIDTH, 128), GROUP * HEAD_WIDTH)
        top[...] = jnp.full_like(top, masked_score)
        acc[...] = jnp.zeros_like(acc)
        q_t = q_ref[:, lanes_g].T
        for h in range(GROUP):
            head = q_t[64 * h : 64 * h + 64, :]
            qm[h, 0:64, :] = barred if h % 2 else head
            qm[h, 64:128, :] = head if h % 2 else barred

        def step(s, carry):
            keys = kv_ref[s, :, lanes_g]
            values_t = kv_ref[s, :, lanes_v].T
            marks = key_marks(kid_ref[s], width)
            for h in range(GROUP):
                lanes = slice(128 * (h // 2), 128 * (h // 2) + 128)
                pair = keys[:, lanes]
                marked = jnp.where(upper, pair, marks) if h % 2 else jnp.where(upper, marks, pair)
                sc[h] = nn(marked, qm[h])
            for h in range(GROUP):
                score = sc[h]
                old = top[h : h + 1, :]
                new = jnp.maximum(old, jnp.max(score, axis=0, keepdims=True))
                fade = jnp.exp(old - new)
                weight = jnp.exp(score - new).astype(bf16)
                top[h : h + 1, :] = new
                rows = slice(80 * h, 80 * h + 80)
                left = jnp.concatenate([values_t[64 * h : 64 * h + 64, :], one_rows], axis=0)
                acc[rows, :] = acc[rows, :] * fade + nn(left, weight)
            return carry

        lax.fori_loop(bound_ref[0], bound_ref[1], step, 0)
        outs, lses = [], []
        for h in range(GROUP):
            total = acc[80 * h + 64 : 80 * h + 65, :]
            outs.append(acc[80 * h : 80 * h + 64, :] / total)
            lses.append(top[h : h + 1, :] + jnp.log(total))
        o_ref[:, lanes_g] = jnp.concatenate(outs, axis=0).T.astype(bf16)
        lse_ref[g] = jnp.concatenate(lses, axis=0)
        return carry

    lax.fori_loop(0, steps, group, 0)


def spread_rows(table, plain, target, lanes, half):
    part = plain.shape[0] // (4 * half)
    for side in range(2):
        for h in range(2):
            for p in range(half):
                owner = table[half * (1 + 2 * h + side) + p]
                place = pl.multiple_of((2 * owner + h) * part, 8)
                to = ((side * 2 + h) * half + p) * part
                target[to : to + part, lanes] = plain[pl.ds(place, part), :].astype(bf16)


def ffn_kernel(
    half,
    table,
    o_ref,
    wo_ref,
    raw_ref,
    mean_ref,
    std_ref,
    vec_ref,
    cot_ref,
    w1_ref,
    w2_ref,
    out_ref,
    gm_ref,
    ga_ref,
    sk_ref,
    ss_ref,
    ek_ref,
    es_ref,
    row_ref,
    middle_s,
    gsec,
    s2,
    s2t,
    ot,
    plain,
    rows_s,
    acc,
):
    features = gm_ref.shape[1]
    inner = w1_ref.shape[1]
    chunk = inner // half
    wide = chunk // 2
    normed = (raw_ref[...] - mean_ref[...]) * std_ref[...]
    middle = normed + nn(o_ref[...], wo_ref[...]) + vec_ref[6:7, :]
    middle_s[...] = middle
    unit, _ = unit_rows(middle)
    second = unit * vec_ref[2:3, :] + vec_ref[3:4, :]
    s2[...] = second.astype(bf16)
    plain[...] = second.T
    spread_rows(table, plain, s2t, slice(None), half)
    plain[...] = o_ref[...].T.astype(f32)
    spread_rows(table, plain, ot, slice(None), half)
    acc[...] = jnp.zeros_like(acc)
    gsec[...] = jnp.zeros_like(gsec)
    own = table[half] % 2

    def step(i, carry):
        place = table[i] * chunk
        lanes = pl.ds(pl.multiple_of(place, 128), chunk)
        row = pl.ds(8 + place // features, 1)
        row_lanes = pl.ds(pl.multiple_of(place % features, 128), chunk)
        w1 = w1_ref[:, lanes]
        w2 = w2_ref[lanes, :]
        pre = nn(s2[...], w1) + vec_ref[row, row_lanes]
        back = nt(cot_ref[...], w2)
        area = 0.5 * (1.0 + lax.erf(pre * (0.5**0.5)))
        bell = jnp.exp(-0.5 * pre * pre) * (1.0 / (2.0 * jnp.pi) ** 0.5)
        hidden = (pre * area).astype(bf16)
        grad = ((area + pre * bell) * back).astype(bf16)
        acc[...] += nn(hidden, w2)
        gsec[...] += nt(grad, w1)
        row_ref[row, row_lanes] = column_sum(grad.astype(f32))
        rows_s[...] = nn(hidden.T, cot_ref[...]).astype(bf16)
        for side, ref in ((0, sk_ref), (1, ss_ref)):
            first = jnp.where(own == side, 0, wide)
            for h, at in ((0, i), (1, table[5 * half + i])):
                start = pl.multiple_of(first + h * (wide // 2), 16)
                ref[h, at] = rows_s[pl.ds(start, wide // 2), :]
        ek_ref[:, lanes] = nn(s2t[: features // 2, :], grad).astype(bf16)
        es_ref[:, lanes] = nn(s2t[features // 2 :, :], grad).astype(bf16)
        return carry

    lax.fori_loop(0, half, step, 0, unroll=True)
    out_ref[...] = (middle_s[...] + acc[...] + vec_ref[7:8, :]).astype(bf16)
    unit, scale = unit_rows(middle_s[...])
    grad = gsec[...]
    cot = cot_ref[...].astype(f32)
    row_ref[0:1, :] = column_sum(grad * unit)
    row_ref[1:2, :] = column_sum(grad)
    grad_middle = cot + norm_back(grad, unit, scale, vec_ref[2:3, :])
    gm_ref[...] = grad_middle
    branch = grad_middle.astype(bf16)
    row_ref[2:3, :] = column_sum(branch.astype(f32))
    row_ref[3:4, :] = column_sum(cot)
    ga_ref[...] = nt(branch, wo_ref[...]).astype(bf16)
    ek_ref[:, inner:] = nn(ot[: features // 2, :], branch).astype(bf16)
    es_ref[:, inner:] = nn(ot[features // 2 :, :], branch).astype(bf16)


def attend_back_kernel(
    g,
    bounds,
    q_ref,
    kv_ref,
    o_ref,
    g_ref,
    lse_ref,
    qid_ref,
    kid_ref,
    dq_ref,
    dk_ref,
    dv_ref,
    row_ref,
    acc,
    qm,
    gm,
    q_stack,
    g_stack,
    sc,
    dp,
    p_wide,
    g_wide,
    rows_s,
):
    width, features = q_ref.shape
    slots = kv_ref.shape[0]
    barred = mask_rows(qid_ref[...].astype(f32), width)
    nothing = jnp.zeros((64, width), bf16)
    upper = lane_half(width, 1)

    def blank(s, carry):
        dk_ref[s] = jnp.zeros(dk_ref.shape[1:], dk_ref.dtype)
        dv_ref[s] = jnp.zeros(dv_ref.shape[1:], dv_ref.dtype)
        return carry

    lax.fori_loop(0, bounds[0], blank, 0)
    lax.fori_loop(bounds[1], slots, blank, 0)

    base = g * GROUP * HEAD_WIDTH
    lanes_g = slice(base, base + GROUP * HEAD_WIDTH)
    lanes_v = slice(features + base, features + base + GROUP * HEAD_WIDTH)
    acc[...] = jnp.zeros_like(acc)
    q_all, g_all = q_ref[:, lanes_g], g_ref[:, lanes_g]
    product = (g_all.astype(f32) * o_ref[:, lanes_g].astype(f32)).T
    q_t, g_t = q_all.T, g_all.T
    for h in range(GROUP):
        lanes = slice(128 * (h // 2), 128 * (h // 2) + 128)
        rows = slice(64 * h, 64 * h + 64)
        odd = h % 2
        qm[h, 0:64, :] = barred if odd else q_t[rows, :]
        qm[h, 64:128, :] = q_t[rows, :] if odd else barred
        gm[h, 0:64, :] = nothing if odd else g_t[rows, :]
        gm[h, 64:128, :] = g_t[rows, :] if odd else nothing
        half = lane_half(width, odd)
        place = slice(width * odd, width * odd + width)
        pair = q_all[:, lanes]
        q_stack[h // 2, place, :] = jnp.where(half, pair, jnp.zeros_like(pair))
        pair = g_all[:, lanes]
        g_stack[h // 2, place, :] = jnp.where(half, pair, jnp.zeros_like(pair))
        rows_s[h : h + 1, :] = column_sum(product[rows, :])
    rows_s[8:9, :] = jnp.zeros((1, GROUP * HEAD_WIDTH), f32)

    def step(s, carry):
        keys = kv_ref[s, :, lanes_g]
        values = kv_ref[s, :, lanes_v]
        keys_t = keys.T
        marks = key_marks(kid_ref[s], width)
        for h in range(GROUP):
            lanes = slice(128 * (h // 2), 128 * (h // 2) + 128)
            pair = keys[:, lanes]
            marked = jnp.where(upper, pair, marks) if h % 2 else jnp.where(upper, marks, pair)
            sc[h] = nn(marked, qm[h])
            dp[h] = nn(values[:, lanes], gm[h])
        for h in range(GROUP):
            place = slice(width * (h % 2), width * (h % 2) + width)
            prob = jnp.exp(sc[h] - lse_ref[g, h : h + 1, :])
            p_wide[h // 2, :, place] = prob.astype(bf16)
            g_wide[h // 2, :, place] = (prob * (dp[h] - rows_s[h : h + 1, :])).astype(bf16)
        for h in range(GROUP):
            place = slice(width * (h % 2), width * (h % 2) + width)
            rows = slice(64 * h, 64 * h + 64)
            acc[rows, :] += nn(keys_t[rows, :], g_wide[h // 2, :, place])
        key_parts, value_parts = [], []
        for j in range(GROUP // 2):
            value_parts.append(nn(p_wide[j], g_stack[j]))
            key_parts.append(nn(g_wide[j], q_stack[j]))
        value_all = jnp.concatenate(value_parts, axis=1)
        dk_ref[s] = jnp.concatenate(key_parts, axis=1).astype(bf16)
        dv_ref[s] = value_all.astype(bf16)
        rows_s[8:9, :] += column_sum(value_all)
        return carry

    lax.fori_loop(bounds[0], bounds[1], step, 0)
    dq = (acc[...].T.astype(bf16).astype(f32) * score_scale).astype(bf16)
    dq_ref[...] = dq
    row_ref[0:1, :] = column_sum(dq.astype(f32))
    row_ref[1:2, :] = rows_s[8:9, :]


def parts_kernel(reach, bounds, *refs):
    groups = (len(refs) - 3) // 3
    dqs, dks, dvs = (refs[k * groups : (k + 1) * groups] for k in range(3))
    w_ref, p_ref, own_ref = refs[3 * groups :]
    features = p_ref.shape[2]
    size = features // groups

    def part(s):
        total = None
        for g in range(groups):
            for ref, base in ((dks[g], features), (dvs[g], 2 * features)):
                now = nt(ref[s], w_ref[:, base + g * size : base + (g + 1) * size])
                total = now if total is None else total + now
        return total

    def one(s, to):
        active = (s >= bounds[0]) & (s < bounds[1])

        @pl.when(active)
        def _():
            p_ref[to] = part(s).astype(bf16)

        @pl.when(jnp.logical_not(active))
        def _():
            p_ref[to] = jnp.zeros(p_ref.shape[1:], p_ref.dtype)

    def some(i, carry):
        one(jnp.where(i < reach, i, i + 1), i)
        return carry

    lax.fori_loop(0, 2 * reach, some, 0)
    total = part(reach)
    for g in range(groups):
        total = total + nt(dqs[g][...], w_ref[:, g * size : (g + 1) * size])
    own_ref[...] = total


def weight_kernel(reach, half, groups, table, *refs):
    slots = 2 * reach + 1
    xs, bounds = refs[:slots], refs[slots]
    refs = refs[slots + 1 :]
    dqs, dks, dvs = (refs[k * groups : (k + 1) * groups] for k in range(3))
    keep_ref, send_ref, xt, plain = refs[3 * groups :]
    width, size = dqs[0].shape
    features = size * groups
    few = min(3, slots)
    small = bounds[1] - bounds[0] <= few
    start = jnp.minimum(bounds[0], slots - few)

    for s in range(slots):

        @pl.when(jnp.logical_not(small) | ((s >= start) & (s < start + few)))
        def _(s=s):
            plain[...] = xs[s][0:width, :].T.astype(f32)
            spread_rows(table, plain, xt, slice(width * s, width * s + width), half)

    def put(tokens, right, base):
        lanes = slice(base, base + size)
        keep_ref[:, lanes] = nn(xt[: features // 2, tokens], right).astype(bf16)
        send_ref[:, lanes] = nn(xt[features // 2 :, tokens], right).astype(bf16)

    for g in range(groups):
        put(slice(width * reach, width * reach + width), dqs[g][...], g * size)

    def over(start, count):
        tokens = pl.ds(pl.multiple_of(start * width, 128), count * width)
        for base, group in ((features, dks), (2 * features, dvs)):
            for g in range(groups):
                rows = group[g][pl.ds(start, count)].reshape(count * width, size)
                put(tokens, rows, base + g * size)

    @pl.when(small)
    def _():
        over(start, few)

    @pl.when(jnp.logical_not(small))
    def _():
        over(0, slots)


def leave_kernel(
    table,
    raw_ref,
    mean_ref,
    std_ref,
    vec_ref,
    gm_ref,
    own_ref,
    left_ref,
    right_ref,
    ffn_rows,
    *refs,
):
    attend_rows, (gn_ref, row_ref) = refs[:-2], refs[-2:]
    features = raw_ref.shape[1]
    centred = raw_ref[...] - mean_ref[...]
    unit, scale = unit_rows(centred * std_ref[...])
    grad = own_ref[...] + left_ref[...].astype(f32) + right_ref[...].astype(f32)
    row_ref[0:1, :] = column_sum(grad * unit)
    row_ref[1:2, :] = column_sum(grad)
    row_ref[2:4, :] = ffn_rows[0:2, :]
    size = features // len(attend_rows)
    for g, ref in enumerate(attend_rows):
        row_ref[4:6, g * size : (g + 1) * size] = ref[...]
    row_ref[6:8, :] = ffn_rows[2:4, :]
    row_ref[8:12, :] = ffn_rows[8:12, :]
    whole_grad = gm_ref[...] + norm_back(grad, unit, scale, vec_ref[0:1, :])
    gn_ref[...] = whole_grad
    row_ref[12:13, :] = column_sum(whole_grad)
    row_ref[13:14, :] = column_sum(whole_grad * centred)
    row_ref[14:16, :] = jnp.zeros((2, features), f32)


def adam_rule(master, moment, square, gradient, step_value, step_rate, weight_decay):
    moment_new = beta_one * moment + (1.0 - beta_one) * gradient
    square_new = beta_two * square + (1.0 - beta_two) * gradient * gradient
    fix_first = 1.0 - jnp.power(beta_one, step_value)
    fix_second = 1.0 - jnp.power(beta_two, step_value)
    planned = step_rate * jnp.minimum(1.0, step_value / warmup_length)
    direction = moment_new / fix_first / (jnp.sqrt(square_new / fix_second) + adam_epsilon)
    weight_new = master - planned * (direction + weight_decay * master)
    return (weight_new, moment_new, square_new, weight_new.astype(bf16))


def per_device(
    raw_input,
    cotangent,
    segment_ids,
    step_count,
    inlet_copy,
    inlet_master,
    inlet_moment,
    inlet_square,
    outlet_copy,
    outlet_master,
    outlet_moment,
    outlet_square,
    expand_copy,
    expand_master,
    expand_moment,
    expand_square,
    shrink_copy,
    shrink_master,
    shrink_moment,
    shrink_square,
    vector_copy,
    vector_master,
    vector_moment,
    vector_square,
):
    sequences, block_length, features = raw_input.shape
    assert sequences == 1
    width = block_length
    group_size = lax.axis_size("blk")
    group_index = lax.axis_index("blk")
    owners = lax.axis_size("dp")
    owner = lax.axis_index("dp")
    half = owners // 2
    total_tokens = owners * group_size * block_length
    reach = group_size // 2
    slots = 2 * reach + 1
    inner = expand_copy.shape[1]
    chunk = inner // half
    vectors = vector_copy.astype(f32)
    raw = raw_input.reshape(width, features)
    cot = cotangent.reshape(width, features)
    own_ids = segment_ids
    count = owners.bit_length() - 1
    scalar = pl.BlockSpec(memory_space=pltpu.SMEM)
    vmem = pltpu.VMEM

    def reversed_bits(value):
        return int(format(value, f"0{count - 1}b")[::-1], 2) if count > 1 else 0

    straight = [reversed_bits(p) for p in range(half)]
    other_way = list(range(half))
    relative = jnp.array(
        [2 * v for v in straight]
        + [2 * v for v in straight]
        + [2 * v + 1 for v in straight]
        + [2 * v for v in other_way]
        + [2 * v + 1 for v in other_way],
        jnp.int32,
    ) ^ owner
    inside = [group_index >= d for d in range(1, reach + 1)]
    inside += [group_index + d < group_size for d in range(1, reach + 1)]
    table = jnp.concatenate(
        [
            relative[:half] // 2,
            relative[half:],
            jnp.array(straight, jnp.int32),
            jnp.stack([flag for pair in zip(inside[:reach], inside[reach:]) for flag in pair]).astype(jnp.int32),
        ]
    )
    lows = [(group_index // bit) % 2 == 0 for bit in bits_of("blk")]
    column_count = vector_master.shape[1]
    column_start = owner * column_count
    step_value = step_count[0].astype(f32)

    tokens, row = (width, features), (1, features)
    wkv = 3 * features
    lanes = GROUP * HEAD_WIDTH
    steps = features // lanes

    (totals,) = call(
        totals_kernel, "totals", jnp.zeros((1,), jnp.int32), [raw], [struct((2, features), f32)], mib=2
    )
    rounds = SmallSum(totals)
    rounds.send()
    rounds.take()
    rounds.send()
    tied = together(*rounds.arrived, table, column_start, vectors, *lows)
    ways = len(rounds.arrived)
    rounds.arrived = list(tied[:ways])
    table, column_start, vectors = tied[ways : ways + 3]
    lows = list(tied[ways + 3 :])
    rounds.take()
    while rounds.left():
        rounds.send()
        rounds.take()
    totals = rounds.block
    packed = width + 16
    x, mean_row, inverse_row = call(
        functools.partial(enter_kernel, total_tokens),
        "enter",
        table,
        [raw, totals, vectors, own_ids],
        [struct((packed, features), bf16), struct(row, f32), struct(row, f32)],
        mib=6,
    )

    xs = [None] * slots
    xs[reach] = x
    ahead, behind = moved(x, "blk", 1), moved(x, "blk", -1)
    queries, pairs, columns = call(
        project_own_kernel,
        "project_own",
        table,
        [x, inlet_copy, vectors],
        [
            struct(tokens, bf16),
            struct((slots, width, 2 * features), bf16),
            struct((slots, width, 128), f32),
        ],
        mib=6,
    )
    ahead, behind, queries = together(ahead, behind, queries)
    for d in range(1, reach + 1):
        if d > 1:
            ahead, behind = moved(ahead, "blk", 1), moved(behind, "blk", -1)
            ahead, behind, pairs = together(ahead, behind, pairs)
        xs[reach - d], xs[reach + d] = ahead, behind
        pairs, columns = call(
            functools.partial(project_pair_kernel, d, 6 * half + 2 * (d - 1)),
            "project_pair",
            table,
            [ahead, behind, x, inlet_copy, vectors, pairs, columns],
            [struct(pairs.shape, bf16), struct(columns.shape, f32)],
            [vmem((2, packed, features), bf16)],
            mib=6,
        )

    attended, lse, bounds = call(
        functools.partial(attend_kernel, reach),
        "attend",
        table,
        [queries, pairs, own_ids, columns],
        [struct(tokens, bf16), struct((steps, GROUP, width), f32), struct((2,), jnp.int32)],
        [
            vmem((80 * GROUP, width), f32),
            vmem((8, width), f32),
            vmem((GROUP, 128, width), bf16),
            vmem((GROUP, width, width), f32),
        ],
        mib=6,
    )

    owned_wide, owned = inner // owners, features // owners
    kept_shrink = struct((2, half, owned_wide // 2, features), bf16)
    kept_expand = struct((features // 2, inner + features), bf16)
    layer_output, grad_middle, grad_attended, shrink_keep, shrink_send, expand_keep, expand_send, ffn_rows = call(
        functools.partial(ffn_kernel, half),
        "ffn",
        table,
        [attended, outlet_copy, raw, mean_row, inverse_row, vectors, cot, expand_copy, shrink_copy],
        [
            struct(tokens, bf16),
            struct(tokens, f32),
            struct(tokens, bf16),
            kept_shrink,
            kept_shrink,
            kept_expand,
            kept_expand,
            struct((12, features), f32),
        ],
        [
            vmem(tokens, f32),
            vmem(tokens, f32),
            vmem(tokens, bf16),
            vmem((features, width), bf16),
            vmem((features, width), bf16),
            vmem((features, width), f32),
            vmem((chunk, features), bf16),
            vmem(tokens, f32),
        ],
        mib=14,
    )
    bits = bits_of("dp")
    orders = (bits[1:], bits[:0:-1])

    def scatters(keep, arrived, rows):
        shape = (2,) + (2,) * (count - 1) + (rows // 2, keep.shape[-1])
        keep, arrived = keep.reshape(shape), arrived.reshape(shape)
        return [Scatter([keep[h], arrived[h]], orders[h]) for h in range(2)]

    token = [grad_attended]

    def after(*values):
        tied = together(*values, *token)[: len(values)]
        token[:] = tied
        return tied

    def launch(pair):
        for one in pair:
            one.prepare()
        token[:] = [one.sent for one in pair]
        for one in pair:
            one.send()

    def advance(pair):
        for one, value in zip(pair, after(*[one.arrived for one in pair])):
            one.arrived = value
            one.take()
        if pair[0].order:
            launch(pair)

    def follow(line, stage):
        (line.arrived,) = after(line.arrived)
        stage(line)
        token[:] = [line.keep]

    def begin(pair):
        line = Line(*pair, lows)
        token[:] = [line.sent]
        line.scatter()
        return line

    def next_round():
        rounds.take(after)
        token[:] = [rounds.block]
        if rounds.left():
            rounds.send()

    shrink_in = flipped(shrink_send, "dp", 1)
    expand_in = flipped(expand_send, "dp", 1)
    spread = struct((slots, width, lanes), bf16)
    back = []
    for g in range(steps):
        (grad_attended,) = after(grad_attended)
        back.append(
            call(
                functools.partial(attend_back_kernel, g),
                "attend_back",
                bounds,
                [queries, pairs, attended, grad_attended, lse, own_ids, columns],
                [struct((width, lanes), bf16), spread, spread, struct((2, lanes), f32)],
                [
                    vmem((lanes, width), f32),
                    vmem((GROUP, 128, width), bf16),
                    vmem((GROUP, 128, width), bf16),
                    vmem((GROUP // 2, 2 * width, 128), bf16),
                    vmem((GROUP // 2, 2 * width, 128), bf16),
                    vmem((GROUP, width, width), f32),
                    vmem((GROUP, width, width), f32),
                    vmem((GROUP // 2, width, 2 * width), bf16),
                    vmem((GROUP // 2, width, 2 * width), bf16),
                    vmem((16, width), f32),
                ],
                mib=8,
            )
        )
        token[:] = [back[-1][0]]
        if g == 0:
            (shrink_in,) = after(shrink_in)
            first = scatters(shrink_keep, shrink_in, owned_wide)
            launch(first)
    query_low, key_low, value_low, attend_rows = zip(*back)
    grads = [*query_low, *key_low, *value_low]
    (expand_in,) = after(expand_in)

    grads = after(*grads)
    parts, own_part = call(
        functools.partial(parts_kernel, reach),
        "parts",
        bounds,
        [*grads, inlet_copy],
        [struct((2 * reach, width, features), bf16), struct(tokens, f32)],
        mib=6,
    )
    to_left, to_right = parts[0], parts[2 * reach - 1]
    kept_inlet = struct((features // 2, wkv), bf16)
    inlet_keep, inlet_send = call(
        functools.partial(weight_kernel, reach, half, steps),
        "weights",
        table,
        xs + [(scalar, bounds), *grads],
        [kept_inlet, kept_inlet],
        [vmem((features, slots * width), bf16), vmem((features, width), f32)],
        mib=8,
    )
    inlet_in = flipped(inlet_send, "dp", 1)

    def taken(pair, arrived):
        for one, value in zip(pair, arrived):
            one.arrived = value
            one.take()

    *arrived, expand_in, inlet_keep = together(
        *[one.arrived for one in first], expand_in, inlet_keep
    )
    taken(first, arrived)
    for one in first:
        one.prepare()
    expand_in, first[0].sent, first[1].sent = together(expand_in, first[0].sent, first[1].sent)
    for one in first:
        one.send()
    second = scatters(expand_keep, expand_in, owned)
    for one in second:
        one.prepare()
        one.send()
    while True:
        *arrived, to_left, to_right, inlet_in = together(
            *[one.arrived for one in first], to_left, to_right, inlet_in
        )
        taken(first, arrived)
        if not first[0].order:
            break
        for one in first:
            one.prepare()
            one.send()
    from_right, from_left = moved(to_left, "blk", -1), moved(to_right, "blk", 1)
    line_one = Line(*first, lows)
    line_one.scatter()
    for d in range(reach - 1, 0, -1):
        from_right, from_left, line_one.keep = together(from_right, from_left, line_one.keep)
        to_left = added(parts[reach - d], from_right)
        to_right = added(parts[reach + d - 1], from_left)
        from_right, from_left = moved(to_left, "blk", -1), moved(to_right, "blk", 1)
    *arrived, line_one.arrived, line_one.keep = together(
        *[one.arrived for one in second], line_one.arrived, line_one.keep
    )
    taken(second, arrived)
    for one in second:
        one.prepare()
        one.send()
    line_one.exchange()
    from_right, from_left, inlet_in, line_one.keep = together(
        from_right, from_left, inlet_in, line_one.keep
    )
    third = scatters(inlet_keep, inlet_in, owned)
    for one in third:
        one.prepare()
        one.send()
    grad_normed, small = call(
        leave_kernel,
        "leave",
        table,
        [
            raw,
            mean_row,
            inverse_row,
            vectors,
            grad_middle,
            own_part,
            from_left,
            from_right,
            ffn_rows,
            *attend_rows,
        ],
        [struct(tokens, f32), struct((16, features), f32)],
        mib=8,
    )
    rounds = SmallSum(small, paired=False)
    while True:
        *arrived, rounds.block, line_one.keep = together(
            *[one.arrived for one in second], rounds.block, line_one.keep
        )
        taken(second, arrived)
        if not second[0].order:
            break
        for one in second:
            one.prepare()
            one.send()
    line_two = Line(*second, lows)
    line_two.scatter()

    def round_beside(line):
        *rounds.arrived, line.keep = together(*rounds.arrived, line.keep)
        rounds.take()

    rounds.send()
    round_beside(line_two)
    rounds.send()
    while True:
        *arrived, line_two.keep = together(*[one.arrived for one in third], line_two.keep)
        taken(third, arrived)
        for one in third:
            one.prepare()
            one.send()
        if not third[0].order:
            break
    line_two.arrived, line_one.keep = together(line_two.arrived, line_one.keep)
    line_two.exchange()
    for _ in bits_of("dp")[1:-1]:
        round_beside(line_two)
        rounds.send()
    *arrived, line_two.keep = together(*[one.arrived for one in third], line_two.keep)
    taken(third, arrived)
    line_three = Line(*third, lows)
    line_three.scatter()
    line_one.arrived, line_three.keep = together(line_one.arrived, line_three.keep)
    line_one.gather()
    round_beside(line_three)
    rounds.send()
    line_two.arrived, line_three.arrived, *rounds.arrived = together(
        line_two.arrived, line_three.arrived, *rounds.arrived
    )
    rounds.take()
    line_three.exchange()
    line_two.gather()
    line_one.arrived, line_three.keep = together(line_one.arrived, line_three.keep)
    shrink_new = adam_rule(
        shrink_master,
        shrink_moment,
        shrink_square,
        line_one.result().astype(f32),
        step_value,
        rate_matrix,
        decay_matrix,
    )
    line_three.arrived, rounds.block, *shrink_new = together(
        line_three.arrived, rounds.block, *shrink_new
    )
    line_three.gather()
    while rounds.left():
        rounds.send()
        round_beside(line_three)
    small = rounds.block
    expand_share = line_two.result()
    inlet_share = line_three.result()

    band_mean = totals[0] / total_tokens
    band_variance = totals[1] / total_tokens - band_mean * band_mean
    inverse = lax.rsqrt(band_variance + stat_epsilon)
    back_totals = small[12:14]
    grad_variance = -0.5 * back_totals[1] * inverse * inverse * inverse
    grad_centre = -inverse * back_totals[0] - 2.0 * band_mean * grad_variance
    input_gradient = (
        grad_normed * inverse
        + grad_centre / total_tokens
        + 2.0 * grad_variance * raw / total_tokens
    ).reshape(sequences, block_length, features)
    vector_share = lax.dynamic_slice(
        small[:12], (0, column_start), (12, column_count), allow_negative_indices=False
    )

    updates = []
    for master, moment, square, share in (
        (inlet_master, inlet_moment, inlet_square, inlet_share),
        (outlet_master, outlet_moment, outlet_square, expand_share[:, inner:]),
        (expand_master, expand_moment, expand_square, expand_share[:, :inner]),
    ):
        updates.extend(
            adam_rule(
                master, moment, square, share.astype(f32), step_value, rate_matrix, decay_matrix
            )
        )
    updates.extend(shrink_new)
    updates.extend(
        adam_rule(
            vector_master, vector_moment, vector_square, vector_share, step_value, rate_vector, 0.0
        )
    )
    layer_output = layer_output.reshape(sequences, block_length, features)
    return (layer_output, input_gradient, band_mean, band_variance, *updates)


def solution(mesh):
    tokens = P("dp", "blk", None)
    rows = P("dp", None)
    columns = P(None, "dp")
    matrix = (P(), rows, rows, rows)
    return jax.shard_map(
        per_device,
        mesh=mesh,
        in_specs=(tokens, tokens, P("dp", "blk"), P())
        + matrix * 4
        + (P(), columns, columns, columns),
        out_specs=(tokens, tokens, P(), P()) + (rows,) * 16 + (columns,) * 4,
        check_vma=False,
    )
```

```python
import functools

import jax
import jax.numpy as jnp
from jax import lax
from jax.experimental import pallas as pl
from jax.experimental.pallas import tpu as pltpu
from jax.sharding import PartitionSpec as P

HEADS = 12
HEAD_WIDTH = 64
GROUP = 4

ln_epsilon = 1e-05
stat_epsilon = 1e-06
beta_one = 0.5
beta_two = 0.6
rate_matrix = 0.04
rate_vector = 0.8
warmup_length = 20.0
decay_matrix = 0.05
adam_epsilon = 1e-08
score_scale = 0.125
masked_score = -1e30

f32 = jnp.float32
bf16 = jnp.bfloat16


def nn(a, b):
    return lax.dot_general(a, b, (((1,), (0,)), ((), ())), preferred_element_type=f32)


def nt(a, b):
    return lax.dot_general(a, b, (((1,), (1,)), ((), ())), preferred_element_type=f32)


def tn(a, b):
    return lax.dot_general(a, b, (((0,), (0,)), ((), ())), preferred_element_type=f32)


def flipped(block, axis, bit):
    size = lax.axis_size(axis)
    return lax.ppermute(block, axis, [(i, i ^ bit) for i in range(size)])


def moved(block, axis, distance):
    size = lax.axis_size(axis)
    route = [(i, i + distance) for i in range(size) if 0 <= i + distance < size]
    return lax.ppermute(block, axis, route)


def bits_of(axis):
    size = lax.axis_size(axis)
    return [1 << i for i in range(size.bit_length() - 1)]


class SmallSum:
    def __init__(self, block, paired=True):
        self.block, self.rounds = block, []
        if not paired:
            self.rounds = [(axis, [bit]) for axis in ("blk", "dp") for bit in bits_of(axis)]
            return
        for axis in ("dp", "blk"):
            bits = bits_of(axis)
            odd = len(bits) % 2
            parts = [bits[:odd]] * odd + [bits[i : i + 2] for i in range(odd, len(bits), 2)]
            self.rounds += [(axis, part) for part in parts]

    def left(self):
        return len(self.rounds)

    def send(self):
        axis, part = self.rounds.pop(0)
        ways = part if len(part) == 1 else [part[0], part[1], part[0] | part[1]]
        self.arrived = [flipped(self.block, axis, way) for way in ways]

    def take(self, tie=lambda *values: values):
        others = tie(*self.arrived)
        if len(others) == 1:
            self.block = self.block + others[0]
        else:
            self.block = (self.block + others[0]) + (others[1] + others[2])


def added(kept, arrived):
    return (kept.astype(f32) + arrived.astype(f32)).astype(bf16)


def summed(addends):
    total = addends[0].astype(f32)
    for addend in addends[1:]:
        total = total + addend.astype(f32)
    return total.astype(bf16)


class Scatter:
    def __init__(self, addends, order):
        self.addends, self.order = list(addends), list(order)

    def prepare(self):
        self.sent = summed([addend[1] for addend in self.addends])

    def send(self):
        self.arrived = flipped(self.sent, "dp", self.order.pop(0))

    def take(self):
        self.addends = [addend[0] for addend in self.addends] + [self.arrived]


class Line:
    def __init__(self, first, second, lows):
        self.bits, self.lows = bits_of("blk"), lows
        first, second = summed(first.addends), summed(second.addends)
        self.keep = jnp.where(lows[0], first, second)
        self.sent = jnp.where(lows[0], second, first)

    def scatter(self):
        self.arrived = flipped(self.sent, "blk", 1)

    def exchange(self):
        share = added(self.keep, self.arrived)
        for bit, low in zip(self.bits[1:-1], self.lows[1:]):
            middle = share.shape[0] // 2
            keep = jnp.where(low, share[:middle], share[middle:])
            sent = jnp.where(low, share[middle:], share[:middle])
            share = added(keep, flipped(sent, "blk", bit))
        self.keep = share
        self.arrived = flipped(share, "blk", self.bits[-1])

    def joined(self, low):
        mine, other = self.keep, self.arrived
        return jnp.concatenate(
            [jnp.where(low, mine, other), jnp.where(low, other, mine)], axis=0
        )

    def gather(self):
        share = added(self.keep, self.arrived)
        for bit, low in reversed(list(zip(self.bits[1:-1], self.lows[1:]))):
            self.keep, self.arrived = share, flipped(share, "blk", bit)
            share = self.joined(low)
        self.keep = share
        self.arrived = flipped(share, "blk", 1)

    def result(self):
        return self.joined(self.lows[0])


def together(*values):
    return lax.optimization_barrier(values)


def whole(shape):
    return pl.BlockSpec(shape, lambda *a: (0,) * len(shape))


def call(kernel, name, table, operands, outs, scratch=(), mib=8):
    scalar = pl.BlockSpec(memory_space=pltpu.SMEM)
    return pl.pallas_call(
        kernel,
        grid_spec=pltpu.PrefetchScalarGridSpec(
            num_scalar_prefetch=1,
            grid=(1,),
            in_specs=[
                spec if isinstance(spec, pl.BlockSpec) else whole(spec.shape)
                for spec in (o[0] if isinstance(o, tuple) else o for o in operands)
            ],
            out_specs=[scalar if o.shape == (2,) else whole(o.shape) for o in outs],
            scratch_shapes=list(scratch),
        ),
        out_shape=outs,
        cost_estimate=pl.CostEstimate(flops=1 << 20, bytes_accessed=1 << 16, transcendentals=0),
        compiler_params=pltpu.CompilerParams(vmem_limit_bytes=mib << 20),
        name=name,
    )(table, *[o[1] if isinstance(o, tuple) else o for o in operands])


def struct(shape, dtype):
    return jax.ShapeDtypeStruct(shape, dtype)


def unit_rows(rows):
    centred = rows - jnp.mean(rows, axis=-1, keepdims=True)
    scale = lax.rsqrt(jnp.mean(centred * centred, axis=-1, keepdims=True) + ln_epsilon)
    return centred * scale, scale


def norm_back(grad, unit, scale, gain):
    inner = grad * gain
    return scale * (
        inner
        - jnp.mean(inner, axis=-1, keepdims=True)
        - unit * jnp.mean(inner * unit, axis=-1, keepdims=True)
    )


def column_sum(rows):
    return jnp.sum(rows, axis=0, keepdims=True)


def totals_kernel(table, raw_ref, out_ref):
    raw = raw_ref[...]
    out_ref[0:1, :] = column_sum(raw)
    out_ref[1:2, :] = column_sum(raw * raw)


def enter_kernel(total_tokens, table, raw_ref, sum_ref, vec_ref, id_ref, x_ref, mean_ref, std_ref):
    width = raw_ref.shape[0]
    mean = sum_ref[0:1, :] / total_tokens
    variance = sum_ref[1:2, :] / total_tokens - mean * mean
    inverse = lax.rsqrt(variance + stat_epsilon)
    mean_ref[...] = mean
    std_ref[...] = inverse
    unit, _ = unit_rows((raw_ref[...] - mean) * inverse)
    x_ref[0:width, :] = (unit * vec_ref[0:1, :] + vec_ref[1:2, :]).astype(bf16)
    x_ref[width:, :] = jnp.zeros((x_ref.shape[0] - width, x_ref.shape[1]), bf16)
    ids = jnp.broadcast_to(id_ref[...], (16, width)).astype(f32).astype(bf16)
    x_ref[width:, 0:width] = ids


def id_columns(ids, width):
    return jnp.broadcast_to(ids, (128, width)).T


def id_row(rows):
    return rows.astype(f32)[0:1]


def project_own_kernel(table, x_ref, w_ref, vec_ref, q_ref, kv_ref, id_ref):
    width = q_ref.shape[0]
    features = q_ref.shape[1]
    slot = kv_ref.shape[0] // 2
    x = x_ref[0:width, :]
    q_ref[...] = ((nn(x, w_ref[:, :features]) + vec_ref[4:5, :]) * score_scale).astype(bf16)
    kv_ref[slot, :, :features] = nn(x, w_ref[:, features : 2 * features]).astype(bf16)
    kv_ref[slot, :, features:] = (nn(x, w_ref[:, 2 * features :]) + vec_ref[5:6, :]).astype(bf16)
    id_ref[slot] = id_columns(id_row(x_ref[width : width + 8, 0:width]), width)


def project_pair_kernel(
    d, inside_at, table, xa_ref, xb_ref, x_ref, w_ref, vec_ref, kv_in, id_in, kv_ref, id_ref, both
):
    width = kv_ref.shape[1]
    features = kv_ref.shape[2] // 2
    reach = kv_ref.shape[0] // 2
    done = slice(reach - d + 1, reach + d)
    kv_ref[done] = kv_in[done]
    id_ref[done] = id_in[done]
    both[0], both[1] = xa_ref[...], xb_ref[...]
    own = id_row(x_ref[width : width + 8, 0:width])
    low, high = jnp.min(own), jnp.max(own)

    def one(i, carry):
        slot = reach - d + 2 * d * i
        ids = id_row(both[i, width : width + 8, 0:width])
        near = (table[inside_at + i] > 0) & (jnp.max(ids) >= low) & (jnp.min(ids) <= high)
        id_ref[slot] = jnp.full((width, 128), -1.0, f32)

        @pl.when(near)
        def _():
            x = both[i, 0:width, :]
            kv_ref[slot, :, :features] = nn(x, w_ref[:, features : 2 * features]).astype(bf16)
            kv_ref[slot, :, features:] = (
                nn(x, w_ref[:, 2 * features :]) + vec_ref[5:6, :]
            ).astype(bf16)
            id_ref[slot] = id_columns(ids, width)

        return carry

    lax.fori_loop(0, 2, one, 0)


def lane_half(rows, which):
    lanes = lax.broadcasted_iota(jnp.int32, (rows, 128), 1)
    return (lanes >= 64) if which else (lanes < 64)


def mask_rows(own_row, width):
    ids = lax.broadcasted_iota(jnp.int32, (64, width), 0).astype(f32)
    return jnp.where(ids == own_row, 0.0, masked_score).astype(bf16)


def key_marks(column, width):
    lane_ids = (lax.broadcasted_iota(jnp.int32, (width, 128), 1) % 64).astype(f32)
    return (column == lane_ids).astype(f32).astype(bf16)


def lane_group(g):
    return pl.ds(pl.multiple_of(g * GROUP * HEAD_WIDTH, 128), GROUP * HEAD_WIDTH)


def attend_kernel(reach, table, q_ref, kv_ref, qid_ref, kid_ref, o_ref, lse_ref, bound_ref, acc, top, qm, sc):
    width, features = q_ref.shape
    slots = kv_ref.shape[0]
    steps = features // (GROUP * HEAD_WIDTH)
    low = kid_ref[reach, 0:1, :]
    high = kid_ref[reach, width - 1 : width, :]
    start = jnp.full_like(low, float(reach))
    end = jnp.full_like(low, float(reach))
    for s in range(slots):
        active = (kid_ref[s, width - 1 : width, :] >= low) & (kid_ref[s, 0:1, :] <= high)
        start = jnp.where(active, jnp.minimum(start, float(s)), start)
        end = jnp.where(active, jnp.maximum(end, float(s)), end)
    bound_ref[0] = jnp.min(start).astype(jnp.int32)
    bound_ref[1] = jnp.max(end).astype(jnp.int32) + 1
    barred = mask_rows(qid_ref[...].astype(f32), width)
    upper = lane_half(width, 1)
    one_rows = (lax.broadcasted_iota(jnp.int32, (16, width), 0) == 0).astype(f32).astype(bf16)

    def group(g, carry):
        lanes_g = lane_group(g)
        lanes_v = pl.ds(pl.multiple_of(features + g * GROUP * HEAD_WIDTH, 128), GROUP * HEAD_WIDTH)
        top[...] = jnp.full_like(top, masked_score)
        acc[...] = jnp.zeros_like(acc)
        q_t = q_ref[:, lanes_g].T
        for h in range(GROUP):
            head = q_t[64 * h : 64 * h + 64, :]
            qm[h, 0:64, :] = barred if h % 2 else head
            qm[h, 64:128, :] = head if h % 2 else barred

        def step(s, carry):
            keys = kv_ref[s, :, lanes_g]
            values_t = kv_ref[s, :, lanes_v].T
            marks = key_marks(kid_ref[s], width)
            for h in range(GROUP):
                lanes = slice(128 * (h // 2), 128 * (h // 2) + 128)
                pair = keys[:, lanes]
                marked = jnp.where(upper, pair, marks) if h % 2 else jnp.where(upper, marks, pair)
                sc[h] = nn(marked, qm[h])
            for h in range(GROUP):
                score = sc[h]
                old = top[h : h + 1, :]
                new = jnp.maximum(old, jnp.max(score, axis=0, keepdims=True))
                fade = jnp.exp(old - new)
                weight = jnp.exp(score - new).astype(bf16)
                top[h : h + 1, :] = new
                rows = slice(80 * h, 80 * h + 80)
                left = jnp.concatenate([values_t[64 * h : 64 * h + 64, :], one_rows], axis=0)
                acc[rows, :] = acc[rows, :] * fade + nn(left, weight)
            return carry

        lax.fori_loop(bound_ref[0], bound_ref[1], step, 0)
        outs, lses = [], []
        for h in range(GROUP):
            total = acc[80 * h + 64 : 80 * h + 65, :]
            outs.append(acc[80 * h : 80 * h + 64, :] / total)
            lses.append(top[h : h + 1, :] + jnp.log(total))
        o_ref[:, lanes_g] = jnp.concatenate(outs, axis=0).T.astype(bf16)
        lse_ref[g] = jnp.concatenate(lses, axis=0)
        return carry

    lax.fori_loop(0, steps, group, 0)


def spread_rows(table, plain, target, lanes, half):
    part = plain.shape[0] // (4 * half)
    for side in range(2):
        for h in range(2):
            for p in range(half):
                owner = table[half * (1 + 2 * h + side) + p]
                place = pl.multiple_of((2 * owner + h) * part, 8)
                to = ((side * 2 + h) * half + p) * part
                target[to : to + part, lanes] = plain[pl.ds(place, part), :].astype(bf16)


def ffn_kernel(
    half,
    table,
    o_ref,
    wo_ref,
    raw_ref,
    mean_ref,
    std_ref,
    vec_ref,
    cot_ref,
    w1_ref,
    w2_ref,
    out_ref,
    gm_ref,
    ga_ref,
    sk_ref,
    ss_ref,
    ek_ref,
    es_ref,
    row_ref,
    middle_s,
    gsec,
    s2,
    s2t,
    ot,
    plain,
    rows_s,
    acc,
):
    features = gm_ref.shape[1]
    inner = w1_ref.shape[1]
    chunk = inner // half
    wide = chunk // 2
    normed = (raw_ref[...] - mean_ref[...]) * std_ref[...]
    middle = normed + nn(o_ref[...], wo_ref[...]) + vec_ref[6:7, :]
    middle_s[...] = middle
    unit, _ = unit_rows(middle)
    second = unit * vec_ref[2:3, :] + vec_ref[3:4, :]
    s2[...] = second.astype(bf16)
    plain[...] = second.T
    spread_rows(table, plain, s2t, slice(None), half)
    plain[...] = o_ref[...].T.astype(f32)
    spread_rows(table, plain, ot, slice(None), half)
    acc[...] = jnp.zeros_like(acc)
    gsec[...] = jnp.zeros_like(gsec)
    own = table[half] % 2

    def step(i, carry):
        place = table[i] * chunk
        lanes = pl.ds(pl.multiple_of(place, 128), chunk)
        row = pl.ds(8 + place // features, 1)
        row_lanes = pl.ds(pl.multiple_of(place % features, 128), chunk)
        w1 = w1_ref[:, lanes]
        w2 = w2_ref[lanes, :]
        pre = nn(s2[...], w1) + vec_ref[row, row_lanes]
        back = nt(cot_ref[...], w2)
        area = 0.5 * (1.0 + lax.erf(pre * (0.5**0.5)))
        bell = jnp.exp(-0.5 * pre * pre) * (1.0 / (2.0 * jnp.pi) ** 0.5)
        hidden = (pre * area).astype(bf16)
        grad = ((area + pre * bell) * back).astype(bf16)
        acc[...] += nn(hidden, w2)
        gsec[...] += nt(grad, w1)
        row_ref[row, row_lanes] = column_sum(grad.astype(f32))
        rows_s[...] = nn(hidden.T, cot_ref[...]).astype(bf16)
        for side, ref in ((0, sk_ref), (1, ss_ref)):
            first = jnp.where(own == side, 0, wide)
            for h, at in ((0, i), (1, table[5 * half + i])):
                start = pl.multiple_of(first + h * (wide // 2), 16)
                ref[h, at] = rows_s[pl.ds(start, wide // 2), :]
        ek_ref[:, lanes] = nn(s2t[: features // 2, :], grad).astype(bf16)
        es_ref[:, lanes] = nn(s2t[features // 2 :, :], grad).astype(bf16)
        return carry

    lax.fori_loop(0, half, step, 0, unroll=True)
    out_ref[...] = (middle_s[...] + acc[...] + vec_ref[7:8, :]).astype(bf16)
    unit, scale = unit_rows(middle_s[...])
    grad = gsec[...]
    cot = cot_ref[...].astype(f32)
    row_ref[0:1, :] = column_sum(grad * unit)
    row_ref[1:2, :] = column_sum(grad)
    grad_middle = cot + norm_back(grad, unit, scale, vec_ref[2:3, :])
    gm_ref[...] = grad_middle
    branch = grad_middle.astype(bf16)
    row_ref[2:3, :] = column_sum(branch.astype(f32))
    row_ref[3:4, :] = column_sum(cot)
    ga_ref[...] = nt(branch, wo_ref[...]).astype(bf16)
    ek_ref[:, inner:] = nn(ot[: features // 2, :], branch).astype(bf16)
    es_ref[:, inner:] = nn(ot[features // 2 :, :], branch).astype(bf16)


def attend_back_kernel(
    g,
    bounds,
    q_ref,
    kv_ref,
    o_ref,
    g_ref,
    lse_ref,
    qid_ref,
    kid_ref,
    dq_ref,
    dk_ref,
    dv_ref,
    row_ref,
    acc,
    qm,
    gm,
    q_stack,
    g_stack,
    sc,
    dp,
    p_wide,
    g_wide,
    rows_s,
):
    width, features = q_ref.shape
    slots = kv_ref.shape[0]
    barred = mask_rows(qid_ref[...].astype(f32), width)
    nothing = jnp.zeros((64, width), bf16)
    upper = lane_half(width, 1)

    def blank(s, carry):
        dk_ref[s] = jnp.zeros(dk_ref.shape[1:], dk_ref.dtype)
        dv_ref[s] = jnp.zeros(dv_ref.shape[1:], dv_ref.dtype)
        return carry

    lax.fori_loop(0, bounds[0], blank, 0)
    lax.fori_loop(bounds[1], slots, blank, 0)

    base = g * GROUP * HEAD_WIDTH
    lanes_g = slice(base, base + GROUP * HEAD_WIDTH)
    lanes_v = slice(features + base, features + base + GROUP * HEAD_WIDTH)
    acc[...] = jnp.zeros_like(acc)
    q_all, g_all = q_ref[:, lanes_g], g_ref[:, lanes_g]
    product = (g_all.astype(f32) * o_ref[:, lanes_g].astype(f32)).T
    q_t, g_t = q_all.T, g_all.T
    for h in range(GROUP):
        lanes = slice(128 * (h // 2), 128 * (h // 2) + 128)
        rows = slice(64 * h, 64 * h + 64)
        odd = h % 2
        qm[h, 0:64, :] = barred if odd else q_t[rows, :]
        qm[h, 64:128, :] = q_t[rows, :] if odd else barred
        gm[h, 0:64, :] = nothing if odd else g_t[rows, :]
        gm[h, 64:128, :] = g_t[rows, :] if odd else nothing
        half = lane_half(width, odd)
        place = slice(width * odd, width * odd + width)
        pair = q_all[:, lanes]
        q_stack[h // 2, place, :] = jnp.where(half, pair, jnp.zeros_like(pair))
        pair = g_all[:, lanes]
        g_stack[h // 2, place, :] = jnp.where(half, pair, jnp.zeros_like(pair))
        rows_s[h : h + 1, :] = column_sum(product[rows, :])
    rows_s[8:9, :] = jnp.zeros((1, GROUP * HEAD_WIDTH), f32)

    def step(s, carry):
        keys = kv_ref[s, :, lanes_g]
        values = kv_ref[s, :, lanes_v]
        keys_t = keys.T
        marks = key_marks(kid_ref[s], width)
        for h in range(GROUP):
            lanes = slice(128 * (h // 2), 128 * (h // 2) + 128)
            pair = keys[:, lanes]
            marked = jnp.where(upper, pair, marks) if h % 2 else jnp.where(upper, marks, pair)
            sc[h] = nn(marked, qm[h])
            dp[h] = nn(values[:, lanes], gm[h])
        for h in range(GROUP):
            place = slice(width * (h % 2), width * (h % 2) + width)
            prob = jnp.exp(sc[h] - lse_ref[g, h : h + 1, :])
            p_wide[h // 2, :, place] = prob.astype(bf16)
            g_wide[h // 2, :, place] = (prob * (dp[h] - rows_s[h : h + 1, :])).astype(bf16)
        for h in range(GROUP):
            place = slice(width * (h % 2), width * (h % 2) + width)
            rows = slice(64 * h, 64 * h + 64)
            acc[rows, :] += nn(keys_t[rows, :], g_wide[h // 2, :, place])
        key_parts, value_parts = [], []
        for j in range(GROUP // 2):
            value_parts.append(nn(p_wide[j], g_stack[j]))
            key_parts.append(nn(g_wide[j], q_stack[j]))
        value_all = jnp.concatenate(value_parts, axis=1)
        dk_ref[s] = jnp.concatenate(key_parts, axis=1).astype(bf16)
        dv_ref[s] = value_all.astype(bf16)
        rows_s[8:9, :] += column_sum(value_all)
        return carry

    lax.fori_loop(bounds[0], bounds[1], step, 0)
    dq = (acc[...].T.astype(bf16).astype(f32) * score_scale).astype(bf16)
    dq_ref[...] = dq
    row_ref[0:1, :] = column_sum(dq.astype(f32))
    row_ref[1:2, :] = rows_s[8:9, :]


def parts_kernel(reach, bounds, *refs):
    groups = (len(refs) - 3) // 3
    dqs, dks, dvs = (refs[k * groups : (k + 1) * groups] for k in range(3))
    w_ref, p_ref, own_ref = refs[3 * groups :]
    features = p_ref.shape[2]
    size = features // groups

    def part(s):
        total = None
        for g in range(groups):
            for ref, base in ((dks[g], features), (dvs[g], 2 * features)):
                now = nt(ref[s], w_ref[:, base + g * size : base + (g + 1) * size])
                total = now if total is None else total + now
        return total

    def one(s, to):
        active = (s >= bounds[0]) & (s < bounds[1])

        @pl.when(active)
        def _():
            p_ref[to] = part(s).astype(bf16)

        @pl.when(jnp.logical_not(active))
        def _():
            p_ref[to] = jnp.zeros(p_ref.shape[1:], p_ref.dtype)

    def some(i, carry):
        one(jnp.where(i < reach, i, i + 1), i)
        return carry

    lax.fori_loop(0, 2 * reach, some, 0)
    total = part(reach)
    for g in range(groups):
        total = total + nt(dqs[g][...], w_ref[:, g * size : (g + 1) * size])
    own_ref[...] = total


def weight_kernel(reach, half, groups, table, *refs):
    slots = 2 * reach + 1
    xs, bounds = refs[:slots], refs[slots]
    refs = refs[slots + 1 :]
    dqs, dks, dvs = (refs[k * groups : (k + 1) * groups] for k in range(3))
    keep_ref, send_ref, xt, plain = refs[3 * groups :]
    width, size = dqs[0].shape
    features = size * groups
    few = min(3, slots)
    small = bounds[1] - bounds[0] <= few
    start = jnp.minimum(bounds[0], slots - few)

    for s in range(slots):

        @pl.when(jnp.logical_not(small) | ((s >= start) & (s < start + few)))
        def _(s=s):
            plain[...] = xs[s][0:width, :].T.astype(f32)
            spread_rows(table, plain, xt, slice(width * s, width * s + width), half)

    def put(tokens, right, base):
        lanes = slice(base, base + size)
        keep_ref[:, lanes] = nn(xt[: features // 2, tokens], right).astype(bf16)
        send_ref[:, lanes] = nn(xt[features // 2 :, tokens], right).astype(bf16)

    for g in range(groups):
        put(slice(width * reach, width * reach + width), dqs[g][...], g * size)

    def over(start, count):
        tokens = pl.ds(pl.multiple_of(start * width, 128), count * width)
        for base, group in ((features, dks), (2 * features, dvs)):
            for g in range(groups):
                rows = group[g][pl.ds(start, count)].reshape(count * width, size)
                put(tokens, rows, base + g * size)

    @pl.when(small)
    def _():
        over(start, few)

    @pl.when(jnp.logical_not(small))
    def _():
        over(0, slots)


def leave_kernel(
    table,
    raw_ref,
    mean_ref,
    std_ref,
    vec_ref,
    gm_ref,
    own_ref,
    left_ref,
    right_ref,
    ffn_rows,
    *refs,
):
    attend_rows, (gn_ref, row_ref) = refs[:-2], refs[-2:]
    features = raw_ref.shape[1]
    centred = raw_ref[...] - mean_ref[...]
    unit, scale = unit_rows(centred * std_ref[...])
    grad = own_ref[...] + left_ref[...].astype(f32) + right_ref[...].astype(f32)
    row_ref[0:1, :] = column_sum(grad * unit)
    row_ref[1:2, :] = column_sum(grad)
    row_ref[2:4, :] = ffn_rows[0:2, :]
    size = features // len(attend_rows)
    for g, ref in enumerate(attend_rows):
        row_ref[4:6, g * size : (g + 1) * size] = ref[...]
    row_ref[6:8, :] = ffn_rows[2:4, :]
    row_ref[8:12, :] = ffn_rows[8:12, :]
    whole_grad = gm_ref[...] + norm_back(grad, unit, scale, vec_ref[0:1, :])
    gn_ref[...] = whole_grad
    row_ref[12:13, :] = column_sum(whole_grad)
    row_ref[13:14, :] = column_sum(whole_grad * centred)
    row_ref[14:16, :] = jnp.zeros((2, features), f32)


def adam_rule(master, moment, square, gradient, step_value, step_rate, weight_decay):
    moment_new = beta_one * moment + (1.0 - beta_one) * gradient
    square_new = beta_two * square + (1.0 - beta_two) * gradient * gradient
    fix_first = 1.0 - jnp.power(beta_one, step_value)
    fix_second = 1.0 - jnp.power(beta_two, step_value)
    planned = step_rate * jnp.minimum(1.0, step_value / warmup_length)
    direction = moment_new / fix_first / (jnp.sqrt(square_new / fix_second) + adam_epsilon)
    weight_new = master - planned * (direction + weight_decay * master)
    return (weight_new, moment_new, square_new, weight_new.astype(bf16))


def per_device(
    raw_input,
    cotangent,
    segment_ids,
    step_count,
    inlet_copy,
    inlet_master,
    inlet_moment,
    inlet_square,
    outlet_copy,
    outlet_master,
    outlet_moment,
    outlet_square,
    expand_copy,
    expand_master,
    expand_moment,
    expand_square,
    shrink_copy,
    shrink_master,
    shrink_moment,
    shrink_square,
    vector_copy,
    vector_master,
    vector_moment,
    vector_square,
):
    sequences, block_length, features = raw_input.shape
    assert sequences == 1
    width = block_length
    group_size = lax.axis_size("blk")
    group_index = lax.axis_index("blk")
    owners = lax.axis_size("dp")
    owner = lax.axis_index("dp")
    half = owners // 2
    total_tokens = owners * group_size * block_length
    reach = group_size // 2
    slots = 2 * reach + 1
    inner = expand_copy.shape[1]
    chunk = inner // half
    vectors = vector_copy.astype(f32)
    raw = raw_input.reshape(width, features)
    cot = cotangent.reshape(width, features)
    own_ids = segment_ids.astype(f32)
    count = owners.bit_length() - 1
    scalar = pl.BlockSpec(memory_space=pltpu.SMEM)
    vmem = pltpu.VMEM

    def reversed_bits(value):
        return int(format(value, f"0{count - 1}b")[::-1], 2) if count > 1 else 0

    straight = [reversed_bits(p) for p in range(half)]
    other_way = list(range(half))
    relative = jnp.array(
        [2 * v for v in straight]
        + [2 * v for v in straight]
        + [2 * v + 1 for v in straight]
        + [2 * v for v in other_way]
        + [2 * v + 1 for v in other_way],
        jnp.int32,
    ) ^ owner
    inside = [group_index >= d for d in range(1, reach + 1)]
    inside += [group_index + d < group_size for d in range(1, reach + 1)]
    table = jnp.concatenate(
        [
            relative[:half] // 2,
            relative[half:],
            jnp.array(straight, jnp.int32),
            jnp.stack([flag for pair in zip(inside[:reach], inside[reach:]) for flag in pair]).astype(jnp.int32),
        ]
    )
    lows = [(group_index // bit) % 2 == 0 for bit in bits_of("blk")]
    column_count = vector_master.shape[1]
    column_start = owner * column_count
    step_value = step_count[0].astype(f32)

    tokens, row = (width, features), (1, features)
    wkv = 3 * features
    lanes = GROUP * HEAD_WIDTH
    steps = features // lanes

    (totals,) = call(
        totals_kernel, "totals", jnp.zeros((1,), jnp.int32), [raw], [struct((2, features), f32)], mib=2
    )
    rounds = SmallSum(totals)
    rounds.send()
    rounds.take()
    rounds.send()
    tied = together(*rounds.arrived, table, column_start, vectors, own_ids, *lows)
    ways = len(rounds.arrived)
    rounds.arrived = list(tied[:ways])
    table, column_start, vectors, own_ids = tied[ways : ways + 4]
    lows = list(tied[ways + 4 :])
    rounds.take()
    while rounds.left():
        rounds.send()
        rounds.take()
    totals = rounds.block
    packed = width + 16
    x, mean_row, inverse_row = call(
        functools.partial(enter_kernel, total_tokens),
        "enter",
        table,
        [raw, totals, vectors, own_ids],
        [struct((packed, features), bf16), struct(row, f32), struct(row, f32)],
        mib=6,
    )

    xs = [None] * slots
    xs[reach] = x
    ahead, behind = moved(x, "blk", 1), moved(x, "blk", -1)
    queries, pairs, columns = call(
        project_own_kernel,
        "project_own",
        table,
        [x, inlet_copy, vectors],
        [
            struct(tokens, bf16),
            struct((slots, width, 2 * features), bf16),
            struct((slots, width, 128), f32),
        ],
        mib=6,
    )
    ahead, behind, queries = together(ahead, behind, queries)
    for d in range(1, reach + 1):
        if d > 1:
            ahead, behind = moved(ahead, "blk", 1), moved(behind, "blk", -1)
            ahead, behind, pairs = together(ahead, behind, pairs)
        xs[reach - d], xs[reach + d] = ahead, behind
        pairs, columns = call(
            functools.partial(project_pair_kernel, d, 6 * half + 2 * (d - 1)),
            "project_pair",
            table,
            [ahead, behind, x, inlet_copy, vectors, pairs, columns],
            [struct(pairs.shape, bf16), struct(columns.shape, f32)],
            [vmem((2, packed, features), bf16)],
            mib=6,
        )

    attended, lse, bounds = call(
        functools.partial(attend_kernel, reach),
        "attend",
        table,
        [queries, pairs, own_ids, columns],
        [struct(tokens, bf16), struct((steps, GROUP, width), f32), struct((2,), jnp.int32)],
        [
            vmem((80 * GROUP, width), f32),
            vmem((8, width), f32),
            vmem((GROUP, 128, width), bf16),
            vmem((GROUP, width, width), f32),
        ],
        mib=6,
    )

    owned_wide, owned = inner // owners, features // owners
    kept_shrink = struct((2, half, owned_wide // 2, features), bf16)
    kept_expand = struct((features // 2, inner + features), bf16)
    layer_output, grad_middle, grad_attended, shrink_keep, shrink_send, expand_keep, expand_send, ffn_rows = call(
        functools.partial(ffn_kernel, half),
        "ffn",
        table,
        [attended, outlet_copy, raw, mean_row, inverse_row, vectors, cot, expand_copy, shrink_copy],
        [
            struct(tokens, bf16),
            struct(tokens, f32),
            struct(tokens, bf16),
            kept_shrink,
            kept_shrink,
            kept_expand,
            kept_expand,
            struct((12, features), f32),
        ],
        [
            vmem(tokens, f32),
            vmem(tokens, f32),
            vmem(tokens, bf16),
            vmem((features, width), bf16),
            vmem((features, width), bf16),
            vmem((features, width), f32),
            vmem((chunk, features), bf16),
            vmem(tokens, f32),
        ],
        mib=14,
    )
    bits = bits_of("dp")
    orders = (bits[1:], bits[:0:-1])

    def scatters(keep, arrived, rows):
        shape = (2,) + (2,) * (count - 1) + (rows // 2, keep.shape[-1])
        keep, arrived = keep.reshape(shape), arrived.reshape(shape)
        return [Scatter([keep[h], arrived[h]], orders[h]) for h in range(2)]

    token = [grad_attended]

    def after(*values):
        tied = together(*values, *token)[: len(values)]
        token[:] = tied
        return tied

    def launch(pair):
        for one in pair:
            one.prepare()
        token[:] = [one.sent for one in pair]
        for one in pair:
            one.send()

    def advance(pair):
        for one, value in zip(pair, after(*[one.arrived for one in pair])):
            one.arrived = value
            one.take()
        if pair[0].order:
            launch(pair)

    def follow(line, stage):
        (line.arrived,) = after(line.arrived)
        stage(line)
        token[:] = [line.keep]

    def begin(pair):
        line = Line(*pair, lows)
        token[:] = [line.sent]
        line.scatter()
        return line

    def next_round():
        rounds.take(after)
        token[:] = [rounds.block]
        if rounds.left():
            rounds.send()

    shrink_in = flipped(shrink_send, "dp", 1)
    expand_in = flipped(expand_send, "dp", 1)
    spread = struct((slots, width, lanes), bf16)
    back = []
    for g in range(steps):
        (grad_attended,) = after(grad_attended)
        back.append(
            call(
                functools.partial(attend_back_kernel, g),
                "attend_back",
                bounds,
                [queries, pairs, attended, grad_attended, lse, own_ids, columns],
                [struct((width, lanes), bf16), spread, spread, struct((2, lanes), f32)],
                [
                    vmem((lanes, width), f32),
                    vmem((GROUP, 128, width), bf16),
                    vmem((GROUP, 128, width), bf16),
                    vmem((GROUP // 2, 2 * width, 128), bf16),
                    vmem((GROUP // 2, 2 * width, 128), bf16),
                    vmem((GROUP, width, width), f32),
                    vmem((GROUP, width, width), f32),
                    vmem((GROUP // 2, width, 2 * width), bf16),
                    vmem((GROUP // 2, width, 2 * width), bf16),
                    vmem((16, width), f32),
                ],
                mib=8,
            )
        )
        token[:] = [back[-1][0]]
        if g == 0:
            (shrink_in,) = after(shrink_in)
            first = scatters(shrink_keep, shrink_in, owned_wide)
            launch(first)
    query_low, key_low, value_low, attend_rows = zip(*back)
    grads = [*query_low, *key_low, *value_low]
    (expand_in,) = after(expand_in)

    grads = after(*grads)
    parts, own_part = call(
        functools.partial(parts_kernel, reach),
        "parts",
        bounds,
        [*grads, inlet_copy],
        [struct((2 * reach, width, features), bf16), struct(tokens, f32)],
        mib=6,
    )
    to_left, to_right = parts[0], parts[2 * reach - 1]
    token[:] = [to_left, to_right]
    from_right, from_left = moved(to_left, "blk", -1), moved(to_right, "blk", 1)
    advance(first)

    kept_inlet = struct((features // 2, wkv), bf16)
    grads = after(*grads)
    inlet_keep, inlet_send = call(
        functools.partial(weight_kernel, reach, half, steps),
        "weights",
        table,
        xs + [(scalar, bounds), *grads],
        [kept_inlet, kept_inlet],
        [vmem((features, slots * width), bf16), vmem((features, width), f32)],
        mib=8,
    )
    token[:] = [inlet_keep]
    inlet_in = flipped(inlet_send, "dp", 1)
    while first[0].order:
        advance(first)
    advance(first)
    (expand_in,) = after(expand_in)
    second = scatters(expand_keep, expand_in, owned)
    launch(second)
    for d in range(reach - 1, 0, -1):
        from_right, from_left = after(from_right, from_left)
        to_left = added(parts[reach - d], from_right)
        to_right = added(parts[reach + d - 1], from_left)
        token[:] = [to_left, to_right]
        from_right, from_left = moved(to_left, "blk", -1), moved(to_right, "blk", 1)
    line_one = begin(first)
    from_right, from_left = after(from_right, from_left)
    grad_normed, small = call(
        leave_kernel,
        "leave",
        table,
        [
            raw,
            mean_row,
            inverse_row,
            vectors,
            grad_middle,
            own_part,
            from_left,
            from_right,
            ffn_rows,
            *attend_rows,
        ],
        [struct(tokens, f32), struct((16, features), f32)],
        mib=8,
    )
    token[:] = [small]
    rounds = SmallSum(small, paired=False)
    rounds.send()
    advance(second)
    (inlet_in,) = after(inlet_in)
    third = scatters(inlet_keep, inlet_in, owned)
    launch(third)
    next_round()
    follow(line_one, Line.exchange)
    while second[0].order:
        advance(second)
    advance(second)
    line_two = begin(second)
    next_round()
    advance(third)
    follow(line_two, Line.exchange)
    follow(line_one, Line.gather)
    next_round()
    while third[0].order:
        advance(third)
    advance(third)
    line_three = begin(third)
    while rounds.left():
        next_round()
    (line_two.arrived, line_three.arrived) = after(line_two.arrived, line_three.arrived)
    line_three.exchange()
    line_two.gather()
    *rounds.arrived, line_three.keep = together(*rounds.arrived, line_three.keep)
    rounds.take()
    small = rounds.block
    line_one.arrived, line_three.keep = together(line_one.arrived, line_three.keep)
    shrink_new = adam_rule(
        shrink_master,
        shrink_moment,
        shrink_square,
        line_one.result().astype(f32),
        step_value,
        rate_matrix,
        decay_matrix,
    )
    line_three.arrived, small, *shrink_new = together(line_three.arrived, small, *shrink_new)
    line_three.gather()
    expand_share = line_two.result()
    inlet_share = line_three.result()

    band_mean = totals[0] / total_tokens
    band_variance = totals[1] / total_tokens - band_mean * band_mean
    inverse = lax.rsqrt(band_variance + stat_epsilon)
    back_totals = small[12:14]
    grad_variance = -0.5 * back_totals[1] * inverse * inverse * inverse
    grad_centre = -inverse * back_totals[0] - 2.0 * band_mean * grad_variance
    input_gradient = (
        grad_normed * inverse
        + grad_centre / total_tokens
        + 2.0 * grad_variance * raw / total_tokens
    ).reshape(sequences, block_length, features)
    vector_share = lax.dynamic_slice(
        small[:12], (0, column_start), (12, column_count), allow_negative_indices=False
    )

    updates = []
    for master, moment, square, share in (
        (inlet_master, inlet_moment, inlet_square, inlet_share),
        (outlet_master, outlet_moment, outlet_square, expand_share[:, inner:]),
        (expand_master, expand_moment, expand_square, expand_share[:, :inner]),
    ):
        updates.extend(
            adam_rule(
                master, moment, square, share.astype(f32), step_value, rate_matrix, decay_matrix
            )
        )
    updates.extend(shrink_new)
    updates.extend(
        adam_rule(
            vector_master, vector_moment, vector_square, vector_share, step_value, rate_vector, 0.0
        )
    )
    layer_output = layer_output.reshape(sequences, block_length, features)
    return (layer_output, input_gradient, band_mean, band_variance, *updates)


def solution(mesh):
    tokens = P("dp", "blk", None)
    rows = P("dp", None)
    columns = P(None, "dp")
    matrix = (P(), rows, rows, rows)
    return jax.shard_map(
        per_device,
        mesh=mesh,
        in_specs=(tokens, tokens, P("dp", "blk"), P())
        + matrix * 4
        + (P(), columns, columns, columns),
        out_specs=(tokens, tokens, P(), P()) + (rows,) * 16 + (columns,) * 4,
        check_vma=False,
    )
```
